32 devices in a mesh: seq: 8 (over y, x, core), dp: 4 (over z).
Axes of the slice: x: 2, y: 2, z: 4, core: 2. Of those that a mesh axis runs over, the one named last changes fastest.
Arguments:
- tokens: bfloat16 [4, 4096, 1024], P('dp', 'seq'), may hold values from -6 to 6
- item_starts: int32 [4, 8], P('dp', 'seq'), may hold values from 0 to 1, as said below
- attn_gain: float32 [1024], replicated, may hold values from 0.5 to 1.5
- query_weight: bfloat16 [1024, 1024], replicated, may hold values from -0.1875 to 0.1875
- key_weight: bfloat16 [1024, 1024], replicated, may hold values from -0.1875 to 0.1875
- value_weight: bfloat16 [1024, 1024], replicated, may hold values from -0.1875 to 0.1875
- output_weight: bfloat16 [1024, 1024], replicated, may hold values from -1.5 to 1.5
- state_queries: bfloat16 [512, 1024], replicated, may hold values from -6 to 6
- state_weight: bfloat16 [1024, 2048], replicated, may hold values from -1.5 to 1.5
- gate_bias: float32 [1024], replicated, may hold values from -2 to 6
- initial_state: float32 [512, 1024], replicated, may hold values from -6 to 6
- mlp_gain: float32 [1024], replicated, may hold values from 0.5 to 1.5
- up_weight: bfloat16 [1024, 4096], replicated, may hold values from -0.1875 to 0.1875
- down_weight: bfloat16 [4096, 1024], replicated, may hold values from -0.09375 to 0.09375
- out_cotangent: bfloat16 [4, 4096, 1024], P('dp', 'seq'), may hold values from -6 to 6
- state_cotangent: float32 [4, 8, 512, 1024], P('dp', 'seq'), may hold values from -6 to 6
Outputs:
- mixed: bfloat16 [4, 4096, 1024], P('dp', 'seq')
- states: float32 [4, 8, 512, 1024], P('dp', 'seq')
- tokens_grad: float32 [4, 4096, 1024], P('dp', 'seq')
- attn_gain_grad: float32 [1024], P('seq')
- query_grad: float32 [1024, 1024], P('seq')
- key_grad: float32 [1024, 1024], P('seq')
- value_grad: float32 [1024, 1024], P('seq')
- output_grad: float32 [1024, 1024], P('seq')
- state_queries_grad: float32 [512, 1024], P('seq')
- state_weight_grad: float32 [1024, 2048], P('seq')
- gate_bias_grad: float32 [1024], P('seq')
- initial_state_grad: float32 [512, 1024], P('seq')
- mlp_gain_grad: float32 [1024], P('seq')
- up_grad: float32 [1024, 4096], P('seq')
- down_grad: float32 [4096, 1024], P('seq')
The draws below stay inside these ranges and needn't reach their ends.
Inputs may be any that keep to these rules, and one draw needn't show every extreme that they name: item_starts is 1 exactly at the first block of each item. Block 0 of every group starts an item; each aligned run of 8 blocks holds one item of 8 blocks or two of 4 blocks; some item has 8 blocks.
All inputs are finite; a program needn't handle non-finite values.
Results may differ from the reference program's by a relative error of at most 0.023.
Values may be sent and summed in bfloat16 or wider, within the bound.
No kernel may reach another device: no remote copies, remote signals or barrier semaphores. Data moves between devices by JAX's collectives and lax.ppermute only.
A program may use at most 512 MiB of HBM per device.

```python
import math
import jax
import jax.numpy as jnp
from jax import lax

D = 1024
HEADS = 8
HEAD_DIM = 128
FF = 4096
W = 512
NS = 512
ITEM_BLOCKS = 8
GROUPS = 4
BLOCKS = 8
GROUP_TOKENS = 4096


def draw_item_starts(key, part):
    octets = BLOCKS // ITEM_BLOCKS
    split_key = jax.random.fold_in(key, 11)
    pick_key = jax.random.fold_in(key, 23)
    halves = jax.random.randint(split_key, (GROUPS, octets), 0, 2)
    chosen = jax.random.randint(pick_key, (), 0, GROUPS * octets)
    places = jnp.arange(GROUPS * octets).reshape(GROUPS, octets)
    halves = jnp.where(places == chosen, 0, halves)
    position = jnp.arange(BLOCKS)
    within = position % ITEM_BLOCKS
    owner = position // ITEM_BLOCKS
    split_here = halves[:, owner] == 1
    starts = (within == 0)[None, :] | (within == ITEM_BLOCKS // 2)[None, :] & split_here
    return starts.astype(jnp.int32)


def shard_levels(own_key, extent, shards, low, top_value):
    gain, own = 1.0, jax.random.fold_in(own_key, 6)
    for dim, parts in shards:
        steps = jnp.exp(jax.random.uniform(jax.random.fold_in(own, dim), (parts,), jnp.float32, low / len(shards), top_value / len(shards)))
        gain = gain * jnp.repeat(steps, extent[dim] // parts).reshape([-1 if axis == dim else 1 for axis in range(len(extent))])
    return gain


def scatter_about(stream_key, shape, width, most, pieces=(), dtype=jnp.bfloat16):
    gain = shard_levels(stream_key, shape, pieces, -0.22, 0.18) if pieces else 1.0
    values = jax.random.normal(stream_key, shape, jnp.float32) * width * gain
    return jnp.minimum(jnp.maximum(values, -most), most).astype(dtype)


def setup_inputs(seed: int = 0) -> dict:
    streams_of = jax.random.split(jax.random.key(seed), 17)
    return {
        "tokens": scatter_about(streams_of[0], (GROUPS, GROUP_TOKENS, D), 1.0, 6.0, ((0, 4), (1, 8))),
        "item_starts": draw_item_starts(jax.random.fold_in(streams_of[16], 71), 0),
        "attn_gain": jnp.clip(1.0 + 0.1 * jax.random.normal(streams_of[2], (D,), jnp.float32), 0.5, 1.5),
        "query_weight": scatter_about(streams_of[3], (D, D), D ** -0.5, 0.1875),
        "key_weight": scatter_about(streams_of[4], (D, D), D ** -0.5, 0.1875),
        "value_weight": scatter_about(streams_of[5], (D, D), D ** -0.5, 0.1875),
        "output_weight": scatter_about(streams_of[6], (D, D), (D // 64) ** -0.5, 1.5),
        "state_queries": scatter_about(streams_of[7], (NS, D), 1.0, 6.0),
        "state_weight": scatter_about(streams_of[8], (D, 2 * D), (D // 64) ** -0.5, 1.5),
        "gate_bias": jnp.clip(jax.random.uniform(streams_of[9], (D,), jnp.float32, -2.0, 6.0), -2.0, 6.0),
        "initial_state": scatter_about(streams_of[10], (NS, D), 1.0, 6.0, (), jnp.float32),
        "mlp_gain": jnp.clip(1.0 + 0.1 * jax.random.normal(streams_of[11], (D,), jnp.float32), 0.5, 1.5),
        "up_weight": scatter_about(streams_of[12], (D, FF), D ** -0.5, 0.1875),
        "down_weight": scatter_about(streams_of[13], (FF, D), FF ** -0.5, 0.09375),
        "out_cotangent": scatter_about(streams_of[14], (GROUPS, GROUP_TOKENS, D), 1.0, 6.0, ((0, 4), (1, 8))),
        "state_cotangent": scatter_about(streams_of[15], (GROUPS, BLOCKS, NS, D), 1.0, 6.0, ((0, 4), (1, 8)), jnp.float32),
    }


@jax.custom_vjp
def low(v):
    return lax.optimization_barrier(v.astype(jnp.bfloat16)).astype(jnp.float32)

@jax.custom_vjp
def low_back(v):
    return v

def low_keep(v):
    return (low(v), None)

def low_pass(kept, grad):
    return (grad,)

def back_keep(v):
    return (v, None)

def back_low(kept, grad):
    return (low(grad),)
low.defvjp(low_keep, low_pass)
low_back.defvjp(back_keep, back_low)
EPSILON = 1e-06
NEGATIVE = -1e+30
GELU_SCALE = 0.7978845608028654
GELU_CUBIC = 0.044715
PRECISE = lax.Precision.HIGHEST

def gelu_tanh(upper):
    inner = GELU_SCALE * (upper + GELU_CUBIC * upper * upper * upper)
    return 0.5 * upper * (1.0 + jnp.tanh(inner))

def product(left, right):
    return jnp.dot(left, right, precision=PRECISE)

def rms_scale(field):
    return lax.rsqrt(lax.optimization_barrier(jnp.mean(field * field, axis=-1, keepdims=True)) + EPSILON)

def split_heads(field):
    return field.reshape(field.shape[0], HEADS, HEAD_DIM)

def group_forward(weights, group_tokens, group_starts):
    attn_gain, query_weight, key_weight, value_weight, output_weight, state_queries, state_weight, gate_bias, initial_state, mlp_gain, up_weight, down_weight = weights
    scale = 1.0 / math.sqrt(HEAD_DIM)
    normed = low(group_tokens * rms_scale(group_tokens) * attn_gain)
    queries = low(low_back(product(normed, query_weight)))
    keys = low(low_back(product(normed, key_weight)))
    values = low(low_back(product(normed, value_weight)))
    blank = jnp.zeros((W, D), jnp.float32)
    left_keys = jnp.concatenate([blank, keys[:-W]], axis=0)
    left_values = jnp.concatenate([blank, values[:-W]], axis=0)
    rows = lax.broadcasted_iota(jnp.int32, (W, W), 0)
    cols = lax.broadcasted_iota(jnp.int32, (W, W), 1)
    causal = cols <= rows
    starts = group_starts.astype(jnp.float32)
    query_heads = split_heads(state_queries)

    def one_block(carry, block):
        block_queries, block_keys, block_values, block_left_keys, block_left_values, start = block
        summary_raw = low_back(jnp.einsum('nhd,whd->hnw', query_heads, split_heads(block_keys), precision=PRECISE))
        summary_probs = jax.nn.softmax(summary_raw * scale, axis=-1)
        summary = jnp.einsum('hnw,whd->nhd', low(summary_probs), split_heads(block_values), precision=PRECISE)
        summary = low(low_back(summary.reshape(NS, D)))
        projected = low_back(product(summary, state_weight))
        update = projected[:, :D]
        forget = jax.nn.sigmoid(projected[:, D:] + gate_bias)
        state_in = (1.0 - start) * carry + start * initial_state
        state_out = forget * state_in + (1.0 - forget) * update
        state_low = low(state_in)
        state_keys = low(low_back(product(state_low, key_weight)))
        state_values = low(low_back(product(state_low, value_weight)))
        seen_keys = jnp.concatenate([block_left_keys, block_keys, state_keys], axis=0)
        seen_values = jnp.concatenate([block_left_values, block_values, state_values], axis=0)
        raw = low_back(jnp.einsum('whd,khd->hwk', split_heads(block_queries), split_heads(seen_keys), precision=PRECISE))
        left_ok = jnp.broadcast_to(start < 0.5, (W, W))
        valid = jnp.concatenate([left_ok, causal, jnp.ones((W, NS), bool)], axis=1)
        scores = jnp.where(valid[None], raw * scale, NEGATIVE)
        probs = jax.nn.softmax(scores, axis=-1)
        attended = jnp.einsum('hwk,khd->whd', low(probs), split_heads(seen_values), precision=PRECISE)
        attended = low(low_back(attended.reshape(W, D)))
        return (state_out, (attended, state_out))
    blocks = (queries.reshape(BLOCKS, W, D), keys.reshape(BLOCKS, W, D), values.reshape(BLOCKS, W, D), left_keys.reshape(BLOCKS, W, D), left_values.reshape(BLOCKS, W, D), starts)
    first = jnp.zeros((NS, D), jnp.float32)
    unused, (attended, states) = lax.scan(jax.checkpoint(one_block), first, blocks)
    attended = attended.reshape(GROUP_TOKENS, D)
    hidden = group_tokens + low_back(product(attended, output_weight))
    normed_mlp = low(hidden * rms_scale(hidden) * mlp_gain)
    upper = low_back(product(normed_mlp, up_weight))
    activated = low(low_back(gelu_tanh(upper)))
    result = hidden + low_back(product(activated, down_weight))
    return (result, states)

def reference(tokens, item_starts, attn_gain, query_weight, key_weight, value_weight, output_weight, state_queries, state_weight, gate_bias, initial_state, mlp_gain, up_weight, down_weight, out_cotangent, state_cotangent):
    weights = tuple((weight.astype(jnp.float32) for weight in (attn_gain, query_weight, key_weight, value_weight, output_weight, state_queries, state_weight, gate_bias, initial_state, mlp_gain, up_weight, down_weight)))

    def group_grads(totals, group):
        group_tokens, group_starts, group_cotangent, group_state_cotangent = group

        def forward(weights_in, tokens_in):
            return group_forward(weights_in, tokens_in, group_starts)
        (result, states), pullback = jax.vjp(forward, weights, group_tokens.astype(jnp.float32))
        weight_grads, token_grad = pullback((group_cotangent.astype(jnp.float32), group_state_cotangent))
        totals = jax.tree.map(lambda first, second: first + second, totals, weight_grads)
        return (totals, (result.astype(jnp.bfloat16), states, token_grad))
    zeros = jax.tree.map(jnp.zeros_like, weights)
    totals, (mixed, states, tokens_grad) = lax.scan(group_grads, zeros, (tokens, item_starts, out_cotangent, state_cotangent))
    return (mixed, states, tokens_grad, totals[0], totals[1], totals[2], totals[3], totals[4], totals[5], totals[6], totals[7], totals[8], totals[9], totals[10], totals[11])
```

```python
import math

import jax
import jax.numpy as jnp
from jax import lax
from jax.sharding import PartitionSpec as P

D = 1024
HEADS = 8
HEAD_DIM = 128
W = 512
NS = 512


EPSILON = 1e-06
NEGATIVE = -1e30
GELU_SCALE = 0.7978845608028654
GELU_CUBIC = 0.044715


def shifted(value, axis, steps):
    count = lax.axis_size(axis)
    first, last = (max(0, -steps), min(count, count - steps))
    return lax.ppermute(value, axis, [(source, source + steps) for source in range(first, last)])


def swapped(value, axis, distance):
    count = lax.axis_size(axis)
    return lax.ppermute(value, axis, [(place, place ^ distance) for place in range(count)])


def add_low(first, second):
    return (first.astype(jnp.float32) + second.astype(jnp.float32)).astype(jnp.bfloat16)


def pick(value, index, axis):
    return lax.dynamic_index_in_dim(value, index, axis, False)


def scatter_bits(value, bits, names):
    place = lax.axis_index("seq")
    names = list(names)
    for bit in bits:
        at = names.index(bit)
        mine = (place >> bit) & 1
        recv = swapped(pick(value, 1 - mine, at), "seq", 1 << bit)
        value = add_low(pick(value, mine, at), recv)
        names.pop(at)
    return value


def weight_scatter(left, right, forward):
    count = lax.axis_size("seq")
    levels = count.bit_length() - 1
    place = lax.axis_index("seq")
    tokens, rows = left.shape
    parts = left.reshape(tokens, count // 2, 2, rows // count)
    mine = place & 1
    give = product_tn(pick(parts, 1 - mine, 2).reshape(tokens, rows // 2), right).astype(jnp.bfloat16)
    recv = swapped(give, "seq", 1)
    keep = product_tn(pick(parts, mine, 2).reshape(tokens, rows // 2), right)
    total = (keep + recv.astype(jnp.float32)).astype(jnp.bfloat16)
    total = total.reshape((2,) * (levels - 1) + (rows // count, right.shape[1]))
    names = list(range(levels - 1, 0, -1))
    bits = names[::-1] if forward else names
    return scatter_bits(total, bits, names)


def whole_scatter(value, forward):
    count = lax.axis_size("seq")
    levels = count.bit_length() - 1
    names = list(range(levels - 1, -1, -1))
    value = value.reshape((2,) * levels + (value.shape[0] // count,) + value.shape[1:])
    bits = [0] + (names[-2::-1] if forward else names[:-1])
    return scatter_bits(value, bits, names)


def sum_over_dp(value):
    count, place = lax.axis_size("dp"), lax.axis_index("dp")
    half = count // 2
    for step in range(half - 1):
        value = add_low(
            value,
            lax.ppermute(value, "dp", [(step, step + 1), (count - 1 - step, count - 2 - step)]),
        )
    value = add_low(value, lax.ppermute(value, "dp", [(half - 1, half), (half, half - 1)]))
    for step in range(half - 2, -1, -1):
        recv = lax.ppermute(value, "dp", [(step + 1, step), (count - 2 - step, count - 1 - step)])
        outer = (place == step) | (place == count - 1 - step)
        value = jnp.where(outer, recv, value)
    return value.astype(jnp.float32)


def halves_of(value, core):
    return pick(value.reshape((2, NS // 2) + value.shape[1:]), core, 0)


def chip_rows(value, chip):
    return pick(value.reshape((4, NS // 8) + value.shape[1:]), chip, 0)


def chips_exchange(value, place):
    chip = (place >> 1) & 3
    own = pick(value, chip, 0)
    came = [own] + [swapped(pick(value, chip ^ far, 0), "seq", 2 * far) for far in (1, 2, 3)]
    came = jnp.stack(came)
    return [pick(came, chip ^ source, 0) for source in range(4)]


def scan_states(scale, base, forward_products=None):
    place = lax.axis_index("seq")
    core = place & 1
    pair = jnp.stack([scale, base]).astype(jnp.bfloat16)
    parts = pair.reshape(2, 2, NS // 2, D)
    recv = swapped(pick(parts, 1 - core, 1), "seq", 1).astype(jnp.float32)
    own = pick(parts, core, 1).astype(jnp.float32)
    even = jnp.where(core == 0, own, recv)
    odd = jnp.where(core == 0, recv, own)
    chip_scale = odd[0] * even[0]
    chip_base = odd[0] * even[1] + odd[1]
    chip_pair = jnp.stack([chip_scale, chip_base]).astype(jnp.bfloat16)
    chip_pair = chip_pair.reshape(2, 4, NS // 8, D).transpose(1, 0, 2, 3)
    got = [part.astype(jnp.float32) for part in chips_exchange(chip_pair, place)]
    enter = [jnp.zeros_like(got[0][1]), got[0][1]]
    for chip in (1, 2):
        enter.append(got[chip][0] * enter[-1] + got[chip][1])
    back = chips_exchange(jnp.stack(enter).astype(jnp.bfloat16), place)
    before = jnp.concatenate(back, axis=0).astype(jnp.float32)
    between = even[0] * before + even[1]
    mine = jnp.where(core == 0, before, between)
    other = jnp.where(core == 0, between, before).astype(jnp.bfloat16)
    recv = swapped(other, "seq", 1).astype(jnp.float32)
    previous = jnp.where(
        core == 0, jnp.concatenate([mine, recv], axis=0), jnp.concatenate([recv, mine], axis=0)
    )
    kept = (even[0], odd[0], [part[0] for part in got])
    return previous, kept


def scan_grads(base, kept):
    even_scale, odd_scale, chip_scales = kept
    place = lax.axis_index("seq")
    core = place & 1
    parts = base.astype(jnp.bfloat16).reshape(2, NS // 2, D)
    recv = swapped(pick(parts, 1 - core, 0), "seq", 1).astype(jnp.float32)
    own = pick(parts, core, 0).astype(jnp.float32)
    even = jnp.where(core == 0, own, recv)
    odd = jnp.where(core == 0, recv, own)
    chip_base = (even_scale * odd + even).astype(jnp.bfloat16).reshape(4, NS // 8, D)
    got = [part.astype(jnp.float32) for part in chips_exchange(chip_base, place)]
    enter = [jnp.zeros_like(got[3]), got[3]]
    for chip in (2, 1):
        enter.append(chip_scales[chip] * enter[-1] + got[chip])
    back = chips_exchange(jnp.stack(enter[::-1]).astype(jnp.bfloat16), place)
    after = jnp.concatenate(back, axis=0).astype(jnp.float32)
    between = odd_scale * after + odd
    mine = jnp.where(core == 1, after, between)
    other = jnp.where(core == 1, between, after).astype(jnp.bfloat16)
    recv = swapped(other, "seq", 1).astype(jnp.float32)
    return jnp.where(
        core == 0, jnp.concatenate([mine, recv], axis=0), jnp.concatenate([recv, mine], axis=0)
    )


def gelu_tanh(upper):
    inner = GELU_SCALE * (upper + GELU_CUBIC * upper * upper * upper)
    return 0.5 * upper * (1.0 + jnp.tanh(inner))


def gelu_slope(upper):
    inner = GELU_SCALE * (upper + GELU_CUBIC * upper * upper * upper)
    tvalue = jnp.tanh(inner)
    return 0.5 * (1.0 + tvalue) + 0.5 * upper * (1.0 - tvalue * tvalue) * GELU_SCALE * (
        1.0 + 3.0 * GELU_CUBIC * upper * upper
    )


def product(left, right):
    return jnp.dot(left, right, preferred_element_type=jnp.float32)


def product_tn(left, right):
    return lax.dot_general(
        left, right, (((0,), (0,)), ((), ())), preferred_element_type=jnp.float32
    )


def product_nt(left, right):
    return lax.dot_general(
        left, right, (((1,), (1,)), ((), ())), preferred_element_type=jnp.float32
    )


def rms_scale(field):
    return lax.rsqrt(jnp.mean(field * field, axis=-1, keepdims=True) + EPSILON)


def rms_back(field, scaled, gain, grad):
    gain_grad = jnp.sum(grad * field * scaled, axis=0)
    weighted = grad * gain
    field_grad = scaled * weighted - field * scaled * scaled * scaled * jnp.mean(
        weighted * field, axis=-1, keepdims=True
    )
    return (gain_grad, field_grad)


def split_heads(field):
    return field.reshape(field.shape[0], HEADS, HEAD_DIM)


def key_mask(keep_left):
    rows = lax.broadcasted_iota(jnp.int32, (W, 2 * W + NS), 0)
    cols = lax.broadcasted_iota(jnp.int32, (W, 2 * W + NS), 1)
    left_part = (cols < W) & keep_left
    own_part = (cols >= W) & (cols < 2 * W) & (cols - W <= rows)
    return left_part | own_part | (cols >= 2 * W)


def body(
    tokens,
    item_starts,
    attn_gain,
    query_weight,
    key_weight,
    value_weight,
    output_weight,
    state_queries,
    state_weight,
    gate_bias,
    initial_state,
    mlp_gain,
    up_weight,
    down_weight,
    out_cotangent,
    state_cotangent,
):
    scale = 1.0 / math.sqrt(HEAD_DIM)
    inputs = tokens[0].astype(jnp.float32)
    start_flag = item_starts[0, 0]
    start = start_flag.astype(jnp.float32)
    keep = 1.0 - start
    attn_scale = rms_scale(inputs)
    normed = (inputs * attn_scale * attn_gain).astype(jnp.bfloat16)
    queries = product(normed, query_weight).astype(jnp.bfloat16)
    keys = product(normed, key_weight).astype(jnp.bfloat16)
    values = product(normed, value_weight).astype(jnp.bfloat16)
    left_keys = shifted(keys, "seq", 1)
    left_values = shifted(values, "seq", 1)
    query_heads = split_heads(state_queries)
    key_heads = split_heads(keys)
    value_heads = split_heads(values)
    summary_raw = (
        jnp.einsum("nhd,whd->hnw", query_heads, key_heads, preferred_element_type=jnp.float32)
        * scale
    )
    summary_peak = jnp.max(summary_raw, axis=-1, keepdims=True)
    summary_exp = jnp.exp(summary_raw - summary_peak)
    summary_total = jnp.sum(summary_exp, axis=-1, keepdims=True)
    summary_lse = summary_peak + jnp.log(summary_total)
    summary_low = (summary_exp / summary_total).astype(jnp.bfloat16)
    summary = jnp.einsum(
        "hnw,whd->nhd", summary_low, value_heads, preferred_element_type=jnp.float32
    )
    summary = summary.reshape(NS, D).astype(jnp.bfloat16)
    projected = product(summary, state_weight)
    update = projected[:, :D]
    forget = jax.nn.sigmoid(projected[:, D:] + gate_bias)
    fresh = (1.0 - forget) * update
    carried_scale = keep * forget
    carried_base = start * forget * initial_state + fresh
    previous, kept_scales = scan_states(carried_scale, carried_base)
    state_in = keep * previous + start * initial_state
    state_out = forget * state_in + fresh
    state_low = state_in.astype(jnp.bfloat16)
    state_keys = product(state_low, key_weight).astype(jnp.bfloat16)
    state_values = product(state_low, value_weight).astype(jnp.bfloat16)
    seen_keys = split_heads(jnp.concatenate([left_keys, keys, state_keys], axis=0))
    seen_values = split_heads(jnp.concatenate([left_values, values, state_values], axis=0))
    token_heads = split_heads(queries)
    valid = key_mask(start_flag == 0)
    raw = jnp.einsum("whd,khd->hwk", token_heads, seen_keys, preferred_element_type=jnp.float32)
    scores = jnp.where(valid, raw * scale, NEGATIVE)
    peak = jnp.max(scores, axis=-1, keepdims=True)
    expos = jnp.exp(scores - peak)
    totals = jnp.sum(expos, axis=-1, keepdims=True)
    log_total = peak + jnp.log(totals)
    probs_low = (expos / totals).astype(jnp.bfloat16)
    attended = jnp.einsum(
        "hwk,khd->whd", probs_low, seen_values, preferred_element_type=jnp.float32
    )
    attended = attended.reshape(W, D).astype(jnp.bfloat16)
    hidden = inputs + product(attended, output_weight)
    mlp_scale = rms_scale(hidden)
    normed_mlp = (hidden * mlp_scale * mlp_gain).astype(jnp.bfloat16)
    upper = product(normed_mlp, up_weight)
    activated = gelu_tanh(upper).astype(jnp.bfloat16)
    mixed = (hidden + product(activated, down_weight)).astype(jnp.bfloat16)
    cotangent = out_cotangent[0]
    down_grad = sum_over_dp(weight_scatter(activated, cotangent, True))
    activated_grad = product_nt(cotangent, down_weight).astype(jnp.bfloat16)
    upper_grad = (activated_grad.astype(jnp.float32) * gelu_slope(upper)).astype(jnp.bfloat16)
    up_grad = sum_over_dp(weight_scatter(normed_mlp, upper_grad, False))
    normed_mlp_grad = product_nt(upper_grad, up_weight)
    mlp_gain_grad, hidden_part = rms_back(hidden, mlp_scale, mlp_gain, normed_mlp_grad)
    hidden_grad = hidden_part + cotangent.astype(jnp.float32)
    attended_grad = hidden_grad.astype(jnp.bfloat16)
    output_grad = sum_over_dp(weight_scatter(attended, attended_grad, True))
    attended_heads_grad = split_heads(product_nt(attended_grad, output_weight).astype(jnp.bfloat16))
    again = jnp.einsum("whd,khd->hwk", token_heads, seen_keys, preferred_element_type=jnp.float32)
    probs = jnp.exp(jnp.where(valid, again * scale, NEGATIVE) - log_total)
    probs_again = probs.astype(jnp.bfloat16)
    prob_grad = jnp.einsum(
        "whd,khd->hwk", attended_heads_grad, seen_values, preferred_element_type=jnp.float32
    )
    seen_values_grad = jnp.einsum(
        "hwk,whd->khd", probs_again, attended_heads_grad, preferred_element_type=jnp.float32
    ).reshape(2 * W + NS, D)
    rowdot = jnp.sum(probs * prob_grad, axis=-1, keepdims=True)
    score_grad = (probs * (prob_grad - rowdot) * scale).astype(jnp.bfloat16)
    queries_grad = (
        jnp.einsum("hwk,khd->whd", score_grad, seen_keys, preferred_element_type=jnp.float32)
        .reshape(W, D)
        .astype(jnp.bfloat16)
    )
    seen_keys_grad = jnp.einsum(
        "hwk,whd->khd", score_grad, token_heads, preferred_element_type=jnp.float32
    ).reshape(2 * W + NS, D)
    state_keys_grad = seen_keys_grad[2 * W :].astype(jnp.bfloat16)
    state_values_grad = seen_values_grad[2 * W :].astype(jnp.bfloat16)
    direct = product_nt(state_keys_grad, key_weight) + product_nt(state_values_grad, value_weight)
    state_cot = state_cotangent[0, 0]
    back_base = keep * (forget * state_cot + direct)
    incoming = scan_grads(back_base, kept_scales)
    out_state_grad = state_cot + incoming
    in_state_grad = forget * out_state_grad + direct
    initial_state_grad = start * in_state_grad
    gate_grad = out_state_grad * (state_in - update) * forget * (1.0 - forget)
    gate_bias_grad = jnp.sum(gate_grad, axis=0)
    projected_grad = jnp.concatenate([out_state_grad * (1.0 - forget), gate_grad], axis=1).astype(
        jnp.bfloat16
    )
    state_weight_grad = sum_over_dp(weight_scatter(summary, projected_grad, False))
    summary_grad = split_heads(product_nt(projected_grad, state_weight).astype(jnp.bfloat16))
    summary_again = jnp.einsum(
        "nhd,whd->hnw", query_heads, key_heads, preferred_element_type=jnp.float32
    )
    summary_probs = jnp.exp(summary_again * scale - summary_lse)
    summary_prob_grad = jnp.einsum(
        "nhd,whd->hnw", summary_grad, value_heads, preferred_element_type=jnp.float32
    )
    summary_rowdot = jnp.sum(summary_probs * summary_prob_grad, axis=-1, keepdims=True)
    summary_score_grad = (summary_probs * (summary_prob_grad - summary_rowdot) * scale).astype(
        jnp.bfloat16
    )
    state_queries_grad = jnp.einsum(
        "hnw,whd->nhd", summary_score_grad, key_heads, preferred_element_type=jnp.float32
    ).reshape(NS, D)
    keys_from_summary = jnp.einsum(
        "hnw,nhd->whd", summary_score_grad, query_heads, preferred_element_type=jnp.float32
    ).reshape(W, D)
    values_from_summary = jnp.einsum(
        "hnw,nhd->whd", summary_low, summary_grad, preferred_element_type=jnp.float32
    ).reshape(W, D)
    returned = (
        shifted(seen_keys_grad[:W].astype(jnp.bfloat16), "seq", -1).astype(jnp.float32),
        shifted(seen_values_grad[:W].astype(jnp.bfloat16), "seq", -1).astype(jnp.float32),
    )
    keys_total = (seen_keys_grad[W : 2 * W] + keys_from_summary + returned[0]).astype(jnp.bfloat16)
    values_total = (seen_values_grad[W : 2 * W] + values_from_summary + returned[1]).astype(
        jnp.bfloat16
    )
    query_grad = sum_over_dp(weight_scatter(normed, queries_grad, False))
    both = jnp.concatenate([normed, state_low], axis=0)
    key_grad = sum_over_dp(
        weight_scatter(both, jnp.concatenate([keys_total, state_keys_grad], axis=0), True)
    )
    value_grad = sum_over_dp(
        weight_scatter(both, jnp.concatenate([values_total, state_values_grad], axis=0), False)
    )
    normed_grad = (
        product_nt(queries_grad, query_weight)
        + product_nt(keys_total, key_weight)
        + product_nt(values_total, value_weight)
    )
    attn_gain_grad, token_part = rms_back(inputs, attn_scale, attn_gain, normed_grad)
    tokens_grad = hidden_grad + token_part
    count = lax.axis_size("seq")
    vectors = jnp.stack([attn_gain_grad, gate_bias_grad, mlp_gain_grad]).reshape(3, count, D // count)
    vectors = vectors.transpose(1, 0, 2).reshape(count, 1, 3 * (D // count))
    vectors = jnp.pad(vectors, ((0, 0), (0, 7), (0, D - vectors.shape[2])))
    rest = jnp.concatenate(
        [
            state_queries_grad.reshape(count, NS // count, D),
            initial_state_grad.reshape(count, NS // count, D),
            vectors,
        ],
        axis=1,
    ).astype(jnp.bfloat16)
    rest = whole_scatter(rest.reshape(-1, D), True)
    rest = sum_over_dp(rest)
    rows, lanes = NS // count, D // count
    state_queries_grad = rest[:rows]
    initial_state_grad = rest[rows : 2 * rows]
    vectors = rest[2 * rows, : 3 * lanes]
    attn_gain_grad, gate_bias_grad, mlp_gain_grad = (
        vectors[:lanes],
        vectors[lanes : 2 * lanes],
        vectors[2 * lanes :],
    )
    return (
        mixed[None],
        state_out[None, None],
        tokens_grad[None],
        attn_gain_grad,
        query_grad,
        key_grad,
        value_grad,
        output_grad,
        state_queries_grad,
        state_weight_grad,
        gate_bias_grad,
        initial_state_grad,
        mlp_gain_grad,
        up_grad,
        down_grad,
    )


def solution(mesh):
    in_specs = (
        P("dp", "seq", None),
        P("dp", "seq"),
        P(),
        P(),
        P(),
        P(),
        P(),
        P(),
        P(),
        P(),
        P(),
        P(),
        P(),
        P(),
        P("dp", "seq", None),
        P("dp", "seq", None, None),
    )
    out_specs = (
        P("dp", "seq", None),
        P("dp", "seq", None, None),
        P("dp", "seq", None),
        P("seq"),
        P("seq", None),
        P("seq", None),
        P("seq", None),
        P("seq", None),
        P("seq", None),
        P("seq", None),
        P("seq"),
        P("seq", None),
        P("seq"),
        P("seq", None),
        P("seq", None),
    )
    return jax.shard_map(body, mesh=mesh, in_specs=in_specs, out_specs=out_specs, check_vma=False)
```

```python
import functools
import math

import jax
import jax.numpy as jnp
from jax import lax
from jax.experimental import pallas as pl
from jax.experimental.pallas import tpu as pltpu
from jax.sharding import PartitionSpec as P

D = 1024
HEADS = 8
HEAD_DIM = 128
FF = 4096
W = 512
NS = 512
HALF = NS // 2
QUARTER = NS // 8

EPSILON = 1e-06
NEGATIVE = -1e30
GELU_SCALE = 0.7978845608028654
GELU_CUBIC = 0.044715
SCALE = 1.0 / math.sqrt(HEAD_DIM)
SCALE_LOG2 = SCALE * math.log2(math.e)

BF = jnp.bfloat16
F32 = jnp.float32
MIB = 1 << 20


def swapped(value, axis, distance):
    count = lax.axis_size(axis)
    return lax.ppermute(value, axis, [(place, place ^ distance) for place in range(count)])


def shifted(value, axis, steps):
    count = lax.axis_size(axis)
    first, last = (max(0, -steps), min(count, count - steps))
    return lax.ppermute(value, axis, [(source, source + steps) for source in range(first, last)])


def add_low(*terms):
    total = terms[0].astype(F32)
    for term in terms[1:]:
        total = total + term.astype(F32)
    return total.astype(BF)


def pick(value, index, axis):
    return lax.dynamic_index_in_dim(value, index, axis, False)


def product(left, right):
    return jnp.dot(left, right, preferred_element_type=F32)


def product_tn(left, right):
    return lax.dot_general(left, right, (((0,), (0,)), ((), ())), preferred_element_type=F32)


def product_nt(left, right):
    return lax.dot_general(left, right, (((1,), (1,)), ((), ())), preferred_element_type=F32)


def rms_scale(field):
    return lax.rsqrt(jnp.mean(field * field, axis=-1, keepdims=True) + EPSILON)


def shape(dims, dtype):
    return jax.ShapeDtypeStruct(dims, dtype)


def whole(dims):
    return pl.BlockSpec(dims, lambda *_: (0,) * len(dims))


def fixed(dims):
    return pl.BlockSpec(dims, lambda *_: (0,) * len(dims), pipeline_mode=pl.Buffered(1))


def run(kernel, outs, args, grid, in_specs, out_specs, scratch=(), flops=0, limit=32, flags=None):
    nbytes = sum(math.prod(a.shape) * a.dtype.itemsize for a in args) + sum(
        math.prod(o.shape) * o.dtype.itemsize for o in outs
    )
    prefetch = () if flags is None else (flags,)
    return pl.pallas_call(
        kernel,
        out_shape=outs,
        grid_spec=pltpu.PrefetchScalarGridSpec(
            num_scalar_prefetch=len(prefetch),
            grid=grid,
            in_specs=in_specs,
            out_specs=out_specs,
            scratch_shapes=list(scratch),
        ),
        compiler_params=pltpu.CompilerParams(
            dimension_semantics=("arbitrary",) * len(grid), vmem_limit_bytes=limit * MIB
        ),
        cost_estimate=pl.CostEstimate(
            flops=int(flops), bytes_accessed=int(nbytes), transcendentals=0
        ),
    )(*prefetch, *args)


START, CORE, CHIP = 0, 1, 2


def front_kernel(tokens, gain, wq, wk, wv, normed, queries, pair):
    @pl.when(pl.program_id(0) == 0)
    def _():
        inputs = tokens[...].astype(F32)
        normed[...] = (inputs * rms_scale(inputs) * gain[...]).astype(BF)

    rows = normed[...]
    queries[...] = product(rows, wq[...]).astype(BF)
    pair[0] = product(rows, wk[...]).astype(BF)
    pair[1] = product(rows, wv[...]).astype(BF)


def front(tokens, gain, wq, wk, wv):
    step = 256
    column = pl.BlockSpec((D, step), lambda j: (0, j))
    return run(
        front_kernel,
        (shape((W, D), BF), shape((W, D), BF), shape((2, W, D), BF)),
        (tokens, gain, wq, wk, wv),
        (D // step,),
        [whole((W, D)), whole((1, D)), column, column, column],
        (
            whole((W, D)),
            pl.BlockSpec((W, step), lambda j: (0, j)),
            pl.BlockSpec((2, W, step), lambda j: (0, 0, j)),
        ),
        flops=6 * W * D * D,
    )


def summary_probs_of(keys, asks):
    raw = product_nt(keys, asks) * SCALE_LOG2
    expos = jnp.exp2(raw - jnp.max(raw, axis=0, keepdims=True))
    return expos, jnp.sum(expos, axis=0, keepdims=True)


def gates_kernel(
    flags, asks, pair, wu, wg, bias, initial, summary, forget, update, give, own, work
):
    step = pl.program_id(0)

    @pl.when(step < 4)
    def _():
        for head in range(2):
            at = slice(head * HEAD_DIM, (head + 1) * HEAD_DIM)
            expos, total = summary_probs_of(pair[0, :, at], asks[:, at])
            held = product_tn(pair[1, :, at], expos.astype(BF)) / total
            place = pl.multiple_of(step * 256 + head * HEAD_DIM, HEAD_DIM)
            summary[:, pl.ds(place, HEAD_DIM)] = held.T.astype(BF)

    @pl.when(step >= 4)
    def _():
        start = flags[START].astype(F32)
        rows = summary[...]
        fresh = product(rows, wu[...])
        gate = jax.nn.sigmoid(product(rows, wg[...]) + bias[...])
        update[...] = fresh
        forget[...] = gate
        work[0] = (1.0 - start) * gate
        work[1] = start * gate * initial[...] + (1.0 - gate) * fresh
        mine = pl.multiple_of(flags[CORE] * HALF, HALF)
        others = pl.multiple_of((1 - flags[CORE]) * HALF, HALF)
        for part in range(2):
            own[part] = work[part, pl.ds(mine, HALF)].astype(BF)
            give[part] = work[part, pl.ds(others, HALF)].astype(BF)


def gates(flags, asks, pair, state_weight, bias, initial):
    step = 256
    early = lambda i, *_: (0, jnp.minimum(i, 3))
    late = lambda i, *_: (0, jnp.maximum(i - 4, 0))
    late3 = lambda i, *_: (0, 0, jnp.maximum(i - 4, 0))
    return run(
        gates_kernel,
        (
            shape((NS, D), BF),
            shape((NS, D), F32),
            shape((NS, D), F32),
            shape((2, HALF, D), BF),
            shape((2, HALF, D), BF),
        ),
        (asks, pair, state_weight, state_weight, bias, initial),
        (8,),
        [
            pl.BlockSpec((NS, step), early),
            pl.BlockSpec((2, W, step), lambda i, *_: (0, 0, jnp.minimum(i, 3))),
            pl.BlockSpec((D, step), late),
            pl.BlockSpec((D, step), lambda i, *_: (0, jnp.maximum(i - 4, 0) + D // step)),
            pl.BlockSpec((1, step), late),
            pl.BlockSpec((NS, step), late),
        ],
        (
            whole((NS, D)),
            pl.BlockSpec((NS, step), late),
            pl.BlockSpec((NS, step), late),
            pl.BlockSpec((2, HALF, step), late3),
            pl.BlockSpec((2, HALF, step), late3),
        ),
        [pltpu.VMEM((2, NS, step), F32)],
        flops=4 * NS * W * D + 4 * NS * D * D,
        flags=flags,
    )


def rows_of(chip):
    return pl.ds(pl.multiple_of(chip * QUARTER, QUARTER), QUARTER)


def compose_kernel(flags, own, recv, keep, to1, to2, to3, work):
    odd_core = flags[CORE] == 1
    pick2 = lambda part: (own[part].astype(F32), recv[part].astype(F32))
    (own_scale, recv_scale), (own_base, recv_base) = pick2(0), pick2(1)
    later_scale = jnp.where(odd_core, own_scale, recv_scale)
    earlier_base = jnp.where(odd_core, recv_base, own_base)
    later_base = jnp.where(odd_core, own_base, recv_base)
    work[0] = own_scale * recv_scale
    work[1] = later_scale * earlier_base + later_base
    for far, out in enumerate((keep, to1, to2, to3)):
        out[...] = work[:, rows_of(flags[CHIP] ^ far)].astype(BF)


def prefix_kernel(flags, keep, from1, from2, from3, mine, to1, to2, to3, got, enter):
    for far, came in enumerate((keep, from1, from2, from3)):
        got[flags[CHIP] ^ far] = came[...].astype(F32)
    state = got[0, 1]
    enter[0] = jnp.zeros_like(state)
    enter[1] = state
    for chip in (1, 2):
        state = got[chip, 0] * state + got[chip, 1]
        enter[chip + 1] = state
    for far, out in enumerate((mine, to1, to2, to3)):
        out[...] = enter[flags[CHIP] ^ far].astype(BF)


def previous_kernel(flags, mine, from1, from2, from3, own, recv, keep, give, before):
    for far, came in enumerate((mine, from1, from2, from3)):
        before[rows_of(flags[CHIP] ^ far)] = came[...].astype(F32)
    odd_core = flags[CORE] == 1
    scale = jnp.where(odd_core, recv[0].astype(F32), own[0].astype(F32))
    base = jnp.where(odd_core, recv[1].astype(F32), own[1].astype(F32))
    entry = before[...]
    between = scale * entry + base
    keep[...] = jnp.where(odd_core, between, entry).astype(BF)
    give[...] = jnp.where(odd_core, entry, between).astype(BF)


def compose_back_kernel(flags, own, recv, own_pair, recv_pair, keep, to1, to2, to3, work):
    odd_core = flags[CORE] == 1
    scale = jnp.where(odd_core, recv_pair[0].astype(F32), own_pair[0].astype(F32))
    mine, other = own[...].astype(F32), recv[...].astype(F32)
    work[...] = scale * jnp.where(odd_core, mine, other) + jnp.where(odd_core, other, mine)
    for far, out in enumerate((keep, to1, to2, to3)):
        out[...] = work[rows_of(flags[CHIP] ^ far)].astype(BF)


def suffix_kernel(
    flags, keep, from1, from2, from3, kept0, kept1, kept2, kept3, mine, to1, to2, to3, got, enter
):
    pairs = ((keep, kept0), (from1, kept1), (from2, kept2), (from3, kept3))
    for far, (came, kept) in enumerate(pairs):
        got[flags[CHIP] ^ far, 0] = kept[0].astype(F32)
        got[flags[CHIP] ^ far, 1] = came[...].astype(F32)
    state = got[3, 1]
    enter[3] = jnp.zeros_like(state)
    enter[2] = state
    for chip in (2, 1):
        state = got[chip, 0] * state + got[chip, 1]
        enter[chip - 1] = state
    for far, out in enumerate((mine, to1, to2, to3)):
        out[...] = enter[flags[CHIP] ^ far].astype(BF)


def following_kernel(
    flags, mine, from1, from2, from3, own, recv, own_pair, recv_pair, keep, give, after
):
    for far, came in enumerate((mine, from1, from2, from3)):
        after[rows_of(flags[CHIP] ^ far)] = came[...].astype(F32)
    odd_core = flags[CORE] == 1
    scale = jnp.where(odd_core, own_pair[0].astype(F32), recv_pair[0].astype(F32))
    base = jnp.where(odd_core, own[...].astype(F32), recv[...].astype(F32))
    entry = after[...]
    between = scale * entry + base
    keep[...] = jnp.where(odd_core, entry, between).astype(BF)
    give[...] = jnp.where(odd_core, between, entry).astype(BF)


def small(kernel, outs, args, scratch, flags):
    return run(
        kernel,
        tuple(shape(dims, BF) for dims in outs),
        args,
        (1,),
        [whole(a.shape) for a in args],
        tuple(whole(dims) for dims in outs),
        [pltpu.VMEM(dims, F32) for dims in scratch],
        flops=1,
        limit=16,
        flags=flags,
    )


def to_chips(values):
    return (values[0],) + tuple(
        swapped(value, "seq", 2 * far) for far, value in zip((1, 2, 3), values[1:])
    )


def scan_states(flags, own, give):
    recv = swapped(give, "seq", 1)
    quarters = small(
        compose_kernel, [(2, QUARTER, D)] * 4, (own, recv), [(2, HALF, D)], flags
    )
    got = to_chips(quarters)
    enter = small(
        prefix_kernel, [(QUARTER, D)] * 4, got, [(4, 2, QUARTER, D), (4, QUARTER, D)], flags
    )
    back = to_chips(enter)
    mine, other = small(
        previous_kernel, [(HALF, D)] * 2, back + (own, recv), [(HALF, D)], flags
    )
    return mine, swapped(other, "seq", 1), (own, recv, got)


def scan_grads(flags, own, give, kept):
    own_pair, recv_pair, kept_chips = kept
    recv = swapped(give, "seq", 1)
    quarters = small(
        compose_back_kernel,
        [(QUARTER, D)] * 4,
        (own, recv, own_pair, recv_pair),
        [(HALF, D)],
        flags,
    )
    got = to_chips(quarters)
    enter = small(
        suffix_kernel,
        [(QUARTER, D)] * 4,
        got + kept_chips,
        [(4, 2, QUARTER, D), (4, QUARTER, D)],
        flags,
    )
    back = to_chips(enter)
    mine, other = small(
        following_kernel,
        [(HALF, D)] * 2,
        back + (own, recv, own_pair, recv_pair),
        [(HALF, D)],
        flags,
    )
    return mine, swapped(other, "seq", 1)


def state_kernel(
    flags, mine, other, initial, forget, update, wk, wv, state_in, state_low, state_out, pair
):
    @pl.when(pl.program_id(0) == 0)
    def _():
        start = flags[START].astype(F32)
        for core, came in ((flags[CORE], mine), (1 - flags[CORE], other)):
            rows = pl.ds(pl.multiple_of(core * HALF, HALF), HALF)
            entry = (1.0 - start) * came[...].astype(F32) + start * initial[rows, :]
            gate = forget[rows, :]
            state_in[rows, :] = entry
            state_low[rows, :] = entry.astype(BF)
            state_out[rows, :] = gate * entry + (1.0 - gate) * update[rows, :]

    rows = state_low[...]
    pair[0] = product(rows, wk[...]).astype(BF)
    pair[1] = product(rows, wv[...]).astype(BF)


def state_pair(flags, mine, other, initial, forget, update, wk, wv):
    step = 256
    column = pl.BlockSpec((D, step), lambda j, *_: (0, j))
    return run(
        state_kernel,
        (shape((NS, D), F32), shape((NS, D), BF), shape((NS, D), F32), shape((2, NS, D), BF)),
        (mine, other, initial, forget, update, wk, wv),
        (D // step,),
        [whole((HALF, D))] * 2 + [whole((NS, D))] * 3 + [column, column],
        (
            whole((NS, D)),
            whole((NS, D)),
            whole((NS, D)),
            pl.BlockSpec((2, NS, step), lambda j, *_: (0, 0, j)),
        ),
        flops=4 * NS * D * D,
        flags=flags,
    )


def masked_scores(flags, queries, left, own, state):
    seen = []
    left_bias = jnp.where(flags[START] == 0, 0.0, NEGATIVE).astype(F32)
    seen.append(product_nt(left[0], queries) * SCALE_LOG2 + left_bias)
    rows = lax.broadcasted_iota(jnp.int32, (W, W), 0)
    cols = lax.broadcasted_iota(jnp.int32, (W, W), 1)
    seen.append(jnp.where(rows <= cols, product_nt(own[0], queries) * SCALE_LOG2, NEGATIVE))
    seen.append(product_nt(state[0], queries) * SCALE_LOG2)
    return seen


def attend_kernel(flags, queries, left, own, state, attended, lse):
    seen = masked_scores(flags, queries[...], left, own, state)
    peak = functools.reduce(
        jnp.maximum, [jnp.max(part, axis=0, keepdims=True) for part in seen]
    )
    held = 0.0
    total = 0.0
    for part, pair in zip(seen, (left, own, state)):
        expos = jnp.exp2(part - peak)
        total = total + jnp.sum(expos, axis=0, keepdims=True)
        held = held + product_tn(pair[1], expos.astype(BF))
    attended[...] = (held / total).T.astype(BF)
    lse[0] = peak + jnp.log2(total)


def attend(flags, queries, left, own, state):
    head = pl.BlockSpec((W, HEAD_DIM), lambda h, *_: (0, h))
    pair = pl.BlockSpec((2, W, HEAD_DIM), lambda h, *_: (0, 0, h))
    return run(
        attend_kernel,
        (shape((W, D), BF), shape((HEADS, 1, W), F32)),
        (queries, left, own, state),
        (HEADS,),
        [head, pair, pair, pair],
        (head, pl.BlockSpec((1, 1, W), lambda h, *_: (h, 0, 0))),
        flops=4 * W * (2 * W + NS) * D,
        flags=flags,
    )


def attend_back_kernel(
    flags, queries, left, own, state, grad, lse, queries_grad, left_grad, own_grad, state_grad
):
    asks, out_grad = queries[...], grad[...]
    seen = masked_scores(flags, asks, left, own, state)
    probs = [jnp.exp2(part - lse[0]) for part in seen]
    pairs = (left, own, state)
    prob_grads = [product_nt(pair[1], out_grad) for pair in pairs]
    rowdot = sum(
        jnp.sum(prob * prob_grad, axis=0, keepdims=True)
        for prob, prob_grad in zip(probs, prob_grads)
    )
    total = 0.0
    for prob, prob_grad, pair, out in zip(
        probs, prob_grads, pairs, (left_grad, own_grad, state_grad)
    ):
        score_grad = (prob * (prob_grad - rowdot)).astype(BF)
        out[0] = (product(score_grad, asks) * SCALE).astype(out.dtype)
        out[1] = product(prob.astype(BF), out_grad).astype(out.dtype)
        total = total + product_tn(pair[0], score_grad)
    queries_grad[...] = (total * SCALE).T.astype(BF)


def attend_back(flags, queries, left, own, state, grad, lse):
    head = pl.BlockSpec((W, HEAD_DIM), lambda h, *_: (0, h))
    pair = pl.BlockSpec((2, W, HEAD_DIM), lambda h, *_: (0, 0, h))
    return run(
        attend_back_kernel,
        (shape((W, D), BF), shape((2, W, D), BF), shape((2, W, D), F32), shape((2, NS, D), BF)),
        (queries, left, own, state, grad, lse),
        (HEADS,),
        [head, pair, pair, pair, head, pl.BlockSpec((1, 1, W), lambda h, *_: (h, 0, 0))],
        (head, pair, pair, pair),
        flops=10 * W * (2 * W + NS) * D,
        limit=48,
        flags=flags,
    )


def gelu_parts(upper):
    square = upper * upper
    inner = GELU_SCALE * (upper + GELU_CUBIC * square * upper)
    bent = jnp.tanh(inner)
    value = 0.5 * upper * (1.0 + bent)
    slope = 0.5 * (1.0 + bent) + 0.5 * upper * (1.0 - bent * bent) * GELU_SCALE * (
        1.0 + 3.0 * GELU_CUBIC * square
    )
    return value, slope


def mlp_kernel(
    attended,
    tokens,
    out_weight,
    gain,
    cotangent,
    up,
    down,
    mixed,
    activated,
    upper_grad,
    normed_mlp,
    hidden_grad,
    attended_grad,
    heads_grad,
    gain_grad,
    hidden,
    total,
    grad,
):
    step = pl.program_id(0)

    @pl.when(step == 0)
    def _():
        field = tokens[...].astype(F32) + product(attended[...], out_weight[...])
        hidden[...] = field
        normed_mlp[...] = (field * rms_scale(field) * gain[...]).astype(BF)
        total[...] = field
        grad[...] = jnp.zeros_like(field)

    value, slope = gelu_parts(product(normed_mlp[...], up[...]))
    value = value.astype(BF)
    activated[...] = value
    total[...] += product(value, down[...])
    back = product_nt(cotangent[...], down[...]).astype(BF).astype(F32)
    back = (back * slope).astype(BF)
    upper_grad[...] = back
    grad[...] += product_nt(back, up[...])

    @pl.when(step == pl.num_programs(0) - 1)
    def _():
        mixed[...] = total[...].astype(BF)
        field = hidden[...]
        scaled = rms_scale(field)
        gain_grad[...] = jnp.sum(grad[...] * field * scaled, axis=0, keepdims=True)
        weighted = grad[...] * gain[...]
        field_grad = (
            cotangent[...].astype(F32)
            + scaled * weighted
            - field
            * (scaled * scaled * scaled * jnp.mean(weighted * field, axis=-1, keepdims=True))
        )
        hidden_grad[...] = field_grad
        low = field_grad.astype(BF)
        attended_grad[...] = low
        heads_grad[...] = product_nt(low, out_weight[...]).astype(BF)


def mlp(attended, tokens, out_weight, gain, cotangent, up, down):
    step = 512
    rows = whole((W, D))
    return run(
        mlp_kernel,
        (
            shape((W, D), BF),
            shape((W, FF), BF),
            shape((W, FF), BF),
            shape((W, D), BF),
            shape((W, D), F32),
            shape((W, D), BF),
            shape((W, D), BF),
            shape((1, D), F32),
        ),
        (attended, tokens, out_weight, gain, cotangent, up, down),
        (FF // step,),
        [
            fixed((W, D)),
            fixed((W, D)),
            fixed((D, D)),
            fixed((1, D)),
            fixed((W, D)),
            pl.BlockSpec((D, step), lambda j: (0, j)),
            pl.BlockSpec((step, D), lambda j: (j, 0)),
        ],
        (
            rows,
            pl.BlockSpec((W, step), lambda j: (0, j)),
            pl.BlockSpec((W, step), lambda j: (0, j)),
            rows,
            rows,
            rows,
            rows,
            whole((1, D)),
        ),
        [pltpu.VMEM((W, D), F32)] * 3,
        flops=8 * W * D * FF + 4 * W * D * D,
        limit=48,
    )


def direct_kernel(flags, state_grad, wk, wv, forget, cotangent, direct, own, give, work):
    grad = product_nt(state_grad[0], wk[...]) + product_nt(state_grad[1], wv[...])
    direct[...] = grad
    keep = 1.0 - flags[START].astype(F32)
    work[...] = keep * (forget[...] * cotangent[...] + grad)
    own[...] = work[pl.ds(pl.multiple_of(flags[CORE] * HALF, HALF), HALF)].astype(BF)
    give[...] = work[pl.ds(pl.multiple_of((1 - flags[CORE]) * HALF, HALF), HALF)].astype(BF)


def direct_grad(flags, state_grad, wk, wv, forget, cotangent):
    step = 256
    row = pl.BlockSpec((step, D), lambda j, *_: (j, 0))
    column = pl.BlockSpec((NS, step), lambda j, *_: (0, j))
    half = pl.BlockSpec((HALF, step), lambda j, *_: (0, j))
    return run(
        direct_kernel,
        (shape((NS, D), F32), shape((HALF, D), BF), shape((HALF, D), BF)),
        (state_grad, wk, wv, forget, cotangent),
        (D // step,),
        [whole((2, NS, D)), row, row, column, column],
        (column, half, half),
        [pltpu.VMEM((NS, step), F32)],
        flops=4 * NS * D * D,
        flags=flags,
    )


def state_back_kernel(
    flags,
    mine,
    other,
    cotangent,
    forget,
    update,
    state_in,
    direct,
    wu,
    wg,
    initial_grad,
    projected_grad,
    bias_grad,
    summary_grad,
    work,
    total,
):
    step = pl.program_id(0)
    for core, came in ((flags[CORE], mine), (1 - flags[CORE], other)):
        work[pl.ds(pl.multiple_of(core * HALF, HALF), HALF)] = came[...].astype(F32)
    out_grad = cotangent[...] + work[...]
    gate = forget[...]
    start = flags[START].astype(F32)
    initial_grad[...] = (start * (gate * out_grad + direct[...])).astype(BF)
    rest = 1.0 - gate
    gate_grad = out_grad * (state_in[...] - update[...]) * gate * rest
    bias_grad[...] = jnp.sum(gate_grad, axis=0, keepdims=True)
    fresh_grad = (out_grad * rest).astype(BF)
    gate_low = gate_grad.astype(BF)
    projected_grad[0] = fresh_grad
    projected_grad[1] = gate_low
    part = product_nt(fresh_grad, wu[...]) + product_nt(gate_low, wg[...])

    @pl.when(step == 0)
    def _():
        total[...] = part

    @pl.when(step > 0)
    def _():
        total[...] += part

    @pl.when(step == pl.num_programs(0) - 1)
    def _():
        summary_grad[...] = total[...].astype(BF)


def state_back(flags, mine, other, cotangent, forget, update, state_in, direct, state_weight):
    step = 256
    column = pl.BlockSpec((NS, step), lambda j, *_: (0, j))
    half = pl.BlockSpec((HALF, step), lambda j, *_: (0, j))
    return run(
        state_back_kernel,
        (
            shape((NS, D), BF),
            shape((2, NS, D), BF),
            shape((1, D), F32),
            shape((NS, D), BF),
        ),
        (mine, other, cotangent, forget, update, state_in, direct, state_weight, state_weight),
        (D // step,),
        [half, half, column, column, column, column, column]
        + [
            pl.BlockSpec((D, step), lambda j, *_: (0, j)),
            pl.BlockSpec((D, step), lambda j, *_: (0, j + D // step)),
        ],
        (
            column,
            pl.BlockSpec((2, NS, step), lambda j, *_: (0, 0, j)),
            pl.BlockSpec((1, step), lambda j, *_: (0, j)),
            whole((NS, D)),
        ),
        [pltpu.VMEM((NS, step), F32), pltpu.VMEM((NS, D), F32)],
        flops=4 * NS * D * D,
        flags=flags,
    )


def summary_back_kernel(asks, pair, grad, own_grad, returned, asks_grad, pair_total):
    queries, out_grad = asks[...], grad[...]
    expos, total = summary_probs_of(pair[0], queries)
    probs = expos * (1.0 / total)
    prob_grad = product_nt(pair[1], out_grad)
    rowdot = jnp.sum(probs * prob_grad, axis=0, keepdims=True)
    score_grad = (probs * (prob_grad - rowdot)).astype(BF)
    asks_grad[...] = (product_tn(pair[0], score_grad) * SCALE).T.astype(BF)
    pair_total[0] = (
        own_grad[0] + returned[0].astype(F32) + product(score_grad, queries) * SCALE
    ).astype(BF)
    pair_total[1] = (
        own_grad[1] + returned[1].astype(F32) + product(probs.astype(BF), out_grad)
    ).astype(BF)


def summary_back(asks, pair, grad, own_grad, returned):
    head = pl.BlockSpec((W, HEAD_DIM), lambda h: (0, h))
    both = pl.BlockSpec((2, W, HEAD_DIM), lambda h: (0, 0, h))
    return run(
        summary_back_kernel,
        (shape((NS, D), BF), shape((2, W, D), BF)),
        (asks, pair, grad, own_grad, returned),
        (HEADS,),
        [head, both, head, both, both],
        (head, both),
        flops=10 * NS * W * D,
    )


def tokens_back_kernel(
    queries_grad, pair_total, wq, wk, wv, tokens, gain, hidden_grad, tokens_grad, gain_grad, total
):
    step = pl.program_id(0)

    @pl.when(step < 2)
    def _():
        part = product_nt(queries_grad[...], wq[...])
        total[...] = jnp.where(step == 0, part, total[...] + part)

    @pl.when((step >= 2) & (step < 4))
    def _():
        total[...] += product_nt(pair_total[0], wk[...])

    @pl.when(step >= 4)
    def _():
        total[...] += product_nt(pair_total[0], wv[...])

    @pl.when(step == 5)
    def _():
        inputs = tokens[...].astype(F32)
        scaled = rms_scale(inputs)
        grad = total[...]
        gain_grad[...] = jnp.sum(grad * inputs * scaled, axis=0, keepdims=True)
        weighted = grad * gain[...]
        tokens_grad[...] = (
            hidden_grad[...]
            + scaled * weighted
            - inputs
            * (scaled * scaled * scaled * jnp.mean(weighted * inputs, axis=-1, keepdims=True))
        )


def tokens_back(queries_grad, pair_total, wq, wk, wv, tokens, gain, hidden_grad):
    step = D // 2
    clamp = lambda i, low: jnp.clip(i - low, 0, 1)
    weight = lambda low: pl.BlockSpec((D, step), lambda i: (0, clamp(i, low)))
    later = lambda i: jnp.maximum(i - 2, 0)
    return run(
        tokens_back_kernel,
        (shape((W, D), F32), shape((1, D), F32)),
        (queries_grad, pair_total, wq, wk, wv, tokens, gain, hidden_grad),
        (6,),
        [
            pl.BlockSpec((W, step), lambda i: (0, clamp(i, 0))),
            pl.BlockSpec((1, W, step), lambda i: (later(i) // 2, 0, later(i) % 2)),
            weight(0),
            weight(2),
            weight(4),
            whole((W, D)),
            whole((1, D)),
            whole((W, D)),
        ],
        (whole((W, D)), whole((1, D))),
        [pltpu.VMEM((W, D), F32)],
        flops=6 * W * D * D,
    )


def weight_kernel(chunk_of, rows, pairs, merge, flags, *refs):
    lefts, rights = refs[: 2 * pairs : 2], refs[1 : 2 * pairs : 2]
    recv = refs[2 * pairs] if merge else None
    outs, work = refs[2 * pairs + merge : -1], refs[-1]

    @pl.when(pl.program_id(0) == 0)
    def _():
        for pair, left in enumerate(lefts):
            for place in range(4):
                chunk = 2 * chunk_of(flags, place) + (
                    flags[CORE] if merge else 1 - flags[CORE]
                )
                block = left[:, pl.ds(pl.multiple_of(chunk * rows, rows), rows)]
                work[pair, place * rows : (place + 1) * rows] = block.T

    total = product(work[0], rights[0][0])
    for pair in range(1, pairs):
        total = total + product(work[pair], rights[pair][0])
    for place in range(4):
        part = total[place * rows : (place + 1) * rows]
        if merge:
            part = part + recv[chunk_of(flags, place)].astype(F32)
            outs[place // 2][place % 2] = part.astype(BF)
        else:
            outs[0][place] = part.astype(BF)


def chunk_natural(flags, place):
    return place


def chunk_along_x(flags, place):
    x = flags[CHIP] & 1
    return 2 * (place % 2) + (1 - x if place < 2 else x)


def chunk_along_y(flags, place):
    y = flags[CHIP] >> 1
    return 2 * (1 - y if place < 2 else y) + place % 2


def weight_part(flags, chunk_of, pairs, recv):
    left, right = pairs[0]
    rows = left.shape[1] // 8
    blocks, tokens, width = right.shape
    columns = blocks * width
    step = 512
    per = width // step
    specs, args = [], []
    for one, two in pairs:
        specs += [
            fixed(one.shape),
            pl.BlockSpec((1, tokens, step), lambda j, *_: (j // per, 0, j % per)),
        ]
        args += [one, two]
    merge = recv is not None
    if merge:
        specs.append(pl.BlockSpec((4, rows, step), lambda j, *_: (0, 0, j)))
        args.append(recv)
        outs = (shape((2, rows, columns), BF),) * 2
        out_specs = (pl.BlockSpec((2, rows, step), lambda j, *_: (0, 0, j)),) * 2
    else:
        outs = (shape((4, rows, columns), BF),)
        out_specs = (pl.BlockSpec((4, rows, step), lambda j, *_: (0, 0, j)),)
    return run(
        functools.partial(weight_kernel, chunk_of, rows, len(pairs), int(merge)),
        outs,
        tuple(args),
        (columns // step,),
        specs,
        out_specs,
        [pltpu.VMEM((len(pairs), 4 * rows, tokens), BF)],
        flops=len(pairs) * tokens * left.shape[1] * columns,
        flags=flags,
        limit=40,
    )


def scatter_bits(value, bits, names):
    place = lax.axis_index("seq")
    names = list(names)
    for bit in bits:
        at = names.index(bit)
        mine = (place >> bit) & 1
        recv = swapped(pick(value, 1 - mine, at), "seq", 1 << bit)
        value = add_low(pick(value, mine, at), recv)
        names.pop(at)
    return value


def whole_scatter(value, along_x):
    count = lax.axis_size("seq")
    levels = count.bit_length() - 1
    names = list(range(levels - 1, -1, -1))
    value = value.reshape((2,) * levels + (value.shape[0] // count,) + value.shape[1:])
    bits = [0] + (names[-2::-1] if along_x else names[:-1])
    return scatter_bits(value, bits, names)


def weight_scatter(flags, pairs, along_x):
    count = lax.axis_size("seq")
    rows = pairs[0][0].shape[1] // count
    if count != 8:
        total = sum(
            product_tn(left, right.transpose(1, 0, 2).reshape(left.shape[0], -1))
            for left, right in pairs
        )
        return whole_scatter(total.astype(BF), along_x)
    (give,) = weight_part(flags, chunk_natural, pairs, None)
    recv = swapped(give, "seq", 1)
    send, keep = weight_part(flags, chunk_along_x if along_x else chunk_along_y, pairs, recv)
    near, far = (2, 4) if along_x else (4, 2)
    recv = swapped(send, "seq", near)
    mine = (flags[CHIP] >> 1) & 1 if along_x else flags[CHIP] & 1
    send = add_low(pick(keep, 1 - mine, 0), pick(recv, 1 - mine, 0))
    last = swapped(send, "seq", far)
    return add_low(pick(keep, mine, 0), pick(recv, mine, 0), last)


def sum_over_dp(value):
    count, place = lax.axis_size("dp"), lax.axis_index("dp")
    half = count // 2
    for step in range(half - 1):
        value = add_low(
            value,
            lax.ppermute(value, "dp", [(step, step + 1), (count - 1 - step, count - 2 - step)]),
        )
    value = add_low(value, lax.ppermute(value, "dp", [(half - 1, half), (half, half - 1)]))
    for step in range(half - 2, -1, -1):
        recv = lax.ppermute(value, "dp", [(step + 1, step), (count - 2 - step, count - 1 - step)])
        outer = (place == step) | (place == count - 1 - step)
        value = jnp.where(outer, recv, value)
    return value.astype(F32)


def body(
    tokens,
    item_starts,
    attn_gain,
    query_weight,
    key_weight,
    value_weight,
    output_weight,
    state_queries,
    state_weight,
    gate_bias,
    initial_state,
    mlp_gain,
    up_weight,
    down_weight,
    out_cotangent,
    state_cotangent,
):
    count = lax.axis_size("seq")
    place = lax.axis_index("seq")
    flags = jnp.stack([item_starts[0, 0], place & 1, (place >> 1) & 3]).astype(jnp.int32)
    tokens, cotangent, state_cot = tokens[0], out_cotangent[0], state_cotangent[0, 0]
    attn_gain, gate_bias, mlp_gain = attn_gain[None], gate_bias[None], mlp_gain[None]

    normed, queries, own = front(tokens, attn_gain, query_weight, key_weight, value_weight)
    left = shifted(own, "seq", 1)
    summary, forget, update, give_scan, own_scan = gates(
        flags, state_queries, own, state_weight, gate_bias, initial_state
    )
    mine, other, kept = scan_states(flags, own_scan, give_scan)
    state_in, state_low, state_out, state = state_pair(
        flags, mine, other, initial_state, forget, update, key_weight, value_weight
    )
    attended, lse = attend(flags, queries, left, own, state)
    (
        mixed,
        activated,
        upper_grad,
        normed_mlp,
        hidden_grad,
        attended_grad,
        heads_grad,
        mlp_gain_grad,
    ) = mlp(attended, tokens, output_weight, mlp_gain, cotangent, up_weight, down_weight)

    down_grad = weight_scatter(flags, [(activated, cotangent[None])], True)
    up_grad = weight_scatter(flags, [(normed_mlp, upper_grad[None])], False)
    output_grad = weight_scatter(flags, [(attended, attended_grad[None])], True)

    queries_grad, left_grad, own_grad, state_grad = attend_back(
        flags, queries, left, own, state, heads_grad, lse
    )
    query_grad = weight_scatter(flags, [(normed, queries_grad[None])], False)
    returned = shifted(left_grad, "seq", -1)
    direct, own_scan, give_scan = direct_grad(
        flags, state_grad, key_weight, value_weight, forget, state_cot
    )
    mine, other = scan_grads(flags, own_scan, give_scan, kept)
    initial_grad, projected_grad, gate_bias_grad, summary_grad = state_back(
        flags, mine, other, state_cot, forget, update, state_in, direct, state_weight
    )
    state_weight_grad = weight_scatter(flags, [(summary, projected_grad)], True)
    state_queries_grad, pair_total = summary_back(
        state_queries, own, summary_grad, own_grad, returned
    )
    pair_grad = weight_scatter(flags, [(normed, pair_total), (state_low, state_grad)], False)
    tokens_grad, attn_gain_grad = tokens_back(
        queries_grad,
        pair_total,
        query_weight,
        key_weight,
        value_weight,
        tokens,
        attn_gain,
        hidden_grad,
    )

    lanes, rows = D // count, NS // count
    vectors = jnp.concatenate([attn_gain_grad, gate_bias_grad, mlp_gain_grad])
    vectors = vectors.reshape(3, count, lanes).transpose(1, 0, 2).reshape(count, 1, 3 * lanes)
    vectors = jnp.pad(vectors, ((0, 0), (0, 7), (0, D - 3 * lanes))).astype(BF)
    rest = jnp.concatenate(
        [
            state_queries_grad.reshape(count, rows, D),
            initial_grad.reshape(count, rows, D),
            vectors,
        ],
        axis=1,
    )
    rest = whole_scatter(rest.reshape(-1, D), True)

    down_grad = sum_over_dp(down_grad)
    up_grad = sum_over_dp(up_grad)
    output_grad = sum_over_dp(output_grad)
    query_grad = sum_over_dp(query_grad)
    state_weight_grad = sum_over_dp(state_weight_grad)
    pair_grad = sum_over_dp(pair_grad)
    rest = sum_over_dp(rest)
    vectors = rest[2 * rows, : 3 * lanes]
    return (
        mixed[None],
        state_out[None, None],
        tokens_grad[None],
        vectors[:lanes],
        query_grad,
        pair_grad[:, :D],
        pair_grad[:, D:],
        output_grad,
        rest[:rows],
        state_weight_grad,
        vectors[lanes : 2 * lanes],
        rest[rows : 2 * rows],
        vectors[2 * lanes :],
        up_grad,
        down_grad,
    )


def solution(mesh):
    in_specs = (
        P("dp", "seq", None),
        P("dp", "seq"),
        P(),
        P(),
        P(),
        P(),
        P(),
        P(),
        P(),
        P(),
        P(),
        P(),
        P(),
        P(),
        P("dp", "seq", None),
        P("dp", "seq", None, None),
    )
    out_specs = (
        P("dp", "seq", None),
        P("dp", "seq", None, None),
        P("dp", "seq", None),
        P("seq"),
        P("seq", None),
        P("seq", None),
        P("seq", None),
        P("seq", None),
        P("seq", None),
        P("seq", None),
        P("seq"),
        P("seq", None),
        P("seq"),
        P("seq", None),
        P("seq", None),
    )
    return jax.shard_map(body, mesh=mesh, in_specs=in_specs, out_specs=out_specs, check_vma=False)
```

```python
import functools
import math

import jax
import jax.numpy as jnp
from jax import lax
from jax.experimental import pallas as pl
from jax.experimental.pallas import tpu as pltpu
from jax.sharding import PartitionSpec as P

D = 1024
HEADS = 8
HEAD_DIM = 128
FF = 4096
W = 512
NS = 512
HALF = NS // 2
QUARTER = NS // 8

EPSILON = 1e-06
NEGATIVE = -1e30
GELU_SCALE = 0.7978845608028654
GELU_CUBIC = 0.044715
SCALE = 1.0 / math.sqrt(HEAD_DIM)
SCALE_LOG2 = SCALE * math.log2(math.e)

BF = jnp.bfloat16
F32 = jnp.float32
MIB = 1 << 20
LONG = 1e11


def swapped(value, axis, distance):
    count = lax.axis_size(axis)
    return lax.ppermute(value, axis, [(place, place ^ distance) for place in range(count)])


def shifted(value, axis, steps):
    count = lax.axis_size(axis)
    first, last = (max(0, -steps), min(count, count - steps))
    return lax.ppermute(value, axis, [(source, source + steps) for source in range(first, last)])


def add_low(*terms):
    total = terms[0].astype(F32)
    for term in terms[1:]:
        total = total + term.astype(F32)
    return total.astype(BF)


def pick(value, index, axis):
    return lax.dynamic_index_in_dim(value, index, axis, False)


def product(left, right):
    return jnp.dot(left, right, preferred_element_type=F32)


def product_tn(left, right):
    return lax.dot_general(left, right, (((0,), (0,)), ((), ())), preferred_element_type=F32)


def product_nt(left, right):
    return lax.dot_general(left, right, (((1,), (1,)), ((), ())), preferred_element_type=F32)


def rms_scale(field):
    return lax.rsqrt(jnp.mean(field * field, axis=-1, keepdims=True) + EPSILON)


def shape(dims, dtype):
    return jax.ShapeDtypeStruct(dims, dtype)


def whole(dims):
    return pl.BlockSpec(dims, lambda *_: (0,) * len(dims))


def fixed(dims):
    return pl.BlockSpec(dims, lambda *_: (0,) * len(dims), pipeline_mode=pl.Buffered(1))


class Clock:
    def __init__(self, flags):
        self.flags = flags

    def after(self, *values):
        self.flags = lax.optimization_barrier((self.flags, values))[0]

    def at(self, value):
        return lax.optimization_barrier((value, self.flags))[0]

    def run(self, kernel, outs, args, grid, in_specs, out_specs, scratch=(), flops=0, limit=24, stream=False):
        nbytes = sum(math.prod(a.shape) * a.dtype.itemsize for a in args) + sum(
            math.prod(o.shape) * o.dtype.itemsize for o in outs
        )
        args = [
            pltpu.with_memory_space_constraint(arg, pltpu.HBM)
            if stream and spec.block_shape != arg.shape
            else arg
            for arg, spec in zip(args, in_specs)
        ]
        results = pl.pallas_call(
            kernel,
            out_shape=outs,
            grid_spec=pltpu.PrefetchScalarGridSpec(
                num_scalar_prefetch=1,
                grid=grid,
                in_specs=in_specs,
                out_specs=out_specs,
                scratch_shapes=list(scratch),
            ),
            compiler_params=pltpu.CompilerParams(
                dimension_semantics=("arbitrary",) * len(grid), vmem_limit_bytes=limit * MIB
            ),
            cost_estimate=pl.CostEstimate(
                flops=int(flops), bytes_accessed=int(nbytes), transcendentals=0
            ),
        )(self.flags, *args)
        self.after(results[0])
        return results


START, CORE, CHIP = 0, 1, 2


def front_kernel(flags, tokens, gain, wq, wk, wv, normed, queries, pair):
    @pl.when(pl.program_id(0) == 0)
    def _():
        inputs = tokens[...].astype(F32)
        normed[...] = (inputs * rms_scale(inputs) * gain[...]).astype(BF)

    rows = normed[...]
    queries[...] = product(rows, wq[...]).astype(BF)
    pair[0] = product(rows, wk[...]).astype(BF)
    pair[1] = product(rows, wv[...]).astype(BF)


def front(clock, tokens, gain, wq, wk, wv):
    step = 256
    column = pl.BlockSpec((D, step), lambda j, *_: (0, j))
    return clock.run(
        front_kernel,
        (shape((W, D), BF), shape((W, D), BF), shape((2, W, D), BF)),
        (tokens, gain, wq, wk, wv),
        (D // step,),
        [whole((W, D)), whole((1, D)), column, column, column],
        (
            whole((W, D)),
            pl.BlockSpec((W, step), lambda j, *_: (0, j)),
            pl.BlockSpec((2, W, step), lambda j, *_: (0, 0, j)),
        ),
        flops=6 * W * D * D,
        stream=True,
    )


def left_kernel(flags, tokens, gain, wk, wv, pair, normed):
    @pl.when(pl.program_id(0) == 0)
    def _():
        inputs = tokens[...].astype(F32)
        normed[...] = (inputs * rms_scale(inputs) * gain[...]).astype(BF)

    rows = normed[...]
    pair[0] = product(rows, wk[...]).astype(BF)
    pair[1] = product(rows, wv[...]).astype(BF)


def left_pair(clock, tokens, gain, wk, wv):
    step = 256
    column = pl.BlockSpec((D, step), lambda j, *_: (0, j))
    return clock.run(
        left_kernel,
        (shape((2, W, D), BF),),
        (tokens, gain, wk, wv),
        (D // step,),
        [whole((W, D)), whole((1, D)), column, column],
        (pl.BlockSpec((2, W, step), lambda j, *_: (0, 0, j)),),
        [pltpu.VMEM((W, D), BF)],
        flops=LONG,
    )[0]


def summary_probs_of(keys, asks):
    raw = product_nt(keys, asks) * SCALE_LOG2
    expos = jnp.exp2(raw - jnp.max(raw, axis=0, keepdims=True))
    return expos, jnp.sum(expos, axis=0, keepdims=True)


def gates_kernel(
    flags, asks, pair, wu, wg, bias, initial, summary, forget, update, give, own, work
):
    step = pl.program_id(0)

    @pl.when(step < 4)
    def _():
        for head in range(2):
            at = slice(head * HEAD_DIM, (head + 1) * HEAD_DIM)
            expos, total = summary_probs_of(pair[0, :, at], asks[:, at])
            held = product_tn(pair[1, :, at], expos.astype(BF)) / total
            place = pl.multiple_of(step * 256 + head * HEAD_DIM, HEAD_DIM)
            summary[:, pl.ds(place, HEAD_DIM)] = held.T.astype(BF)

    @pl.when(step >= 4)
    def _():
        start = flags[START].astype(F32)
        rows = summary[...]
        fresh = product(rows, wu[...])
        gate = jax.nn.sigmoid(product(rows, wg[...]) + bias[...])
        update[...] = fresh
        forget[...] = gate
        work[0] = (1.0 - start) * gate
        work[1] = start * gate * initial[...] + (1.0 - gate) * fresh
        mine = pl.multiple_of(flags[CORE] * HALF, HALF)
        others = pl.multiple_of((1 - flags[CORE]) * HALF, HALF)
        for part in range(2):
            own[part] = work[part, pl.ds(mine, HALF)].astype(BF)
            give[part] = work[part, pl.ds(others, HALF)].astype(BF)


def gates(clock, asks, pair, state_weight, bias, initial):
    step = 256
    early = lambda i, *_: (0, jnp.minimum(i, 3))
    late = lambda i, *_: (0, jnp.maximum(i - 4, 0))
    late3 = lambda i, *_: (0, 0, jnp.maximum(i - 4, 0))
    return clock.run(
        gates_kernel,
        (
            shape((NS, D), BF),
            shape((NS, D), F32),
            shape((NS, D), F32),
            shape((2, HALF, D), BF),
            shape((2, HALF, D), BF),
        ),
        (asks, pair, state_weight, state_weight, bias, initial),
        (8,),
        [
            pl.BlockSpec((NS, step), early),
            pl.BlockSpec((2, W, step), lambda i, *_: (0, 0, jnp.minimum(i, 3))),
            pl.BlockSpec((D, step), late),
            pl.BlockSpec((D, step), lambda i, *_: (0, jnp.maximum(i - 4, 0) + D // step)),
            pl.BlockSpec((1, step), late),
            pl.BlockSpec((NS, step), late),
        ],
        (
            whole((NS, D)),
            pl.BlockSpec((NS, step), late),
            pl.BlockSpec((NS, step), late),
            pl.BlockSpec((2, HALF, step), late3),
            pl.BlockSpec((2, HALF, step), late3),
        ),
        [pltpu.VMEM((2, NS, step), F32)],
        flops=4 * NS * W * D + 4 * NS * D * D,
    )


def rows_of(chip):
    return pl.ds(pl.multiple_of(chip * QUARTER, QUARTER), QUARTER)


def compose_kernel(flags, own, recv, keep, to1, to2, to3, work):
    odd_core = flags[CORE] == 1
    pick2 = lambda part: (own[part].astype(F32), recv[part].astype(F32))
    (own_scale, recv_scale), (own_base, recv_base) = pick2(0), pick2(1)
    later_scale = jnp.where(odd_core, own_scale, recv_scale)
    earlier_base = jnp.where(odd_core, recv_base, own_base)
    later_base = jnp.where(odd_core, own_base, recv_base)
    work[0] = own_scale * recv_scale
    work[1] = later_scale * earlier_base + later_base
    for far, out in enumerate((keep, to1, to2, to3)):
        out[...] = work[:, rows_of(flags[CHIP] ^ far)].astype(BF)


def prefix_kernel(flags, keep, from1, from2, from3, mine, to1, to2, to3, got, enter):
    for far, came in enumerate((keep, from1, from2, from3)):
        got[flags[CHIP] ^ far] = came[...].astype(F32)
    state = got[0, 1]
    enter[0] = jnp.zeros_like(state)
    enter[1] = state
    for chip in (1, 2):
        state = got[chip, 0] * state + got[chip, 1]
        enter[chip + 1] = state
    for far, out in enumerate((mine, to1, to2, to3)):
        out[...] = enter[flags[CHIP] ^ far].astype(BF)


def previous_kernel(flags, mine, from1, from2, from3, own, recv, keep, give, before):
    for far, came in enumerate((mine, from1, from2, from3)):
        before[rows_of(flags[CHIP] ^ far)] = came[...].astype(F32)
    odd_core = flags[CORE] == 1
    scale = jnp.where(odd_core, recv[0].astype(F32), own[0].astype(F32))
    base = jnp.where(odd_core, recv[1].astype(F32), own[1].astype(F32))
    entry = before[...]
    between = scale * entry + base
    keep[...] = jnp.where(odd_core, between, entry).astype(BF)
    give[...] = jnp.where(odd_core, entry, between).astype(BF)


def compose_back_kernel(flags, own, recv, own_pair, recv_pair, keep, to1, to2, to3, work):
    odd_core = flags[CORE] == 1
    scale = jnp.where(odd_core, recv_pair[0].astype(F32), own_pair[0].astype(F32))
    mine, other = own[...].astype(F32), recv[...].astype(F32)
    work[...] = scale * jnp.where(odd_core, mine, other) + jnp.where(odd_core, other, mine)
    for far, out in enumerate((keep, to1, to2, to3)):
        out[...] = work[rows_of(flags[CHIP] ^ far)].astype(BF)


def suffix_kernel(
    flags, keep, from1, from2, from3, kept0, kept1, kept2, kept3, mine, to1, to2, to3, got, enter
):
    pairs = ((keep, kept0), (from1, kept1), (from2, kept2), (from3, kept3))
    for far, (came, kept) in enumerate(pairs):
        got[flags[CHIP] ^ far, 0] = kept[0].astype(F32)
        got[flags[CHIP] ^ far, 1] = came[...].astype(F32)
    state = got[3, 1]
    enter[3] = jnp.zeros_like(state)
    enter[2] = state
    for chip in (2, 1):
        state = got[chip, 0] * state + got[chip, 1]
        enter[chip - 1] = state
    for far, out in enumerate((mine, to1, to2, to3)):
        out[...] = enter[flags[CHIP] ^ far].astype(BF)


def following_kernel(
    flags, mine, from1, from2, from3, own, recv, own_pair, recv_pair, keep, give, after
):
    for far, came in enumerate((mine, from1, from2, from3)):
        after[rows_of(flags[CHIP] ^ far)] = came[...].astype(F32)
    odd_core = flags[CORE] == 1
    scale = jnp.where(odd_core, own_pair[0].astype(F32), recv_pair[0].astype(F32))
    base = jnp.where(odd_core, own[...].astype(F32), recv[...].astype(F32))
    entry = after[...]
    between = scale * entry + base
    keep[...] = jnp.where(odd_core, entry, between).astype(BF)
    give[...] = jnp.where(odd_core, between, entry).astype(BF)


def small(clock, kernel, outs, args, scratch):
    return clock.run(
        kernel,
        tuple(shape(dims, BF) for dims in outs),
        args,
        (1,),
        [whole(a.shape) for a in args],
        tuple(whole(dims) for dims in outs),
        [pltpu.VMEM(dims, F32) for dims in scratch],
        limit=10,
    )


def to_chips(values):
    return (values[0],) + tuple(
        swapped(value, "seq", 2 * far) for far, value in zip((1, 2, 3), values[1:])
    )


PAIR_WORK = [(4, 2, QUARTER, D), (4, QUARTER, D)]


def compose(clock, own, recv):
    return to_chips(small(clock, compose_kernel, [(2, QUARTER, D)] * 4, (own, recv), [(2, HALF, D)]))


def prefix(clock, got):
    return to_chips(small(clock, prefix_kernel, [(QUARTER, D)] * 4, got, PAIR_WORK))


def previous(clock, back, own, recv):
    mine, other = small(
        clock, previous_kernel, [(HALF, D)] * 2, back + (own, recv), [(HALF, D)]
    )
    return mine, swapped(other, "seq", 1)


def compose_back(clock, *args):
    return to_chips(small(clock, compose_back_kernel, [(QUARTER, D)] * 4, args, [(HALF, D)]))


def suffix(clock, got, kept):
    return to_chips(small(clock, suffix_kernel, [(QUARTER, D)] * 4, got + kept, PAIR_WORK))


def following(clock, back, *args):
    mine, other = small(clock, following_kernel, [(HALF, D)] * 2, back + args, [(HALF, D)])
    return mine, swapped(other, "seq", 1)


def state_kernel(
    flags, mine, other, initial, forget, update, wk, wv, state_in, state_low, state_out, pair
):
    @pl.when(pl.program_id(0) == 0)
    def _():
        start = flags[START].astype(F32)
        for core, came in ((flags[CORE], mine), (1 - flags[CORE], other)):
            rows = pl.ds(pl.multiple_of(core * HALF, HALF), HALF)
            entry = (1.0 - start) * came[...].astype(F32) + start * initial[rows, :]
            gate = forget[rows, :]
            state_in[rows, :] = entry
            state_low[rows, :] = entry.astype(BF)
            state_out[rows, :] = gate * entry + (1.0 - gate) * update[rows, :]

    rows = state_low[...]
    pair[0] = product(rows, wk[...]).astype(BF)
    pair[1] = product(rows, wv[...]).astype(BF)


def state_pair(clock, mine, other, initial, forget, update, wk, wv):
    step = 256
    column = pl.BlockSpec((D, step), lambda j, *_: (0, j))
    return clock.run(
        state_kernel,
        (shape((NS, D), F32), shape((NS, D), BF), shape((NS, D), F32), shape((2, NS, D), BF)),
        (mine, other, initial, forget, update, wk, wv),
        (D // step,),
        [whole((HALF, D))] * 2 + [whole((NS, D))] * 3 + [column, column],
        (
            whole((NS, D)),
            whole((NS, D)),
            whole((NS, D)),
            pl.BlockSpec((2, NS, step), lambda j, *_: (0, 0, j)),
        ),
        flops=4 * NS * D * D,
    )


def masked_scores(flags, queries, left, own, state):
    seen = []
    left_bias = jnp.where(flags[START] == 0, 0.0, NEGATIVE).astype(F32)
    seen.append(product_nt(left[0], queries) * SCALE_LOG2 + left_bias)
    rows = lax.broadcasted_iota(jnp.int32, (W, W), 0)
    cols = lax.broadcasted_iota(jnp.int32, (W, W), 1)
    seen.append(jnp.where(rows <= cols, product_nt(own[0], queries) * SCALE_LOG2, NEGATIVE))
    seen.append(product_nt(state[0], queries) * SCALE_LOG2)
    return seen


def attend_kernel(flags, queries, left, own, state, attended, lse):
    seen = masked_scores(flags, queries[...], left, own, state)
    peak = functools.reduce(
        jnp.maximum, [jnp.max(part, axis=0, keepdims=True) for part in seen]
    )
    held = 0.0
    total = 0.0
    for part, pair in zip(seen, (left, own, state)):
        expos = jnp.exp2(part - peak)
        total = total + jnp.sum(expos, axis=0, keepdims=True)
        held = held + product_tn(pair[1], expos.astype(BF))
    attended[...] = (held / total).T.astype(BF)
    lse[0] = peak + jnp.log2(total)


def attend(clock, queries, left, own, state):
    head = pl.BlockSpec((W, HEAD_DIM), lambda h, *_: (0, h))
    pair = pl.BlockSpec((2, W, HEAD_DIM), lambda h, *_: (0, 0, h))
    return clock.run(
        attend_kernel,
        (shape((W, D), BF), shape((HEADS, 1, W), F32)),
        (queries, left, own, state),
        (HEADS,),
        [head, pair, pair, pair],
        (head, pl.BlockSpec((1, 1, W), lambda h, *_: (h, 0, 0))),
        flops=4 * W * (2 * W + NS) * D,
        stream=True,
    )


def attend_back_kernel(
    flags, queries, left, own, state, grad, lse, queries_grad, left_grad, own_grad, state_grad
):
    asks, out_grad = queries[...], grad[...]
    seen = masked_scores(flags, asks, left, own, state)
    probs = [jnp.exp2(part - lse[0]) for part in seen]
    pairs = (left, own, state)
    prob_grads = [product_nt(pair[1], out_grad) for pair in pairs]
    rowdot = sum(
        jnp.sum(prob * prob_grad, axis=0, keepdims=True)
        for prob, prob_grad in zip(probs, prob_grads)
    )
    total = 0.0
    for prob, prob_grad, pair, out in zip(
        probs, prob_grads, pairs, (left_grad, own_grad, state_grad)
    ):
        score_grad = (prob * (prob_grad - rowdot)).astype(BF)
        out[0] = (product(score_grad, asks) * SCALE).astype(out.dtype)
        out[1] = product(prob.astype(BF), out_grad).astype(out.dtype)
        total = total + product_tn(pair[0], score_grad)
    queries_grad[...] = (total * SCALE).T.astype(BF)


def attend_back(clock, queries, left, own, state, grad, lse):
    head = pl.BlockSpec((W, HEAD_DIM), lambda h, *_: (0, h))
    pair = pl.BlockSpec((2, W, HEAD_DIM), lambda h, *_: (0, 0, h))
    return clock.run(
        attend_back_kernel,
        (shape((W, D), BF), shape((2, W, D), BF), shape((2, W, D), F32), shape((2, NS, D), BF)),
        (queries, left, own, state, grad, lse),
        (HEADS,),
        [head, pair, pair, pair, head, pl.BlockSpec((1, 1, W), lambda h, *_: (h, 0, 0))],
        (head, pair, pair, pair),
        flops=10 * W * (2 * W + NS) * D,
        stream=True,
    )


def gelu_parts(upper):
    square = upper * upper
    inner = GELU_SCALE * (upper + GELU_CUBIC * square * upper)
    bent = jnp.tanh(inner)
    value = 0.5 * upper * (1.0 + bent)
    slope = 0.5 * (1.0 + bent) + 0.5 * upper * (1.0 - bent * bent) * GELU_SCALE * (
        1.0 + 3.0 * GELU_CUBIC * square
    )
    return value, slope


def mlp_step(normed_mlp, cotangent, up1, up2, down, up, activated, upper_grad, total, grad):
    half = up1.shape[1]
    up[:, :half] = up1[...]
    up[:, half:] = up2[...]
    rows = down[...].reshape(2 * half, D)
    value, slope = gelu_parts(product(normed_mlp[...], up[...]))
    value = value.astype(BF)
    activated[...] = value
    total[...] += product(value, rows)
    back = product_nt(cotangent[...], rows).astype(BF).astype(F32)
    back = (back * slope).astype(BF)
    upper_grad[...] = back
    grad[...] += product_nt(back, up[...])


def mlp_first_kernel(
    flags,
    attended,
    tokens,
    out_weight,
    gain,
    cotangent,
    up1,
    up2,
    down,
    activated,
    upper_grad,
    normed_mlp,
    hidden,
    total,
    grad,
    up,
):
    @pl.when(pl.program_id(0) == 0)
    def _():
        field = tokens[...].astype(F32) + product(attended[...], out_weight[...])
        hidden[...] = field
        normed_mlp[...] = (field * rms_scale(field) * gain[...]).astype(BF)
        total[...] = field
        grad[...] = jnp.zeros_like(field)

    mlp_step(normed_mlp, cotangent, up1, up2, down, up, activated, upper_grad, total, grad)


def mlp_second_kernel(
    flags,
    normed_mlp,
    hidden,
    total_in,
    grad_in,
    out_weight,
    gain,
    cotangent,
    up1,
    up2,
    down,
    activated,
    upper_grad,
    mixed,
    hidden_grad,
    attended_grad,
    heads_grad,
    gain_grad,
    total,
    grad,
    up,
):
    step = pl.program_id(0)

    @pl.when(step == 0)
    def _():
        total[...] = total_in[...]
        grad[...] = grad_in[...]

    mlp_step(normed_mlp, cotangent, up1, up2, down, up, activated, upper_grad, total, grad)

    @pl.when(step == pl.num_programs(0) - 1)
    def _():
        mixed[...] = total[...].astype(BF)
        field = hidden[...]
        scaled = rms_scale(field)
        gain_grad[...] = jnp.sum(grad[...] * field * scaled, axis=0, keepdims=True)
        weighted = grad[...] * gain[...]
        field_grad = (
            cotangent[...].astype(F32)
            + scaled * weighted
            - field
            * (scaled * scaled * scaled * jnp.mean(weighted * field, axis=-1, keepdims=True))
        )
        hidden_grad[...] = field_grad
        low = field_grad.astype(BF)
        attended_grad[...] = low
        heads_grad[...] = product_nt(low, out_weight[...]).astype(BF)


PIECE = 256
PAIRS = FF // (4 * PIECE)


def mlp_specs(part):
    return [
        pl.BlockSpec((D, PIECE), lambda j, *_: (0, 4 * j + part)),
        pl.BlockSpec((D, PIECE), lambda j, *_: (0, 4 * j + 2 + part)),
        pl.BlockSpec((2, PIECE, D), lambda j, *_: (j, part, 0)),
    ]


def mlp_halves():
    return pl.BlockSpec((W, 2 * PIECE), lambda j, *_: (0, j))


def mlp_first(clock, attended, tokens, out_weight, gain, cotangent, up, down):
    rows = whole((W, D))
    return clock.run(
        mlp_first_kernel,
        (
            shape((W, FF // 2), BF),
            shape((W, FF // 2), BF),
            shape((W, D), BF),
            shape((W, D), F32),
            shape((W, D), F32),
            shape((W, D), F32),
        ),
        (attended, tokens, out_weight, gain, cotangent, up, up, down),
        (PAIRS,),
        [fixed((W, D)), fixed((W, D)), fixed((D, D)), fixed((1, D)), fixed((W, D))] + mlp_specs(0),
        (mlp_halves(), mlp_halves(), rows, rows, rows, rows),
        [pltpu.VMEM((D, 2 * PIECE), BF)],
        flops=4 * W * D * FF + 2 * W * D * D,
        limit=36,
    )


def mlp_second(clock, normed_mlp, hidden, total, grad, out_weight, gain, cotangent, up, down):
    rows = whole((W, D))
    return clock.run(
        mlp_second_kernel,
        (
            shape((W, FF // 2), BF),
            shape((W, FF // 2), BF),
            shape((W, D), BF),
            shape((W, D), F32),
            shape((W, D), BF),
            shape((W, D), BF),
            shape((1, D), F32),
        ),
        (normed_mlp, hidden, total, grad, out_weight, gain, cotangent, up, up, down),
        (PAIRS,),
        [fixed((W, D))] * 4
        + [fixed((D, D)), fixed((1, D)), fixed((W, D))]
        + mlp_specs(1),
        (mlp_halves(), mlp_halves(), rows, rows, rows, rows, whole((1, D))),
        [pltpu.VMEM((W, D), F32), pltpu.VMEM((W, D), F32), pltpu.VMEM((D, 2 * PIECE), BF)],
        flops=4 * W * D * FF + 2 * W * D * D,
        limit=36,
    )


def direct_kernel(flags, state_grad, wk, wv, forget, cotangent, direct, own, give, work):
    grad = product_nt(state_grad[0], wk[...]) + product_nt(state_grad[1], wv[...])
    direct[...] = grad
    keep = 1.0 - flags[START].astype(F32)
    work[...] = keep * (forget[...] * cotangent[...] + grad)
    own[...] = work[pl.ds(pl.multiple_of(flags[CORE] * HALF, HALF), HALF)].astype(BF)
    give[...] = work[pl.ds(pl.multiple_of((1 - flags[CORE]) * HALF, HALF), HALF)].astype(BF)


def direct_grad(clock, state_grad, wk, wv, forget, cotangent):
    step = 256
    row = pl.BlockSpec((step, D), lambda j, *_: (j, 0))
    column = pl.BlockSpec((NS, step), lambda j, *_: (0, j))
    half = pl.BlockSpec((HALF, step), lambda j, *_: (0, j))
    return clock.run(
        direct_kernel,
        (shape((NS, D), F32), shape((HALF, D), BF), shape((HALF, D), BF)),
        (state_grad, wk, wv, forget, cotangent),
        (D // step,),
        [whole((2, NS, D)), row, row, column, column],
        (column, half, half),
        [pltpu.VMEM((NS, step), F32)],
        flops=4 * NS * D * D,
    )


def state_back_kernel(
    flags,
    mine,
    other,
    cotangent,
    forget,
    update,
    state_in,
    direct,
    wu,
    wg,
    initial_grad,
    projected_grad,
    bias_grad,
    summary_grad,
    work,
    total,
):
    step = pl.program_id(0)
    for core, came in ((flags[CORE], mine), (1 - flags[CORE], other)):
        work[pl.ds(pl.multiple_of(core * HALF, HALF), HALF)] = came[...].astype(F32)
    out_grad = cotangent[...] + work[...]
    gate = forget[...]
    start = flags[START].astype(F32)
    initial_grad[...] = (start * (gate * out_grad + direct[...])).astype(BF)
    rest = 1.0 - gate
    gate_grad = out_grad * (state_in[...] - update[...]) * gate * rest
    bias_grad[...] = jnp.sum(gate_grad, axis=0, keepdims=True)
    fresh_grad = (out_grad * rest).astype(BF)
    gate_low = gate_grad.astype(BF)
    projected_grad[0] = fresh_grad
    projected_grad[1] = gate_low
    part = product_nt(fresh_grad, wu[...]) + product_nt(gate_low, wg[...])

    @pl.when(step == 0)
    def _():
        total[...] = part

    @pl.when(step > 0)
    def _():
        total[...] += part

    @pl.when(step == pl.num_programs(0) - 1)
    def _():
        summary_grad[...] = total[...].astype(BF)


def state_back(clock, mine, other, cotangent, forget, update, state_in, direct, state_weight):
    step = 256
    column = pl.BlockSpec((NS, step), lambda j, *_: (0, j))
    half = pl.BlockSpec((HALF, step), lambda j, *_: (0, j))
    return clock.run(
        state_back_kernel,
        (
            shape((NS, D), BF),
            shape((2, NS, D), BF),
            shape((1, D), F32),
            shape((NS, D), BF),
        ),
        (mine, other, cotangent, forget, update, state_in, direct, state_weight, state_weight),
        (D // step,),
        [half, half, column, column, column, column, column]
        + [
            pl.BlockSpec((D, step), lambda j, *_: (0, j)),
            pl.BlockSpec((D, step), lambda j, *_: (0, j + D // step)),
        ],
        (
            column,
            pl.BlockSpec((2, NS, step), lambda j, *_: (0, 0, j)),
            pl.BlockSpec((1, step), lambda j, *_: (0, j)),
            whole((NS, D)),
        ),
        [pltpu.VMEM((NS, step), F32), pltpu.VMEM((NS, D), F32)],
        flops=4 * NS * D * D,
    )


def summary_back_kernel(flags, asks, pair, grad, own_grad, asks_grad, pair_total):
    queries, out_grad = asks[...], grad[...]
    expos, total = summary_probs_of(pair[0], queries)
    probs = expos * (1.0 / total)
    prob_grad = product_nt(pair[1], out_grad)
    rowdot = jnp.sum(probs * prob_grad, axis=0, keepdims=True)
    score_grad = (probs * (prob_grad - rowdot)).astype(BF)
    asks_grad[...] = (product_tn(pair[0], score_grad) * SCALE).T.astype(BF)
    pair_total[0] = (own_grad[0] + product(score_grad, queries) * SCALE).astype(BF)
    pair_total[1] = (own_grad[1] + product(probs.astype(BF), out_grad)).astype(BF)


def summary_back(clock, asks, pair, grad, own_grad):
    head = pl.BlockSpec((W, HEAD_DIM), lambda h, *_: (0, h))
    both = pl.BlockSpec((2, W, HEAD_DIM), lambda h, *_: (0, 0, h))
    return clock.run(
        summary_back_kernel,
        (shape((NS, D), BF), shape((2, W, D), BF)),
        (asks, pair, grad, own_grad),
        (HEADS,),
        [head, both, head, both],
        (head, both),
        flops=10 * NS * W * D,
        stream=True,
    )


def tokens_back_kernel(
    flags,
    queries_grad,
    pair_total,
    returned,
    wq,
    wk,
    wv,
    tokens,
    gain,
    hidden_grad,
    tokens_grad,
    gain_grad,
    total,
):
    step = pl.program_id(0)

    @pl.when(step < 2)
    def _():
        part = product_nt(queries_grad[...], wq[...])
        total[...] = jnp.where(step == 0, part, total[...] + part)

    @pl.when((step >= 2) & (step < 4))
    def _():
        total[...] += product_nt(add_low(pair_total[0], returned[0]), wk[...])

    @pl.when(step >= 4)
    def _():
        total[...] += product_nt(add_low(pair_total[0], returned[0]), wv[...])

    @pl.when(step == 5)
    def _():
        inputs = tokens[...].astype(F32)
        scaled = rms_scale(inputs)
        grad = total[...]
        gain_grad[...] = jnp.sum(grad * inputs * scaled, axis=0, keepdims=True)
        weighted = grad * gain[...]
        tokens_grad[...] = (
            hidden_grad[...]
            + scaled * weighted
            - inputs
            * (scaled * scaled * scaled * jnp.mean(weighted * inputs, axis=-1, keepdims=True))
        )


def tokens_back(clock, queries_grad, pair_total, returned, wq, wk, wv, tokens, gain, hidden_grad):
    step = D // 2
    clamp = lambda i, low: jnp.clip(i - low, 0, 1)
    weight = lambda low: pl.BlockSpec((D, step), lambda i, *_: (0, clamp(i, low)))
    later = lambda i: jnp.maximum(i - 2, 0)
    pair = pl.BlockSpec((1, W, step), lambda i, *_: (later(i) // 2, 0, later(i) % 2))
    return clock.run(
        tokens_back_kernel,
        (shape((W, D), F32), shape((1, D), F32)),
        (queries_grad, pair_total, returned, wq, wk, wv, tokens, gain, hidden_grad),
        (6,),
        [
            pl.BlockSpec((W, step), lambda i, *_: (0, clamp(i, 0))),
            pair,
            pair,
            weight(0),
            weight(2),
            weight(4),
            fixed((W, D)),
            fixed((1, D)),
            fixed((W, D)),
        ],
        (whole((W, D)), whole((1, D))),
        [pltpu.VMEM((W, D), F32)],
        flops=6 * W * D * D,
    )


def chunk_natural(flags, place):
    return place


def chunk_along_x(flags, place):
    x = flags[CHIP] & 1
    return 2 * (place % 2) + (1 - x if place < 2 else x)


def chunk_along_y(flags, place):
    y = flags[CHIP] >> 1
    return 2 * (1 - y if place < 2 else y) + place % 2


def column_blocks(terms):
    return terms[0][1][0][0].shape[2] // D


def weight_kernel(plan, merge, flags, *refs):
    refs = list(refs)
    lefts = [refs.pop(0) for _ in range(plan["lefts"])]
    rights = [[refs.pop(0) for _ in adds] for adds in plan["rights"]]
    recv = refs.pop(0) if merge else None
    work = refs.pop()
    step, base, start = pl.program_id(0), 0, 0
    for rows, blocks, terms, along in plan["grads"]:
        chunk_of = (chunk_along_x, chunk_along_y)[along] if merge else chunk_natural

        @pl.when(step == base)
        def _():
            for term, (left, _) in enumerate(terms):
                for place in range(4):
                    chunk = 2 * chunk_of(flags, place) + (
                        flags[CORE] if merge else 1 - flags[CORE]
                    )
                    block = lefts[left][:, pl.ds(pl.multiple_of(chunk * rows, rows), rows)]
                    work[term, place * rows : (place + 1) * rows] = block.T

        for block in range(blocks):

            @pl.when(step == base + block)
            def _():
                total = 0.0
                for term, (_, right) in enumerate(terms):
                    parts = [part[0] for part in rights[right]]
                    value = parts[0] if len(parts) == 1 else add_low(*parts)
                    total = total + product(work[term, : 4 * rows], value)
                at = start + block * rows
                for place in range(4):
                    part = total[place * rows : (place + 1) * rows]
                    if merge:
                        part = part + recv[chunk_of(flags, place), at : at + rows].astype(F32)
                        refs[2 * along + place // 2][place % 2] = part.astype(BF)
                    else:
                        refs[0][place, at : at + rows] = part.astype(BF)

        base += blocks
        start += blocks * rows


def weight_pair(clock, grads, recv):
    lefts, left_ids, rights, args, specs, plans = [], {}, [], [], [], []
    base, start, tokens = 0, 0, grads[0][0][0][0].shape[0]
    sizes = []
    for along, group in enumerate(grads):
        first, total = base, 0
        for terms in group:
            rows, blocks = terms[0][0].shape[1] // 8, column_blocks(terms)
            plan = []
            for left, adds in terms:
                if id(left) not in left_ids:
                    left_ids[id(left)] = len(lefts)
                    lefts.append(left)
                plan.append((left_ids[id(left)], len(rights)))
                rights.append(tuple(index for _, index in adds))
                for right, index in adds:
                    args.append(right)
                    specs.append(
                        pl.BlockSpec(
                            (1, tokens, D),
                            lambda j, *_, index=index, base=base, blocks=blocks: (
                                index,
                                0,
                                jnp.clip(j - base, 0, blocks - 1),
                            ),
                        )
                    )
            plans.append((rows, blocks, plan, along))
            base += blocks
            total += blocks
            start += blocks * rows
        sizes.append((rows, total, first))
    args = lefts + args
    specs = [fixed(left.shape) for left in lefts] + specs
    merge = recv is not None
    if merge:
        args.append(recv)
        specs.append(fixed(recv.shape))
        outs, out_specs = [], []
        for rows, blocks, first in sizes:
            outs += [shape((2, rows * blocks, D), BF)] * 2
            out_specs += [
                pl.BlockSpec(
                    (2, rows, D),
                    lambda j, *_, first=first, blocks=blocks: (
                        0,
                        jnp.clip(j - first, 0, blocks - 1),
                        0,
                    ),
                )
            ] * 2
    else:
        outs = [shape((4, start, D), BF)]
        out_specs = [whole((4, start, D))]
    most = max(rows for rows, _, _ in sizes)
    return clock.run(
        functools.partial(
            weight_kernel, {"lefts": len(lefts), "rights": rights, "grads": plans}, merge
        ),
        tuple(outs),
        tuple(args),
        (base,),
        specs,
        tuple(out_specs),
        [pltpu.VMEM((len(grads[0][0]), 4 * most, tokens), BF)],
        flops=2 * tokens * 4 * start * D * len(grads[0][0]),
        limit=30,
    )


def scatter_bits(value, bits, names):
    place = lax.axis_index("seq")
    names = list(names)
    for bit in bits:
        at = names.index(bit)
        mine = (place >> bit) & 1
        recv = swapped(pick(value, 1 - mine, at), "seq", 1 << bit)
        value = add_low(pick(value, mine, at), recv)
        names.pop(at)
    return value


def whole_scatter(value, along_x):
    count = lax.axis_size("seq")
    levels = count.bit_length() - 1
    names = list(range(levels - 1, -1, -1))
    value = value.reshape((2,) * levels + (value.shape[0] // count,) + value.shape[1:])
    bits = [0] + (names[-2::-1] if along_x else names[:-1])
    return scatter_bits(value, bits, names)


def in_rows(value):
    return jnp.concatenate([value[:, at : at + D] for at in range(0, value.shape[1], D)], axis=0)


def turn_kernel(flags, kept1, recv1, kept2, recv2, send1, send2):
    send1[...] = add_low(kept1[0], recv1[0])
    send2[...] = add_low(kept2[0], recv2[0])


def pack_kernel(flags, *refs):
    out, start = refs[-1], 0
    for at in range(0, len(refs) - 1, 3):
        kept, recv, last = refs[at : at + 3]
        rows = last.shape[0]
        out[start : start + rows] = add_low(kept[0], recv[0], last[...])
        start += rows


class Scatter:
    def __init__(self, clock, firsts, seconds):
        self.grads, self.plain = (firsts, seconds), None
        if lax.axis_size("seq") != 8:
            sums = []
            for number, group in enumerate(self.grads):
                for terms in group:
                    total = 0.0
                    for left, adds in terms:
                        parts = [right[index] for right, index in adds]
                        right = add_low(*parts) if len(parts) > 1 else parts[0]
                        total = total + product_tn(left, right)
                    sums.append(in_rows(whole_scatter(total.astype(BF), number == 0)))
            self.plain = jnp.concatenate(sums, axis=0)
            return
        (self.give,) = weight_pair(clock, self.grads, None)

    def core(self, clock):
        if self.plain is None:
            self.recv = swapped(clock.at(self.give), "seq", 1)

    def keep(self, clock):
        if self.plain is None:
            send1, kept1, send2, kept2 = weight_pair(clock, self.grads, self.recv)
            self.kept, self.send = (kept1, kept2), (send1, send2)

    def near(self, clock):
        if self.plain is None:
            self.recv = tuple(
                swapped(clock.at(send), "seq", far) for send, far in zip(self.send, (2, 4))
            )

    def held(self, other):
        args, specs = [], []
        for number, (kept, recv) in enumerate(zip(self.kept, self.recv)):
            bit = 1 - number
            mine = lambda i, flags, bit=bit: (((flags[CHIP] >> bit) & 1) ^ other, 0, 0)
            args.append([kept, recv])
            specs.append([pl.BlockSpec((1,) + kept.shape[1:], mine)] * 2)
        return args, specs

    def turn(self, clock, flops=0):
        if self.plain is None:
            args, specs = self.held(1)
            dims = [kept.shape[1:] for kept in self.kept]
            self.send = clock.run(
                turn_kernel,
                tuple(shape(d, BF) for d in dims),
                tuple(args[0] + args[1]),
                (1,),
                specs[0] + specs[1],
                tuple(whole(d) for d in dims),
                flops=flops,
                limit=10,
            )

    def far(self, clock):
        if self.plain is None:
            self.last = tuple(
                swapped(clock.at(send), "seq", far) for send, far in zip(self.send, (4, 2))
            )

    def parts(self):
        args, specs = self.held(0)
        for number, last in enumerate(self.last):
            args[number].append(last)
            specs[number].append(whole(last.shape))
        return args[0] + args[1], specs[0] + specs[1]


def pack(clock, *scatters):
    if scatters[0].plain is not None:
        return jnp.concatenate([scatter.plain for scatter in scatters], axis=0)
    args, specs = [], []
    for scatter in scatters:
        more = scatter.parts()
        args += more[0]
        specs += more[1]
    total = sum(arg.shape[0] for arg in args[2::3])
    return clock.run(
        pack_kernel,
        (shape((total, D), BF),),
        tuple(args),
        (1,),
        specs,
        (whole((total, D)),),
        limit=16,
    )[0]


class Line:
    def __init__(self, clock, value):
        count = lax.axis_size("dp")
        half = count // 2
        self.value = value
        self.rounds = (
            [([(s, s + 1), (count - 1 - s, count - 2 - s)], None) for s in range(half - 1)]
            + [([(half - 1, half), (half, half - 1)], None)]
            + [
                ([(s + 1, s), (count - 2 - s, count - 1 - s)], (s, count - 1 - s))
                for s in range(half - 2, -1, -1)
            ]
        )
        self.send(clock)

    def send(self, clock):
        self.recv = lax.ppermute(clock.at(self.value), "dp", self.rounds[0][0])

    def step(self, clock):
        place = lax.axis_index("dp")
        takers = self.rounds.pop(0)[1]
        value = clock.at(self.value)
        if takers is None:
            self.value = add_low(value, self.recv)
        else:
            outer = (place == takers[0]) | (place == takers[1])
            self.value = jnp.where(outer, self.recv, value)
        if self.rounds:
            clock.after(self.value)
            self.send(clock)

    def finish(self, clock):
        while self.rounds:
            self.step(clock)
        return self.value.astype(F32)


def interleaved(first, second):
    blocks = []
    for at in range(0, first.shape[1], PIECE):
        blocks += [first[:, at : at + PIECE], second[:, at : at + PIECE]]
    return jnp.concatenate(blocks, axis=1)


def body(
    tokens,
    item_starts,
    attn_gain,
    query_weight,
    key_weight,
    value_weight,
    output_weight,
    state_queries,
    state_weight,
    gate_bias,
    initial_state,
    mlp_gain,
    up_weight,
    down_weight,
    out_cotangent,
    state_cotangent,
):
    count = lax.axis_size("seq")
    place = lax.axis_index("seq")
    clock = Clock(
        jnp.stack([item_starts[0, 0], place & 1, (place >> 1) & 3]).astype(jnp.int32)
    )
    tokens, cotangent, state_cot = tokens[0], out_cotangent[0], state_cotangent[0, 0]
    attn_gain, gate_bias, mlp_gain = attn_gain[None], gate_bias[None], mlp_gain[None]
    down_weight = down_weight.reshape(FF // (2 * PIECE), 2 * PIECE, D)

    tokens_left = shifted(tokens, "seq", 1)
    normed, queries, own = front(clock, tokens, attn_gain, query_weight, key_weight, value_weight)
    summary, forget, update, give_pair, own_pair = gates(
        clock, state_queries, own, state_weight, gate_bias, initial_state
    )
    recv_pair = swapped(give_pair, "seq", 1)
    left = left_pair(clock, tokens_left, attn_gain, key_weight, value_weight)
    kept_chips = compose(clock, own_pair, recv_pair)
    back = prefix(clock, kept_chips)
    mine, other = previous(clock, back, own_pair, recv_pair)
    state_in, state_low, state_out, state = state_pair(
        clock, mine, other, initial_state, forget, update, key_weight, value_weight
    )
    attended, lse = attend(clock, queries, left, own, state)
    split = count == 8
    activated1, upper_grad1, normed_mlp, hidden, total, grad = mlp_first(
        clock, attended, tokens, output_weight, mlp_gain, cotangent, up_weight, down_weight
    )
    out_grads = (cotangent[None], 0)
    if split:
        feed1 = Scatter(
            clock,
            [[(activated1, [out_grads])]],
            [[(normed_mlp, [(upper_grad1[None], 0)])]],
        )
        feed1.core(clock)
        feed1.keep(clock)
        feed1.near(clock)
    activated2, upper_grad2, mixed, hidden_grad, attended_grad, heads_grad, mlp_gain_grad = (
        mlp_second(
            clock,
            normed_mlp,
            hidden,
            total,
            grad,
            output_weight,
            mlp_gain,
            cotangent,
            up_weight,
            down_weight,
        )
    )
    if split:
        feed2 = Scatter(
            clock,
            [[(activated2, [out_grads])]],
            [[(normed_mlp, [(upper_grad2[None], 0)])]],
        )
        feed2.core(clock)
        feed1.turn(clock, LONG)
        feed1.far(clock)
        feed2.keep(clock)
        feed2.near(clock)
    else:
        feed1 = Scatter(
            clock,
            [[(interleaved(activated1, activated2), [out_grads])]],
            [[(normed_mlp, [(interleaved(upper_grad1, upper_grad2)[None], 0)])]],
        )
    queries_grad, left_grad, own_grad, state_grad = attend_back(
        clock, queries, left, own, state, heads_grad, lse
    )
    if split:
        feed2.turn(clock)
        feed2.far(clock)
    direct, own_base, give_base = direct_grad(
        clock, state_grad, key_weight, value_weight, forget, state_cot
    )
    recv_base = swapped(give_base, "seq", 1)
    packed1 = pack(clock, feed1)
    got = compose_back(clock, own_base, recv_base, own_pair, recv_pair)
    packed2 = pack(clock, feed2) if split else None
    line1 = Line(clock, packed1)
    line2 = Line(clock, packed2) if split else None
    back = suffix(clock, got, kept_chips)
    mine, other = following(clock, back, own_base, recv_base, own_pair, recv_pair)
    returned = shifted(clock.at(left_grad), "seq", -1)
    initial_grad, projected_grad, gate_bias_grad, summary_grad = state_back(
        clock, mine, other, state_cot, forget, update, state_in, direct, state_weight
    )
    line1.step(clock)
    others = Scatter(
        clock,
        [[(attended, [(attended_grad[None], 0)])], [(summary, [(projected_grad, 0)])]],
        [[(normed, [(queries_grad[None], 0)])], [(summary, [(projected_grad, 1)])]],
    )
    others.core(clock)
    state_queries_grad, pair_total = summary_back(
        clock, state_queries, own, summary_grad, own_grad
    )
    if split:
        line2.step(clock)
    others.keep(clock)
    others.near(clock)
    line1.step(clock)
    keys_values = Scatter(
        clock,
        [[(normed, [(pair_total, 0), (returned, 0)]), (state_low, [(state_grad, 0)])]],
        [[(normed, [(pair_total, 1), (returned, 1)]), (state_low, [(state_grad, 1)])]],
    )
    keys_values.core(clock)
    if split:
        line2.step(clock)
    keys_values.keep(clock)
    tokens_grad, attn_gain_grad = tokens_back(
        clock,
        queries_grad,
        pair_total,
        returned,
        query_weight,
        key_weight,
        value_weight,
        tokens,
        attn_gain,
        hidden_grad,
    )
    line1 = line1.finish(clock)
    clock.after(line1)
    others.turn(clock)
    others.far(clock)
    keys_values.near(clock)
    if split:
        line2 = line2.finish(clock)
        clock.after(line2)
    lanes, rows = D // count, NS // count
    vectors = jnp.concatenate([attn_gain_grad, gate_bias_grad, mlp_gain_grad])
    vectors = vectors.reshape(3, count, lanes).transpose(1, 0, 2).reshape(count, 1, 3 * lanes)
    vectors = jnp.pad(vectors, ((0, 0), (0, 7), (0, D - 3 * lanes))).astype(BF)
    rest = jnp.concatenate(
        [
            state_queries_grad.reshape(count, rows, D),
            initial_grad.reshape(count, rows, D),
            vectors,
        ],
        axis=1,
    )
    rest = whole_scatter(rest.reshape(-1, D), True)
    line3 = Line(clock, pack(clock, others))
    keys_values.turn(clock)
    keys_values.far(clock)
    line3.step(clock)
    line4 = Line(clock, jnp.concatenate([pack(clock, keys_values), rest], axis=0))
    line3.step(clock)
    line4.step(clock)
    line4.step(clock)

    def unpack(packed, *dims):
        pieces, start = [], 0
        for high, wide in dims:
            parts = [
                packed[start + high * part : start + high * (part + 1)] for part in range(wide // D)
            ]
            start += high * (wide // D)
            pieces.append(parts[0] if len(parts) == 1 else jnp.concatenate(parts, axis=1))
        return pieces

    high, deep = D // count, FF // count
    if split:
        down1, up1 = unpack(line1, (deep // 2, D), (high, FF // 2))
        down2, up2 = unpack(line2, (deep // 2, D), (high, FF // 2))
        down_grad = jnp.concatenate([down1, down2], axis=0)
        up_grad = interleaved(up1, up2)
    else:
        down_grad, up_grad = unpack(line1, (deep, D), (high, FF))
    output_grad, first_grad, query_grad, second_grad = unpack(
        line3.finish(clock), (high, D), (high, D), (high, D), (high, D)
    )
    state_weight_grad = jnp.concatenate([first_grad, second_grad], axis=1)
    key_grad, value_grad, rest = unpack(
        line4.finish(clock), (high, D), (high, D), (2 * rows + 8, D)
    )
    vectors = rest[2 * rows, : 3 * lanes]
    return (
        mixed[None],
        state_out[None, None],
        tokens_grad[None],
        vectors[:lanes],
        query_grad,
        key_grad,
        value_grad,
        output_grad,
        rest[:rows],
        state_weight_grad,
        vectors[lanes : 2 * lanes],
        rest[rows : 2 * rows],
        vectors[2 * lanes :],
        up_grad,
        down_grad,
    )


def solution(mesh):
    in_specs = (
        P("dp", "seq", None),
        P("dp", "seq"),
        P(),
        P(),
        P(),
        P(),
        P(),
        P(),
        P(),
        P(),
        P(),
        P(),
        P(),
        P(),
        P("dp", "seq", None),
        P("dp", "seq", None, None),
    )
    out_specs = (
        P("dp", "seq", None),
        P("dp", "seq", None, None),
        P("dp", "seq", None),
        P("seq"),
        P("seq", None),
        P("seq", None),
        P("seq", None),
        P("seq", None),
        P("seq", None),
        P("seq", None),
        P("seq"),
        P("seq", None),
        P("seq"),
        P("seq", None),
        P("seq", None),
    )
    return jax.shard_map(body, mesh=mesh, in_specs=in_specs, out_specs=out_specs, check_vma=False)
```

```python
import functools
import math

import jax
import jax.numpy as jnp
from jax import lax
from jax.experimental import pallas as pl
from jax.experimental.pallas import tpu as pltpu
from jax.sharding import PartitionSpec as P

D = 1024
HEADS = 8
HEAD_DIM = 128
FF = 4096
W = 512
NS = 512
HALF = NS // 2
QUARTER = NS // 8

EPSILON = 1e-06
NEGATIVE = -1e30
GELU_SCALE = 0.7978845608028654
GELU_CUBIC = 0.044715
SCALE = 1.0 / math.sqrt(HEAD_DIM)
SCALE_LOG2 = SCALE * math.log2(math.e)

BF = jnp.bfloat16
F32 = jnp.float32
MIB = 1 << 20
LONG = 1e11


def swapped(value, axis, distance):
    count = lax.axis_size(axis)
    return lax.ppermute(value, axis, [(place, place ^ distance) for place in range(count)])


def shifted(value, axis, steps):
    count = lax.axis_size(axis)
    first, last = (max(0, -steps), min(count, count - steps))
    return lax.ppermute(value, axis, [(source, source + steps) for source in range(first, last)])


def add_low(*terms):
    total = terms[0].astype(F32)
    for term in terms[1:]:
        total = total + term.astype(F32)
    return total.astype(BF)


def pick(value, index, axis):
    return lax.dynamic_index_in_dim(value, index, axis, False)


def product(left, right):
    return jnp.dot(left, right, preferred_element_type=F32)


def product_tn(left, right):
    return lax.dot_general(left, right, (((0,), (0,)), ((), ())), preferred_element_type=F32)


def product_nt(left, right):
    return lax.dot_general(left, right, (((1,), (1,)), ((), ())), preferred_element_type=F32)


def rms_scale(field):
    return lax.rsqrt(jnp.mean(field * field, axis=-1, keepdims=True) + EPSILON)


def shape(dims, dtype):
    return jax.ShapeDtypeStruct(dims, dtype)


def whole(dims):
    return pl.BlockSpec(dims, lambda *_: (0,) * len(dims))


def fixed(dims):
    return pl.BlockSpec(dims, lambda *_: (0,) * len(dims), pipeline_mode=pl.Buffered(1))


class Clock:
    def __init__(self, flags):
        self.flags = flags

    def after(self, *values):
        self.flags = lax.optimization_barrier((self.flags, values))[0]

    def at(self, value):
        return lax.optimization_barrier((value, self.flags))[0]

    def run(self, kernel, outs, args, grid, in_specs, out_specs, scratch=(), flops=0, limit=24, stream=False):
        nbytes = sum(math.prod(a.shape) * a.dtype.itemsize for a in args) + sum(
            math.prod(o.shape) * o.dtype.itemsize for o in outs
        )
        args = [
            pltpu.with_memory_space_constraint(arg, pltpu.HBM)
            if stream and spec.block_shape != arg.shape
            else arg
            for arg, spec in zip(args, in_specs)
        ]
        results = pl.pallas_call(
            kernel,
            out_shape=outs,
            grid_spec=pltpu.PrefetchScalarGridSpec(
                num_scalar_prefetch=1,
                grid=grid,
                in_specs=in_specs,
                out_specs=out_specs,
                scratch_shapes=list(scratch),
            ),
            compiler_params=pltpu.CompilerParams(
                dimension_semantics=("arbitrary",) * len(grid), vmem_limit_bytes=limit * MIB
            ),
            cost_estimate=pl.CostEstimate(
                flops=int(flops), bytes_accessed=int(nbytes), transcendentals=0
            ),
        )(self.flags, *args)
        self.after(results[0])
        return results


START, CORE, CHIP = 0, 1, 2


def front_kernel(flags, tokens, gain, wq, wk, wv, normed, queries, pair):
    @pl.when(pl.program_id(0) == 0)
    def _():
        inputs = tokens[...].astype(F32)
        normed[...] = (inputs * rms_scale(inputs) * gain[...]).astype(BF)

    rows = normed[...]
    queries[...] = product(rows, wq[...]).astype(BF)
    pair[0] = product(rows, wk[...]).astype(BF)
    pair[1] = product(rows, wv[...]).astype(BF)


def front(clock, tokens, gain, wq, wk, wv):
    step = 256
    column = pl.BlockSpec((D, step), lambda j, *_: (0, j))
    return clock.run(
        front_kernel,
        (shape((W, D), BF), shape((W, D), BF), shape((2, W, D), BF)),
        (tokens, gain, wq, wk, wv),
        (D // step,),
        [whole((W, D)), whole((1, D)), column, column, column],
        (
            whole((W, D)),
            pl.BlockSpec((W, step), lambda j, *_: (0, j)),
            pl.BlockSpec((2, W, step), lambda j, *_: (0, 0, j)),
        ),
        flops=6 * W * D * D,
        stream=True,
    )


def left_kernel(flags, tokens, gain, wk, wv, pair, normed):
    @pl.when(pl.program_id(0) == 0)
    def _():
        inputs = tokens[...].astype(F32)
        normed[...] = (inputs * rms_scale(inputs) * gain[...]).astype(BF)

    rows = normed[...]
    pair[0] = product(rows, wk[...]).astype(BF)
    pair[1] = product(rows, wv[...]).astype(BF)


def left_pair(clock, tokens, gain, wk, wv):
    step = 256
    column = pl.BlockSpec((D, step), lambda j, *_: (0, j))
    return clock.run(
        left_kernel,
        (shape((2, W, D), BF),),
        (tokens, gain, wk, wv),
        (D // step,),
        [whole((W, D)), whole((1, D)), column, column],
        (pl.BlockSpec((2, W, step), lambda j, *_: (0, 0, j)),),
        [pltpu.VMEM((W, D), BF)],
        flops=LONG,
    )[0]


def summary_probs_of(keys, asks):
    raw = product_nt(keys, asks) * SCALE_LOG2
    expos = jnp.exp2(raw - jnp.max(raw, axis=0, keepdims=True))
    return expos, jnp.sum(expos, axis=0, keepdims=True)


def gates_kernel(
    flags, asks, pair, wu, wg, bias, initial, summary, forget, update, give, own, work
):
    step = pl.program_id(0)

    @pl.when(step < 4)
    def _():
        for head in range(2):
            at = slice(head * HEAD_DIM, (head + 1) * HEAD_DIM)
            expos, total = summary_probs_of(pair[0, :, at], asks[:, at])
            held = product_tn(pair[1, :, at], expos.astype(BF)) / total
            place = pl.multiple_of(step * 256 + head * HEAD_DIM, HEAD_DIM)
            summary[:, pl.ds(place, HEAD_DIM)] = held.T.astype(BF)

    @pl.when(step >= 4)
    def _():
        start = flags[START].astype(F32)
        rows = summary[...]
        fresh = product(rows, wu[...])
        gate = jax.nn.sigmoid(product(rows, wg[...]) + bias[...])
        update[...] = fresh
        forget[...] = gate
        work[0] = (1.0 - start) * gate
        work[1] = start * gate * initial[...] + (1.0 - gate) * fresh
        mine = pl.multiple_of(flags[CORE] * HALF, HALF)
        others = pl.multiple_of((1 - flags[CORE]) * HALF, HALF)
        for part in range(2):
            own[part] = work[part, pl.ds(mine, HALF)].astype(BF)
            give[part] = work[part, pl.ds(others, HALF)].astype(BF)


def gates(clock, asks, pair, state_weight, bias, initial):
    step = 256
    early = lambda i, *_: (0, jnp.minimum(i, 3))
    late = lambda i, *_: (0, jnp.maximum(i - 4, 0))
    late3 = lambda i, *_: (0, 0, jnp.maximum(i - 4, 0))
    return clock.run(
        gates_kernel,
        (
            shape((NS, D), BF),
            shape((NS, D), F32),
            shape((NS, D), F32),
            shape((2, HALF, D), BF),
            shape((2, HALF, D), BF),
        ),
        (asks, pair, state_weight, state_weight, bias, initial),
        (8,),
        [
            pl.BlockSpec((NS, step), early),
            pl.BlockSpec((2, W, step), lambda i, *_: (0, 0, jnp.minimum(i, 3))),
            pl.BlockSpec((D, step), late),
            pl.BlockSpec((D, step), lambda i, *_: (0, jnp.maximum(i - 4, 0) + D // step)),
            pl.BlockSpec((1, step), late),
            pl.BlockSpec((NS, step), late),
        ],
        (
            whole((NS, D)),
            pl.BlockSpec((NS, step), late),
            pl.BlockSpec((NS, step), late),
            pl.BlockSpec((2, HALF, step), late3),
            pl.BlockSpec((2, HALF, step), late3),
        ),
        [pltpu.VMEM((2, NS, step), F32)],
        flops=4 * NS * W * D + 4 * NS * D * D,
    )


def rows_of(chip):
    return pl.ds(pl.multiple_of(chip * QUARTER, QUARTER), QUARTER)


def compose_kernel(flags, own, recv, keep, to1, to2, to3, work):
    odd_core = flags[CORE] == 1
    pick2 = lambda part: (own[part].astype(F32), recv[part].astype(F32))
    (own_scale, recv_scale), (own_base, recv_base) = pick2(0), pick2(1)
    later_scale = jnp.where(odd_core, own_scale, recv_scale)
    earlier_base = jnp.where(odd_core, recv_base, own_base)
    later_base = jnp.where(odd_core, own_base, recv_base)
    work[0] = own_scale * recv_scale
    work[1] = later_scale * earlier_base + later_base
    for far, out in enumerate((keep, to1, to2, to3)):
        out[...] = work[:, rows_of(flags[CHIP] ^ far)].astype(BF)


def prefix_kernel(flags, keep, from1, from2, from3, mine, to1, to2, to3, got, enter):
    for far, came in enumerate((keep, from1, from2, from3)):
        got[flags[CHIP] ^ far] = came[...].astype(F32)
    state = got[0, 1]
    enter[0] = jnp.zeros_like(state)
    enter[1] = state
    for chip in (1, 2):
        state = got[chip, 0] * state + got[chip, 1]
        enter[chip + 1] = state
    for far, out in enumerate((mine, to1, to2, to3)):
        out[...] = enter[flags[CHIP] ^ far].astype(BF)


def previous_kernel(flags, mine, from1, from2, from3, own, recv, keep, give, before):
    for far, came in enumerate((mine, from1, from2, from3)):
        before[rows_of(flags[CHIP] ^ far)] = came[...].astype(F32)
    odd_core = flags[CORE] == 1
    scale = jnp.where(odd_core, recv[0].astype(F32), own[0].astype(F32))
    base = jnp.where(odd_core, recv[1].astype(F32), own[1].astype(F32))
    entry = before[...]
    between = scale * entry + base
    keep[...] = jnp.where(odd_core, between, entry).astype(BF)
    give[...] = jnp.where(odd_core, entry, between).astype(BF)


def compose_back_kernel(flags, own, recv, own_pair, recv_pair, keep, to1, to2, to3, work):
    odd_core = flags[CORE] == 1
    scale = jnp.where(odd_core, recv_pair[0].astype(F32), own_pair[0].astype(F32))
    mine, other = own[...].astype(F32), recv[...].astype(F32)
    work[...] = scale * jnp.where(odd_core, mine, other) + jnp.where(odd_core, other, mine)
    for far, out in enumerate((keep, to1, to2, to3)):
        out[...] = work[rows_of(flags[CHIP] ^ far)].astype(BF)


def suffix_kernel(
    flags, keep, from1, from2, from3, kept0, kept1, kept2, kept3, mine, to1, to2, to3, got, enter
):
    pairs = ((keep, kept0), (from1, kept1), (from2, kept2), (from3, kept3))
    for far, (came, kept) in enumerate(pairs):
        got[flags[CHIP] ^ far, 0] = kept[0].astype(F32)
        got[flags[CHIP] ^ far, 1] = came[...].astype(F32)
    state = got[3, 1]
    enter[3] = jnp.zeros_like(state)
    enter[2] = state
    for chip in (2, 1):
        state = got[chip, 0] * state + got[chip, 1]
        enter[chip - 1] = state
    for far, out in enumerate((mine, to1, to2, to3)):
        out[...] = enter[flags[CHIP] ^ far].astype(BF)


def following_kernel(
    flags, mine, from1, from2, from3, own, recv, own_pair, recv_pair, keep, give, after
):
    for far, came in enumerate((mine, from1, from2, from3)):
        after[rows_of(flags[CHIP] ^ far)] = came[...].astype(F32)
    odd_core = flags[CORE] == 1
    scale = jnp.where(odd_core, own_pair[0].astype(F32), recv_pair[0].astype(F32))
    base = jnp.where(odd_core, own[...].astype(F32), recv[...].astype(F32))
    entry = after[...]
    between = scale * entry + base
    keep[...] = jnp.where(odd_core, entry, between).astype(BF)
    give[...] = jnp.where(odd_core, between, entry).astype(BF)


def small(clock, kernel, outs, args, scratch):
    return clock.run(
        kernel,
        tuple(shape(dims, BF) for dims in outs),
        args,
        (1,),
        [whole(a.shape) for a in args],
        tuple(whole(dims) for dims in outs),
        [pltpu.VMEM(dims, F32) for dims in scratch],
        limit=10,
    )


def to_chips(values):
    return (values[0],) + tuple(
        swapped(value, "seq", 2 * far) for far, value in zip((1, 2, 3), values[1:])
    )


PAIR_WORK = [(4, 2, QUARTER, D), (4, QUARTER, D)]


def compose(clock, own, recv):
    return to_chips(small(clock, compose_kernel, [(2, QUARTER, D)] * 4, (own, recv), [(2, HALF, D)]))


def prefix(clock, got):
    return to_chips(small(clock, prefix_kernel, [(QUARTER, D)] * 4, got, PAIR_WORK))


def previous(clock, back, own, recv):
    mine, other = small(
        clock, previous_kernel, [(HALF, D)] * 2, back + (own, recv), [(HALF, D)]
    )
    return mine, swapped(other, "seq", 1)


def compose_back(clock, *args):
    return to_chips(small(clock, compose_back_kernel, [(QUARTER, D)] * 4, args, [(HALF, D)]))


def suffix(clock, got, kept):
    return to_chips(small(clock, suffix_kernel, [(QUARTER, D)] * 4, got + kept, PAIR_WORK))


def following(clock, back, *args):
    mine, other = small(clock, following_kernel, [(HALF, D)] * 2, back + args, [(HALF, D)])
    return mine, swapped(other, "seq", 1)


def state_kernel(
    flags, mine, other, initial, forget, update, wk, wv, state_in, state_low, state_out, pair
):
    @pl.when(pl.program_id(0) == 0)
    def _():
        start = flags[START].astype(F32)
        for core, came in ((flags[CORE], mine), (1 - flags[CORE], other)):
            rows = pl.ds(pl.multiple_of(core * HALF, HALF), HALF)
            entry = (1.0 - start) * came[...].astype(F32) + start * initial[rows, :]
            gate = forget[rows, :]
            state_in[rows, :] = entry
            state_low[rows, :] = entry.astype(BF)
            state_out[rows, :] = gate * entry + (1.0 - gate) * update[rows, :]

    rows = state_low[...]
    pair[0] = product(rows, wk[...]).astype(BF)
    pair[1] = product(rows, wv[...]).astype(BF)


def state_pair(clock, mine, other, initial, forget, update, wk, wv):
    step = 256
    column = pl.BlockSpec((D, step), lambda j, *_: (0, j))
    return clock.run(
        state_kernel,
        (shape((NS, D), F32), shape((NS, D), BF), shape((NS, D), F32), shape((2, NS, D), BF)),
        (mine, other, initial, forget, update, wk, wv),
        (D // step,),
        [whole((HALF, D))] * 2 + [whole((NS, D))] * 3 + [column, column],
        (
            whole((NS, D)),
            whole((NS, D)),
            whole((NS, D)),
            pl.BlockSpec((2, NS, step), lambda j, *_: (0, 0, j)),
        ),
        flops=4 * NS * D * D,
    )


def masked_scores(flags, queries, left, own, state):
    seen = []
    left_bias = jnp.where(flags[START] == 0, 0.0, NEGATIVE).astype(F32)
    seen.append(product_nt(left[0], queries) * SCALE_LOG2 + left_bias)
    rows = lax.broadcasted_iota(jnp.int32, (W, W), 0)
    cols = lax.broadcasted_iota(jnp.int32, (W, W), 1)
    seen.append(jnp.where(rows <= cols, product_nt(own[0], queries) * SCALE_LOG2, NEGATIVE))
    seen.append(product_nt(state[0], queries) * SCALE_LOG2)
    return seen


PER_STEP = 2


def each_head(*refs):
    for head in range(PER_STEP):
        at = pl.ds(head * HEAD_DIM, HEAD_DIM)
        yield head, [ref.at[..., at] for ref in refs]


def attend_kernel(flags, *refs):
    lse = refs[-1]
    for head, (queries, left, own, state, attended) in each_head(*refs[:-1]):
        seen = masked_scores(flags, queries[...], left, own, state)
        peak = functools.reduce(
            jnp.maximum, [jnp.max(part, axis=0, keepdims=True) for part in seen]
        )
        held = 0.0
        total = 0.0
        for part, pair in zip(seen, (left, own, state)):
            expos = jnp.exp2(part - peak)
            total = total + jnp.sum(expos, axis=0, keepdims=True)
            held = held + product_tn(pair[1], expos.astype(BF))
        attended[...] = (held / total).T.astype(BF)
        lse[head] = peak + jnp.log2(total)


HEADS_WIDE = PER_STEP * HEAD_DIM


def attend(clock, queries, left, own, state):
    head = pl.BlockSpec((W, HEADS_WIDE), lambda h, *_: (0, h))
    pair = pl.BlockSpec((2, W, HEADS_WIDE), lambda h, *_: (0, 0, h))
    return clock.run(
        attend_kernel,
        (shape((W, D), BF), shape((HEADS, 1, W), F32)),
        (queries, left, own, state),
        (HEADS // PER_STEP,),
        [head, pair, pair, pair],
        (head, pl.BlockSpec((PER_STEP, 1, W), lambda h, *_: (h, 0, 0))),
        flops=4 * W * (2 * W + NS) * D,
        stream=True,
        limit=36,
    )


def attend_back_kernel(flags, queries, left, own, state, grad, lse, *outs):
    for head, (asks, left_h, own_h, state_h, grad_h, queries_grad, *grads) in each_head(
        queries, left, own, state, grad, *outs
    ):
        asks, out_grad = asks[...], grad_h[...]
        pairs = (left_h, own_h, state_h)
        seen = masked_scores(flags, asks, *pairs)
        probs = [jnp.exp2(part - lse[head]) for part in seen]
        prob_grads = [product_nt(pair[1], out_grad) for pair in pairs]
        rowdot = sum(
            jnp.sum(prob * prob_grad, axis=0, keepdims=True)
            for prob, prob_grad in zip(probs, prob_grads)
        )
        total = 0.0
        for prob, prob_grad, pair, out in zip(probs, prob_grads, pairs, grads):
            score_grad = (prob * (prob_grad - rowdot)).astype(BF)
            out[0] = (product(score_grad, asks) * SCALE).astype(out.dtype)
            out[1] = product(prob.astype(BF), out_grad).astype(out.dtype)
            total = total + product_tn(pair[0], score_grad)
        queries_grad[...] = (total * SCALE).T.astype(BF)


def attend_back(clock, queries, left, own, state, grad, lse):
    head = pl.BlockSpec((W, HEADS_WIDE), lambda h, *_: (0, h))
    pair = pl.BlockSpec((2, W, HEADS_WIDE), lambda h, *_: (0, 0, h))
    return clock.run(
        attend_back_kernel,
        (shape((W, D), BF), shape((2, W, D), BF), shape((2, W, D), F32), shape((2, NS, D), BF)),
        (queries, left, own, state, grad, lse),
        (HEADS // PER_STEP,),
        [head, pair, pair, pair, head, pl.BlockSpec((PER_STEP, 1, W), lambda h, *_: (h, 0, 0))],
        (head, pair, pair, pair),
        flops=10 * W * (2 * W + NS) * D,
        stream=True,
        limit=48,
    )


def gelu_parts(upper):
    square = upper * upper
    inner = GELU_SCALE * (upper + GELU_CUBIC * square * upper)
    bent = jnp.tanh(inner)
    value = 0.5 * upper * (1.0 + bent)
    slope = 0.5 * (1.0 + bent) + 0.5 * upper * (1.0 - bent * bent) * GELU_SCALE * (
        1.0 + 3.0 * GELU_CUBIC * square
    )
    return value, slope


def mlp_step(normed_mlp, cotangent, up1, up2, down, up, activated, upper_grad, total, grad):
    half = up1.shape[1]
    up[:, :half] = up1[...]
    up[:, half:] = up2[...]
    rows = down[...].reshape(2 * half, D)
    value, slope = gelu_parts(product(normed_mlp[...], up[...]))
    value = value.astype(BF)
    activated[...] = value
    total[...] += product(value, rows)
    back = product_nt(cotangent[...], rows).astype(BF).astype(F32)
    back = (back * slope).astype(BF)
    upper_grad[...] = back
    grad[...] += product_nt(back, up[...])


def mlp_first_kernel(
    flags,
    attended,
    tokens,
    out_weight,
    gain,
    cotangent,
    up1,
    up2,
    down,
    activated,
    upper_grad,
    normed_mlp,
    hidden,
    total,
    grad,
    up,
):
    @pl.when(pl.program_id(0) == 0)
    def _():
        field = tokens[...].astype(F32) + product(attended[...], out_weight[...])
        hidden[...] = field
        normed_mlp[...] = (field * rms_scale(field) * gain[...]).astype(BF)
        total[...] = field
        grad[...] = jnp.zeros_like(field)

    mlp_step(normed_mlp, cotangent, up1, up2, down, up, activated, upper_grad, total, grad)


def mlp_second_kernel(
    flags,
    normed_mlp,
    hidden,
    total_in,
    grad_in,
    out_weight,
    gain,
    cotangent,
    up1,
    up2,
    down,
    activated,
    upper_grad,
    mixed,
    hidden_grad,
    attended_grad,
    heads_grad,
    gain_grad,
    total,
    grad,
    up,
):
    step = pl.program_id(0)

    @pl.when(step == 0)
    def _():
        total[...] = total_in[...]
        grad[...] = grad_in[...]

    mlp_step(normed_mlp, cotangent, up1, up2, down, up, activated, upper_grad, total, grad)

    @pl.when(step == pl.num_programs(0) - 1)
    def _():
        mixed[...] = total[...].astype(BF)
        field = hidden[...]
        scaled = rms_scale(field)
        gain_grad[...] = jnp.sum(grad[...] * field * scaled, axis=0, keepdims=True)
        weighted = grad[...] * gain[...]
        field_grad = (
            cotangent[...].astype(F32)
            + scaled * weighted
            - field
            * (scaled * scaled * scaled * jnp.mean(weighted * field, axis=-1, keepdims=True))
        )
        hidden_grad[...] = field_grad
        low = field_grad.astype(BF)
        attended_grad[...] = low
        heads_grad[...] = product_nt(low, out_weight[...]).astype(BF)


PIECE = 256
PAIRS = FF // (4 * PIECE)


def mlp_specs(part):
    return [
        pl.BlockSpec((D, PIECE), lambda j, *_: (0, 4 * j + part)),
        pl.BlockSpec((D, PIECE), lambda j, *_: (0, 4 * j + 2 + part)),
        pl.BlockSpec((2, PIECE, D), lambda j, *_: (j, part, 0)),
    ]


def mlp_halves():
    return pl.BlockSpec((W, 2 * PIECE), lambda j, *_: (0, j))


def mlp_first(clock, attended, tokens, out_weight, gain, cotangent, up, down):
    rows = whole((W, D))
    return clock.run(
        mlp_first_kernel,
        (
            shape((W, FF // 2), BF),
            shape((W, FF // 2), BF),
            shape((W, D), BF),
            shape((W, D), F32),
            shape((W, D), F32),
            shape((W, D), F32),
        ),
        (attended, tokens, out_weight, gain, cotangent, up, up, down),
        (PAIRS,),
        [fixed((W, D)), fixed((W, D)), fixed((D, D)), fixed((1, D)), fixed((W, D))] + mlp_specs(0),
        (mlp_halves(), mlp_halves(), rows, rows, rows, rows),
        [pltpu.VMEM((D, 2 * PIECE), BF)],
        flops=4 * W * D * FF + 2 * W * D * D,
        limit=36,
    )


def mlp_second(clock, normed_mlp, hidden, total, grad, out_weight, gain, cotangent, up, down):
    rows = whole((W, D))
    return clock.run(
        mlp_second_kernel,
        (
            shape((W, FF // 2), BF),
            shape((W, FF // 2), BF),
            shape((W, D), BF),
            shape((W, D), F32),
            shape((W, D), BF),
            shape((W, D), BF),
            shape((1, D), F32),
        ),
        (normed_mlp, hidden, total, grad, out_weight, gain, cotangent, up, up, down),
        (PAIRS,),
        [fixed((W, D))] * 4
        + [fixed((D, D)), fixed((1, D)), fixed((W, D))]
        + mlp_specs(1),
        (mlp_halves(), mlp_halves(), rows, rows, rows, rows, whole((1, D))),
        [pltpu.VMEM((W, D), F32), pltpu.VMEM((W, D), F32), pltpu.VMEM((D, 2 * PIECE), BF)],
        flops=4 * W * D * FF + 2 * W * D * D,
        limit=36,
    )


def direct_kernel(flags, state_grad, wk, wv, forget, cotangent, direct, own, give, work):
    grad = product_nt(state_grad[0], wk[...]) + product_nt(state_grad[1], wv[...])
    direct[...] = grad
    keep = 1.0 - flags[START].astype(F32)
    work[...] = keep * (forget[...] * cotangent[...] + grad)
    own[...] = work[pl.ds(pl.multiple_of(flags[CORE] * HALF, HALF), HALF)].astype(BF)
    give[...] = work[pl.ds(pl.multiple_of((1 - flags[CORE]) * HALF, HALF), HALF)].astype(BF)


def direct_grad(clock, state_grad, wk, wv, forget, cotangent):
    step = 256
    row = pl.BlockSpec((step, D), lambda j, *_: (j, 0))
    column = pl.BlockSpec((NS, step), lambda j, *_: (0, j))
    half = pl.BlockSpec((HALF, step), lambda j, *_: (0, j))
    return clock.run(
        direct_kernel,
        (shape((NS, D), F32), shape((HALF, D), BF), shape((HALF, D), BF)),
        (state_grad, wk, wv, forget, cotangent),
        (D // step,),
        [whole((2, NS, D)), row, row, column, column],
        (column, half, half),
        [pltpu.VMEM((NS, step), F32)],
        flops=4 * NS * D * D,
    )


def state_back_kernel(
    flags,
    mine,
    other,
    cotangent,
    forget,
    update,
    state_in,
    direct,
    wu,
    wg,
    initial_grad,
    projected_grad,
    bias_grad,
    summary_grad,
    work,
    total,
):
    step = pl.program_id(0)
    for core, came in ((flags[CORE], mine), (1 - flags[CORE], other)):
        work[pl.ds(pl.multiple_of(core * HALF, HALF), HALF)] = came[...].astype(F32)
    out_grad = cotangent[...] + work[...]
    gate = forget[...]
    start = flags[START].astype(F32)
    initial_grad[...] = (start * (gate * out_grad + direct[...])).astype(BF)
    rest = 1.0 - gate
    gate_grad = out_grad * (state_in[...] - update[...]) * gate * rest
    bias_grad[...] = jnp.sum(gate_grad, axis=0, keepdims=True)
    fresh_grad = (out_grad * rest).astype(BF)
    gate_low = gate_grad.astype(BF)
    projected_grad[0] = fresh_grad
    projected_grad[1] = gate_low
    part = product_nt(fresh_grad, wu[...]) + product_nt(gate_low, wg[...])

    @pl.when(step == 0)
    def _():
        total[...] = part

    @pl.when(step > 0)
    def _():
        total[...] += part

    @pl.when(step == pl.num_programs(0) - 1)
    def _():
        summary_grad[...] = total[...].astype(BF)


def state_back(clock, mine, other, cotangent, forget, update, state_in, direct, state_weight):
    step = 256
    column = pl.BlockSpec((NS, step), lambda j, *_: (0, j))
    half = pl.BlockSpec((HALF, step), lambda j, *_: (0, j))
    return clock.run(
        state_back_kernel,
        (
            shape((NS, D), BF),
            shape((2, NS, D), BF),
            shape((1, D), F32),
            shape((NS, D), BF),
        ),
        (mine, other, cotangent, forget, update, state_in, direct, state_weight, state_weight),
        (D // step,),
        [half, half, column, column, column, column, column]
        + [
            pl.BlockSpec((D, step), lambda j, *_: (0, j)),
            pl.BlockSpec((D, step), lambda j, *_: (0, j + D // step)),
        ],
        (
            column,
            pl.BlockSpec((2, NS, step), lambda j, *_: (0, 0, j)),
            pl.BlockSpec((1, step), lambda j, *_: (0, j)),
            whole((NS, D)),
        ),
        [pltpu.VMEM((NS, step), F32), pltpu.VMEM((NS, D), F32)],
        flops=4 * NS * D * D,
    )


def summary_back_kernel(flags, *refs):
    for _, (asks, pair, grad, own_grad, asks_grad, pair_total) in each_head(*refs):
        queries, out_grad = asks[...], grad[...]
        expos, total = summary_probs_of(pair[0], queries)
        probs = expos * (1.0 / total)
        prob_grad = product_nt(pair[1], out_grad)
        rowdot = jnp.sum(probs * prob_grad, axis=0, keepdims=True)
        score_grad = (probs * (prob_grad - rowdot)).astype(BF)
        asks_grad[...] = (product_tn(pair[0], score_grad) * SCALE).T.astype(BF)
        pair_total[0] = (own_grad[0] + product(score_grad, queries) * SCALE).astype(BF)
        pair_total[1] = (own_grad[1] + product(probs.astype(BF), out_grad)).astype(BF)


def summary_back(clock, asks, pair, grad, own_grad):
    head = pl.BlockSpec((W, HEADS_WIDE), lambda h, *_: (0, h))
    both = pl.BlockSpec((2, W, HEADS_WIDE), lambda h, *_: (0, 0, h))
    return clock.run(
        summary_back_kernel,
        (shape((NS, D), BF), shape((2, W, D), BF)),
        (asks, pair, grad, own_grad),
        (HEADS // PER_STEP,),
        [head, both, head, both],
        (head, both),
        flops=10 * NS * W * D,
        stream=True,
    )


def tokens_back_kernel(
    flags,
    queries_grad,
    pair_total,
    returned,
    wq,
    wk,
    wv,
    tokens,
    gain,
    hidden_grad,
    tokens_grad,
    gain_grad,
    total,
):
    step = pl.program_id(0)

    @pl.when(step < 2)
    def _():
        part = product_nt(queries_grad[...], wq[...])
        total[...] = jnp.where(step == 0, part, total[...] + part)

    @pl.when((step >= 2) & (step < 4))
    def _():
        total[...] += product_nt(add_low(pair_total[0], returned[0]), wk[...])

    @pl.when(step >= 4)
    def _():
        total[...] += product_nt(add_low(pair_total[0], returned[0]), wv[...])

    @pl.when(step == 5)
    def _():
        inputs = tokens[...].astype(F32)
        scaled = rms_scale(inputs)
        grad = total[...]
        gain_grad[...] = jnp.sum(grad * inputs * scaled, axis=0, keepdims=True)
        weighted = grad * gain[...]
        tokens_grad[...] = (
            hidden_grad[...]
            + scaled * weighted
            - inputs
            * (scaled * scaled * scaled * jnp.mean(weighted * inputs, axis=-1, keepdims=True))
        )


def tokens_back(clock, queries_grad, pair_total, returned, wq, wk, wv, tokens, gain, hidden_grad):
    step = D // 2
    clamp = lambda i, low: jnp.clip(i - low, 0, 1)
    weight = lambda low: pl.BlockSpec((D, step), lambda i, *_: (0, clamp(i, low)))
    later = lambda i: jnp.maximum(i - 2, 0)
    pair = pl.BlockSpec((1, W, step), lambda i, *_: (later(i) // 2, 0, later(i) % 2))
    return clock.run(
        tokens_back_kernel,
        (shape((W, D), F32), shape((1, D), F32)),
        (queries_grad, pair_total, returned, wq, wk, wv, tokens, gain, hidden_grad),
        (6,),
        [
            pl.BlockSpec((W, step), lambda i, *_: (0, clamp(i, 0))),
            pair,
            pair,
            weight(0),
            weight(2),
            weight(4),
            fixed((W, D)),
            fixed((1, D)),
            fixed((W, D)),
        ],
        (whole((W, D)), whole((1, D))),
        [pltpu.VMEM((W, D), F32)],
        flops=6 * W * D * D,
    )


def chunk_natural(flags, place):
    return place


def chunk_along_x(flags, place):
    x = flags[CHIP] & 1
    return 2 * (place % 2) + (1 - x if place < 2 else x)


def chunk_along_y(flags, place):
    y = flags[CHIP] >> 1
    return 2 * (1 - y if place < 2 else y) + place % 2


def column_blocks(terms):
    return terms[0][1][0][0].shape[2] // D


def weight_kernel(plan, merge, flags, *refs):
    refs = list(refs)
    lefts = [refs.pop(0) for _ in range(plan["lefts"])]
    rights = [[refs.pop(0) for _ in adds] for adds in plan["rights"]]
    extras = [refs.pop(0) for _ in range(plan["extras"])]
    recv = refs.pop(0) if merge else None
    work = refs.pop()
    core = flags[CORE] if merge else 1 - flags[CORE]
    step, base, start = pl.program_id(0), 0, 0

    def write(along, place, at, here, part):
        rows = part.shape[0]
        if merge:
            chunk = (chunk_along_x, chunk_along_y)[along](flags, place)
            part = part.astype(F32) + recv[chunk, at : at + rows].astype(F32)
            refs[2 * along + place // 2][place % 2, here : here + rows] = part.astype(BF)
        else:
            refs[0][place, at : at + rows] = part.astype(BF)

    def source(along, place):
        chunk_of = (chunk_along_x, chunk_along_y)[along] if merge else chunk_natural
        return 2 * chunk_of(flags, place) + core

    for along, group in enumerate(plan["grads"]):
        here = 0
        for rows, blocks, terms in group:

            @pl.when(step == base)
            def _():
                for term, (left, _) in enumerate(terms):
                    for place in range(4):
                        first = pl.multiple_of(source(along, place) * rows, rows)
                        block = lefts[left][:, pl.ds(first, rows)]
                        work[term, place * rows : (place + 1) * rows] = block.T

            for block in range(blocks):

                @pl.when(step == base + block)
                def _():
                    total = 0.0
                    for term, (_, right) in enumerate(terms):
                        parts = [part[0] for part in rights[right]]
                        value = parts[0] if len(parts) == 1 else add_low(*parts)
                        total = total + product(work[term, : 4 * rows], value)
                    at = block * rows
                    for place in range(4):
                        part = total[place * rows : (place + 1) * rows]
                        write(along, place, start + at, here + at, part)

            base += blocks
            start += blocks * rows
            here += blocks * rows
        if extras:
            rows = extras[along].shape[0] // 8

            @pl.when(step == 0)
            def _():
                for place in range(4):
                    first = pl.multiple_of(source(along, place) * rows, rows)
                    write(along, place, start, here, extras[along][pl.ds(first, rows)])

            start += rows


def weight_pair(clock, grads, extras, recv):
    lefts, left_ids, rights, args, specs, plans = [], {}, [], [], [], []
    base, start, tokens, most = 0, 0, grads[0][0][0][0].shape[0], 0
    sizes = []
    for along, group in enumerate(grads):
        total, plan = 0, []
        for terms in group:
            rows, blocks = terms[0][0].shape[1] // 8, column_blocks(terms)
            most = max(most, rows)
            steps = []
            for left, adds in terms:
                if id(left) not in left_ids:
                    left_ids[id(left)] = len(lefts)
                    lefts.append(left)
                steps.append((left_ids[id(left)], len(rights)))
                rights.append(tuple(index for _, index in adds))
                for right, index in adds:
                    args.append(right)
                    specs.append(
                        pl.BlockSpec(
                            (1, tokens, D),
                            lambda j, *_, index=index, base=base, blocks=blocks: (
                                index,
                                0,
                                jnp.clip(j - base, 0, blocks - 1),
                            ),
                        )
                    )
            plan.append((rows, blocks, steps))
            base += blocks
            total += blocks * rows
        if extras:
            total += extras[along].shape[0] // 8
        plans.append(plan)
        sizes.append(total)
        start += total
    args = lefts + args + list(extras)
    specs = [fixed(left.shape) for left in lefts] + specs + [fixed(e.shape) for e in extras]
    merge = recv is not None
    if merge:
        args.append(recv)
        specs.append(fixed(recv.shape))
        dims = [(2, total, D) for total in sizes for _ in range(2)]
    else:
        dims = [(4, start, D)]
    plan = {"lefts": len(lefts), "rights": rights, "extras": len(extras), "grads": plans}
    return clock.run(
        functools.partial(weight_kernel, plan, merge),
        tuple(shape(d, BF) for d in dims),
        tuple(args),
        (base,),
        specs,
        tuple(whole(d) for d in dims),
        [pltpu.VMEM((len(grads[0][0]), 4 * most, tokens), BF)],
        flops=2 * tokens * 4 * start * D * len(grads[0][0]),
        limit=30,
    )


def scatter_bits(value, bits, names):
    place = lax.axis_index("seq")
    names = list(names)
    for bit in bits:
        at = names.index(bit)
        mine = (place >> bit) & 1
        recv = swapped(pick(value, 1 - mine, at), "seq", 1 << bit)
        value = add_low(pick(value, mine, at), recv)
        names.pop(at)
    return value


def whole_scatter(value, along_x):
    count = lax.axis_size("seq")
    levels = count.bit_length() - 1
    names = list(range(levels - 1, -1, -1))
    value = value.reshape((2,) * levels + (value.shape[0] // count,) + value.shape[1:])
    bits = [0] + (names[-2::-1] if along_x else names[:-1])
    return scatter_bits(value, bits, names)


def in_rows(value):
    return jnp.concatenate([value[:, at : at + D] for at in range(0, value.shape[1], D)], axis=0)


def turn_kernel(flags, kept1, recv1, kept2, recv2, send1, send2):
    send1[...] = add_low(kept1[0], recv1[0])
    send2[...] = add_low(kept2[0], recv2[0])


def pack_kernel(flags, *refs):
    out, start = refs[-1], 0
    for at in range(0, len(refs) - 1, 3):
        kept, recv, last = refs[at : at + 3]
        rows = last.shape[0]
        out[start : start + rows] = add_low(kept[0], recv[0], last[...])
        start += rows


class Scatter:
    def __init__(self, clock, firsts, seconds, extras=()):
        self.grads, self.extras, self.plain = (firsts, seconds), extras, None
        if lax.axis_size("seq") != 8:
            sums = []
            for number, group in enumerate(self.grads):
                for terms in group:
                    total = 0.0
                    for left, adds in terms:
                        parts = [right[index] for right, index in adds]
                        right = add_low(*parts) if len(parts) > 1 else parts[0]
                        total = total + product_tn(left, right)
                    sums.append(in_rows(whole_scatter(total.astype(BF), number == 0)))
                if extras:
                    sums.append(whole_scatter(extras[number], number == 0))
            self.plain = jnp.concatenate(sums, axis=0)
            return
        (self.give,) = weight_pair(clock, self.grads, self.extras, None)

    def core(self, clock):
        if self.plain is None:
            self.recv = swapped(clock.at(self.give), "seq", 1)

    def keep(self, clock):
        if self.plain is None:
            send1, kept1, send2, kept2 = weight_pair(clock, self.grads, self.extras, self.recv)
            self.kept, self.send = (kept1, kept2), (send1, send2)

    def near(self, clock):
        if self.plain is None:
            self.recv = tuple(
                swapped(clock.at(send), "seq", far) for send, far in zip(self.send, (2, 4))
            )

    def held(self, other):
        args, specs = [], []
        for number, (kept, recv) in enumerate(zip(self.kept, self.recv)):
            bit = 1 - number
            mine = lambda i, flags, bit=bit: (((flags[CHIP] >> bit) & 1) ^ other, 0, 0)
            args.append([kept, recv])
            specs.append([pl.BlockSpec((1,) + kept.shape[1:], mine)] * 2)
        return args, specs

    def turn(self, clock, flops=0):
        if self.plain is None:
            args, specs = self.held(1)
            dims = [kept.shape[1:] for kept in self.kept]
            self.send = clock.run(
                turn_kernel,
                tuple(shape(d, BF) for d in dims),
                tuple(args[0] + args[1]),
                (1,),
                specs[0] + specs[1],
                tuple(whole(d) for d in dims),
                flops=flops,
                limit=10,
            )

    def far(self, clock):
        if self.plain is None:
            self.last = tuple(
                swapped(clock.at(send), "seq", far) for send, far in zip(self.send, (4, 2))
            )

    def parts(self):
        args, specs = self.held(0)
        for number, last in enumerate(self.last):
            args[number].append(last)
            specs[number].append(whole(last.shape))
        return args[0] + args[1], specs[0] + specs[1]


def pack(clock, *scatters):
    if scatters[0].plain is not None:
        return jnp.concatenate([scatter.plain for scatter in scatters], axis=0)
    args, specs = [], []
    for scatter in scatters:
        more = scatter.parts()
        args += more[0]
        specs += more[1]
    total = sum(arg.shape[0] for arg in args[2::3])
    return clock.run(
        pack_kernel,
        (shape((total, D), BF),),
        tuple(args),
        (1,),
        specs,
        (whole((total, D)),),
        limit=16,
    )[0]


class Line:
    def __init__(self, clock, value):
        count = lax.axis_size("dp")
        half = count // 2
        self.value = value
        self.rounds = (
            [([(s, s + 1), (count - 1 - s, count - 2 - s)], None) for s in range(half - 1)]
            + [([(half - 1, half), (half, half - 1)], None)]
            + [
                ([(s + 1, s), (count - 2 - s, count - 1 - s)], (s, count - 1 - s))
                for s in range(half - 2, -1, -1)
            ]
        )
        self.send(clock)

    def send(self, clock):
        self.recv = lax.ppermute(clock.at(self.value), "dp", self.rounds[0][0])

    def take(self, clock):
        place = lax.axis_index("dp")
        takers = self.rounds.pop(0)[1]
        value = clock.at(self.value)
        if takers is None:
            self.value = add_low(value, self.recv)
        else:
            outer = (place == takers[0]) | (place == takers[1])
            self.value = jnp.where(outer, self.recv, value)
        if self.rounds:
            clock.after(self.value)

    def step(self, clock):
        self.take(clock)
        if self.rounds:
            self.send(clock)

    def finish(self, clock):
        while self.rounds:
            self.step(clock)
        return self.value.astype(F32)


def interleaved(first, second):
    blocks = []
    for at in range(0, first.shape[1], PIECE):
        blocks += [first[:, at : at + PIECE], second[:, at : at + PIECE]]
    return jnp.concatenate(blocks, axis=1)


def body(
    tokens,
    item_starts,
    attn_gain,
    query_weight,
    key_weight,
    value_weight,
    output_weight,
    state_queries,
    state_weight,
    gate_bias,
    initial_state,
    mlp_gain,
    up_weight,
    down_weight,
    out_cotangent,
    state_cotangent,
):
    count = lax.axis_size("seq")
    place = lax.axis_index("seq")
    clock = Clock(
        jnp.stack([item_starts[0, 0], place & 1, (place >> 1) & 3]).astype(jnp.int32)
    )
    tokens, cotangent, state_cot = tokens[0], out_cotangent[0], state_cotangent[0, 0]
    attn_gain, gate_bias, mlp_gain = attn_gain[None], gate_bias[None], mlp_gain[None]
    down_weight = down_weight.reshape(FF // (2 * PIECE), 2 * PIECE, D)

    tokens_left = shifted(tokens, "seq", 1)
    normed, queries, own = front(clock, tokens, attn_gain, query_weight, key_weight, value_weight)
    summary, forget, update, give_pair, own_pair = gates(
        clock, state_queries, own, state_weight, gate_bias, initial_state
    )
    recv_pair = swapped(give_pair, "seq", 1)
    left = left_pair(clock, tokens_left, attn_gain, key_weight, value_weight)
    kept_chips = compose(clock, own_pair, recv_pair)
    back = prefix(clock, kept_chips)
    mine, other = previous(clock, back, own_pair, recv_pair)
    state_in, state_low, state_out, state = state_pair(
        clock, mine, other, initial_state, forget, update, key_weight, value_weight
    )
    attended, lse = attend(clock, queries, left, own, state)
    split = count == 8
    activated1, upper_grad1, normed_mlp, hidden, total, grad = mlp_first(
        clock, attended, tokens, output_weight, mlp_gain, cotangent, up_weight, down_weight
    )
    out_grads = (cotangent[None], 0)
    if split:
        feed1 = Scatter(
            clock,
            [[(activated1, [out_grads])]],
            [[(normed_mlp, [(upper_grad1[None], 0)])]],
        )
        feed1.core(clock)
        feed1.keep(clock)
        feed1.near(clock)
    activated2, upper_grad2, mixed, hidden_grad, attended_grad, heads_grad, mlp_gain_grad = (
        mlp_second(
            clock,
            normed_mlp,
            hidden,
            total,
            grad,
            output_weight,
            mlp_gain,
            cotangent,
            up_weight,
            down_weight,
        )
    )
    if split:
        feed2 = Scatter(
            clock,
            [[(activated2, [out_grads])]],
            [[(normed_mlp, [(upper_grad2[None], 0)])]],
        )
        feed2.core(clock)
        feed1.turn(clock, LONG)
        feed1.far(clock)
        feed2.keep(clock)
        feed2.near(clock)
    else:
        feed1 = Scatter(
            clock,
            [[(interleaved(activated1, activated2), [out_grads])]],
            [[(normed_mlp, [(interleaved(upper_grad1, upper_grad2)[None], 0)])]],
        )
    queries_grad, left_grad, own_grad, state_grad = attend_back(
        clock, queries, left, own, state, heads_grad, lse
    )
    direct, own_base, give_base = direct_grad(
        clock, state_grad, key_weight, value_weight, forget, state_cot
    )
    recv_base = swapped(give_base, "seq", 1)
    line1 = Line(clock, pack(clock, feed1))
    got = compose_back(clock, own_base, recv_base, own_pair, recv_pair)
    if split:
        feed2.turn(clock)
    back = suffix(clock, got, kept_chips)
    mine, other = following(clock, back, own_base, recv_base, own_pair, recv_pair)
    if split:
        feed2.far(clock)
    returned = shifted(clock.at(left_grad), "seq", -1)
    line1.step(clock)
    initial_grad, projected_grad, gate_bias_grad, summary_grad = state_back(
        clock, mine, other, state_cot, forget, update, state_in, direct, state_weight
    )
    others = Scatter(
        clock,
        [[(attended, [(attended_grad[None], 0)])], [(summary, [(projected_grad, 0)])]],
        [[(normed, [(queries_grad[None], 0)])], [(summary, [(projected_grad, 1)])]],
    )
    line2 = Line(clock, pack(clock, feed2)) if split else None
    others.core(clock)
    state_queries_grad, pair_total = summary_back(
        clock, state_queries, own, summary_grad, own_grad
    )
    others.keep(clock)
    if split:
        line2.step(clock)
    others.near(clock)
    line1.take(clock)
    keys_values = Scatter(
        clock,
        [[(normed, [(pair_total, 0), (returned, 0)]), (state_low, [(state_grad, 0)])]],
        [[(normed, [(pair_total, 1), (returned, 1)]), (state_low, [(state_grad, 1)])]],
        (state_queries_grad, initial_grad),
    )
    keys_values.core(clock)
    if line1.rounds:
        line1.send(clock)
    keys_values.keep(clock)
    if split:
        line2.take(clock)
    keys_values.near(clock)
    tokens_grad, attn_gain_grad = tokens_back(
        clock,
        queries_grad,
        pair_total,
        returned,
        query_weight,
        key_weight,
        value_weight,
        tokens,
        attn_gain,
        hidden_grad,
    )
    others.turn(clock)
    others.far(clock)
    line1 = line1.finish(clock)
    clock.after(line1)
    lanes, rows = D // count, NS // count
    vectors = jnp.concatenate([attn_gain_grad, gate_bias_grad, mlp_gain_grad])
    vectors = vectors.reshape(3, count, lanes).transpose(1, 0, 2).reshape(count, 1, 3 * lanes)
    vectors = jnp.pad(vectors, ((0, 0), (0, 7), (0, D - 3 * lanes))).astype(BF)
    keys_values.turn(clock)
    keys_values.far(clock)
    vectors = whole_scatter(clock.at(vectors.reshape(-1, D)), True)
    line3 = [Line(clock, half) for half in jnp.split(pack(clock, others), 2)]
    if split:
        line2.send(clock)
    line4 = Line(clock, jnp.concatenate([pack(clock, keys_values), vectors], axis=0))
    for line in line3 + [line4] + line3 + [line4]:
        line.step(clock)
    line3 = [line.finish(clock) for line in line3]
    line4 = line4.finish(clock)
    clock.after(line3, line4)
    line2 = line2.finish(clock) if split else None

    def unpack(packed, *dims):
        pieces, start = [], 0
        for high, wide in dims:
            parts = [
                packed[start + high * part : start + high * (part + 1)] for part in range(wide // D)
            ]
            start += high * (wide // D)
            pieces.append(parts[0] if len(parts) == 1 else jnp.concatenate(parts, axis=1))
        return pieces

    high, deep = D // count, FF // count
    if split:
        down1, up1 = unpack(line1, (deep // 2, D), (high, FF // 2))
        down2, up2 = unpack(line2, (deep // 2, D), (high, FF // 2))
        down_grad = jnp.concatenate([down1, down2], axis=0)
        up_grad = interleaved(up1, up2)
    else:
        down_grad, up_grad = unpack(line1, (deep, D), (high, FF))
    output_grad, first_grad, query_grad, second_grad = unpack(
        jnp.concatenate(line3),
        (high, D),
        (high, D),
        (high, D),
        (high, D),
    )
    state_weight_grad = jnp.concatenate([first_grad, second_grad], axis=1)
    key_grad, state_queries_grad, value_grad, initial_grad, vectors = unpack(
        line4, (high, D), (rows, D), (high, D), (rows, D), (8, D)
    )
    vectors = vectors[0, : 3 * lanes]
    return (
        mixed[None],
        state_out[None, None],
        tokens_grad[None],
        vectors[:lanes],
        query_grad,
        key_grad,
        value_grad,
        output_grad,
        state_queries_grad,
        state_weight_grad,
        vectors[lanes : 2 * lanes],
        initial_grad,
        vectors[2 * lanes :],
        up_grad,
        down_grad,
    )


def solution(mesh):
    in_specs = (
        P("dp", "seq", None),
        P("dp", "seq"),
        P(),
        P(),
        P(),
        P(),
        P(),
        P(),
        P(),
        P(),
        P(),
        P(),
        P(),
        P(),
        P("dp", "seq", None),
        P("dp", "seq", None, None),
    )
    out_specs = (
        P("dp", "seq", None),
        P("dp", "seq", None, None),
        P("dp", "seq", None),
        P("seq"),
        P("seq", None),
        P("seq", None),
        P("seq", None),
        P("seq", None),
        P("seq", None),
        P("seq", None),
        P("seq"),
        P("seq", None),
        P("seq"),
        P("seq", None),
        P("seq", None),
    )
    return jax.shard_map(body, mesh=mesh, in_specs=in_specs, out_specs=out_specs, check_vma=False)
```

```python
import functools
import math

import jax
import jax.numpy as jnp
from jax import lax
from jax.experimental import pallas as pl
from jax.experimental.pallas import tpu as pltpu
from jax.sharding import PartitionSpec as P

D = 1024
HEADS = 8
HEAD_DIM = 128
FF = 4096
W = 512
NS = 512
HALF = NS // 2
QUARTER = NS // 8

EPSILON = 1e-06
NEGATIVE = -1e30
GELU_SCALE = 0.7978845608028654
GELU_CUBIC = 0.044715
SCALE = 1.0 / math.sqrt(HEAD_DIM)
SCALE_LOG2 = SCALE * math.log2(math.e)

BF = jnp.bfloat16
F32 = jnp.float32
MIB = 1 << 20
LONG = 1e11


def swapped(value, axis, distance):
    count = lax.axis_size(axis)
    return lax.ppermute(value, axis, [(place, place ^ distance) for place in range(count)])


def shifted(value, axis, steps):
    count = lax.axis_size(axis)
    first, last = (max(0, -steps), min(count, count - steps))
    return lax.ppermute(value, axis, [(source, source + steps) for source in range(first, last)])


def add_low(*terms):
    total = terms[0].astype(F32)
    for term in terms[1:]:
        total = total + term.astype(F32)
    return total.astype(BF)


def pick(value, index, axis):
    return lax.dynamic_index_in_dim(value, index, axis, False)


def product(left, right):
    return jnp.dot(left, right, preferred_element_type=F32)


def product_tn(left, right):
    return lax.dot_general(left, right, (((0,), (0,)), ((), ())), preferred_element_type=F32)


def product_nt(left, right):
    return lax.dot_general(left, right, (((1,), (1,)), ((), ())), preferred_element_type=F32)


def rms_scale(field):
    return lax.rsqrt(jnp.mean(field * field, axis=-1, keepdims=True) + EPSILON)


def shape(dims, dtype):
    return jax.ShapeDtypeStruct(dims, dtype)


def whole(dims):
    return pl.BlockSpec(dims, lambda *_: (0,) * len(dims))


def fixed(dims):
    return pl.BlockSpec(dims, lambda *_: (0,) * len(dims), pipeline_mode=pl.Buffered(1))


class Clock:
    def __init__(self, flags):
        self.flags = flags

    def after(self, *values):
        self.flags = lax.optimization_barrier((self.flags, values))[0]

    def at(self, value):
        return lax.optimization_barrier((value, self.flags))[0]

    def run(self, kernel, outs, args, grid, in_specs, out_specs, scratch=(), flops=0, limit=20, stream=False):
        nbytes = sum(math.prod(a.shape) * a.dtype.itemsize for a in args) + sum(
            math.prod(o.shape) * o.dtype.itemsize for o in outs
        )
        args = [
            pltpu.with_memory_space_constraint(arg, pltpu.HBM)
            if stream and spec.block_shape != arg.shape
            else arg
            for arg, spec in zip(args, in_specs)
        ]
        results = pl.pallas_call(
            kernel,
            out_shape=outs,
            grid_spec=pltpu.PrefetchScalarGridSpec(
                num_scalar_prefetch=1,
                grid=grid,
                in_specs=in_specs,
                out_specs=out_specs,
                scratch_shapes=list(scratch),
            ),
            compiler_params=pltpu.CompilerParams(
                dimension_semantics=("arbitrary",) * len(grid), vmem_limit_bytes=limit * MIB
            ),
            cost_estimate=pl.CostEstimate(
                flops=int(flops), bytes_accessed=int(nbytes), transcendentals=0
            ),
        )(self.flags, *args)
        self.after(results[0])
        return results


START, CORE, CHIP = 0, 1, 2


def front_kernel(flags, tokens, gain, wq, wk, wv, normed, queries, pair):
    @pl.when(pl.program_id(0) == 0)
    def _():
        inputs = tokens[...].astype(F32)
        normed[...] = (inputs * rms_scale(inputs) * gain[...]).astype(BF)

    rows = normed[...]
    queries[...] = product(rows, wq[...]).astype(BF)
    pair[0] = product(rows, wk[...]).astype(BF)
    pair[1] = product(rows, wv[...]).astype(BF)


def front(clock, tokens, gain, wq, wk, wv):
    step = 256
    column = pl.BlockSpec((D, step), lambda j, *_: (0, j))
    return clock.run(
        front_kernel,
        (shape((W, D), BF), shape((W, D), BF), shape((2, W, D), BF)),
        (tokens, gain, wq, wk, wv),
        (D // step,),
        [whole((W, D)), whole((1, D)), column, column, column],
        (
            whole((W, D)),
            pl.BlockSpec((W, step), lambda j, *_: (0, j)),
            pl.BlockSpec((2, W, step), lambda j, *_: (0, 0, j)),
        ),
        flops=6 * W * D * D,
        stream=True,
    )


def left_kernel(flags, tokens, gain, wk, wv, pair, normed):
    @pl.when(pl.program_id(0) == 0)
    def _():
        inputs = tokens[...].astype(F32)
        normed[...] = (inputs * rms_scale(inputs) * gain[...]).astype(BF)

    rows = normed[...]
    pair[0] = product(rows, wk[...]).astype(BF)
    pair[1] = product(rows, wv[...]).astype(BF)


def left_pair(clock, tokens, gain, wk, wv):
    step = 256
    column = pl.BlockSpec((D, step), lambda j, *_: (0, j))
    return clock.run(
        left_kernel,
        (shape((2, W, D), BF),),
        (tokens, gain, wk, wv),
        (D // step,),
        [whole((W, D)), whole((1, D)), column, column],
        (pl.BlockSpec((2, W, step), lambda j, *_: (0, 0, j)),),
        [pltpu.VMEM((W, D), BF)],
        flops=LONG,
    )[0]


def summary_probs_of(keys, asks):
    raw = product_nt(keys, asks) * SCALE_LOG2
    expos = jnp.exp2(raw - jnp.max(raw, axis=0, keepdims=True))
    return expos, jnp.sum(expos, axis=0, keepdims=True)


def gates_kernel(
    flags, asks, pair, wu, wg, bias, initial, summary, forget, update, give, own, work
):
    step = pl.program_id(0)

    @pl.when(step < 4)
    def _():
        for head in range(2):
            at = slice(head * HEAD_DIM, (head + 1) * HEAD_DIM)
            expos, total = summary_probs_of(pair[0, :, at], asks[:, at])
            held = product_tn(pair[1, :, at], expos.astype(BF)) / total
            place = pl.multiple_of(step * 256 + head * HEAD_DIM, HEAD_DIM)
            summary[:, pl.ds(place, HEAD_DIM)] = held.T.astype(BF)

    @pl.when(step >= 4)
    def _():
        start = flags[START].astype(F32)
        rows = summary[...]
        fresh = product(rows, wu[...])
        gate = jax.nn.sigmoid(product(rows, wg[...]) + bias[...])
        update[...] = fresh
        forget[...] = gate
        work[0] = (1.0 - start) * gate
        work[1] = start * gate * initial[...] + (1.0 - gate) * fresh
        mine = pl.multiple_of(flags[CORE] * HALF, HALF)
        others = pl.multiple_of((1 - flags[CORE]) * HALF, HALF)
        for part in range(2):
            own[part] = work[part, pl.ds(mine, HALF)].astype(BF)
            give[part] = work[part, pl.ds(others, HALF)].astype(BF)


def gates(clock, asks, pair, state_weight, bias, initial):
    step = 256
    early = lambda i, *_: (0, jnp.minimum(i, 3))
    late = lambda i, *_: (0, jnp.maximum(i - 4, 0))
    late3 = lambda i, *_: (0, 0, jnp.maximum(i - 4, 0))
    return clock.run(
        gates_kernel,
        (
            shape((NS, D), BF),
            shape((NS, D), F32),
            shape((NS, D), F32),
            shape((2, HALF, D), BF),
            shape((2, HALF, D), BF),
        ),
        (asks, pair, state_weight, state_weight, bias, initial),
        (8,),
        [
            pl.BlockSpec((NS, step), early),
            pl.BlockSpec((2, W, step), lambda i, *_: (0, 0, jnp.minimum(i, 3))),
            pl.BlockSpec((D, step), late),
            pl.BlockSpec((D, step), lambda i, *_: (0, jnp.maximum(i - 4, 0) + D // step)),
            pl.BlockSpec((1, step), late),
            pl.BlockSpec((NS, step), late),
        ],
        (
            whole((NS, D)),
            pl.BlockSpec((NS, step), late),
            pl.BlockSpec((NS, step), late),
            pl.BlockSpec((2, HALF, step), late3),
            pl.BlockSpec((2, HALF, step), late3),
        ),
        [pltpu.VMEM((2, NS, step), F32)],
        flops=4 * NS * W * D + 4 * NS * D * D,
    )


def rows_of(chip):
    return pl.ds(pl.multiple_of(chip * QUARTER, QUARTER), QUARTER)


def compose_kernel(flags, own, recv, keep, to1, to2, to3, work):
    odd_core = flags[CORE] == 1
    pick2 = lambda part: (own[part].astype(F32), recv[part].astype(F32))
    (own_scale, recv_scale), (own_base, recv_base) = pick2(0), pick2(1)
    later_scale = jnp.where(odd_core, own_scale, recv_scale)
    earlier_base = jnp.where(odd_core, recv_base, own_base)
    later_base = jnp.where(odd_core, own_base, recv_base)
    work[0] = own_scale * recv_scale
    work[1] = later_scale * earlier_base + later_base
    for far, out in enumerate((keep, to1, to2, to3)):
        out[...] = work[:, rows_of(flags[CHIP] ^ far)].astype(BF)


def prefix_kernel(flags, keep, from1, from2, from3, mine, to1, to2, to3, got, enter):
    for far, came in enumerate((keep, from1, from2, from3)):
        got[flags[CHIP] ^ far] = came[...].astype(F32)
    state = got[0, 1]
    enter[0] = jnp.zeros_like(state)
    enter[1] = state
    for chip in (1, 2):
        state = got[chip, 0] * state + got[chip, 1]
        enter[chip + 1] = state
    for far, out in enumerate((mine, to1, to2, to3)):
        out[...] = enter[flags[CHIP] ^ far].astype(BF)


def previous_kernel(flags, mine, from1, from2, from3, own, recv, keep, give, before):
    for far, came in enumerate((mine, from1, from2, from3)):
        before[rows_of(flags[CHIP] ^ far)] = came[...].astype(F32)
    odd_core = flags[CORE] == 1
    scale = jnp.where(odd_core, recv[0].astype(F32), own[0].astype(F32))
    base = jnp.where(odd_core, recv[1].astype(F32), own[1].astype(F32))
    entry = before[...]
    between = scale * entry + base
    keep[...] = jnp.where(odd_core, between, entry).astype(BF)
    give[...] = jnp.where(odd_core, entry, between).astype(BF)


def compose_back_kernel(flags, own, recv, own_pair, recv_pair, keep, to1, to2, to3, work):
    odd_core = flags[CORE] == 1
    scale = jnp.where(odd_core, recv_pair[0].astype(F32), own_pair[0].astype(F32))
    mine, other = own[...].astype(F32), recv[...].astype(F32)
    work[...] = scale * jnp.where(odd_core, mine, other) + jnp.where(odd_core, other, mine)
    for far, out in enumerate((keep, to1, to2, to3)):
        out[...] = work[rows_of(flags[CHIP] ^ far)].astype(BF)


def suffix_kernel(
    flags, keep, from1, from2, from3, kept0, kept1, kept2, kept3, mine, to1, to2, to3, got, enter
):
    pairs = ((keep, kept0), (from1, kept1), (from2, kept2), (from3, kept3))
    for far, (came, kept) in enumerate(pairs):
        got[flags[CHIP] ^ far, 0] = kept[0].astype(F32)
        got[flags[CHIP] ^ far, 1] = came[...].astype(F32)
    state = got[3, 1]
    enter[3] = jnp.zeros_like(state)
    enter[2] = state
    for chip in (2, 1):
        state = got[chip, 0] * state + got[chip, 1]
        enter[chip - 1] = state
    for far, out in enumerate((mine, to1, to2, to3)):
        out[...] = enter[flags[CHIP] ^ far].astype(BF)


def following_kernel(
    flags, mine, from1, from2, from3, own, recv, own_pair, recv_pair, keep, give, after
):
    for far, came in enumerate((mine, from1, from2, from3)):
        after[rows_of(flags[CHIP] ^ far)] = came[...].astype(F32)
    odd_core = flags[CORE] == 1
    scale = jnp.where(odd_core, own_pair[0].astype(F32), recv_pair[0].astype(F32))
    base = jnp.where(odd_core, own[...].astype(F32), recv[...].astype(F32))
    entry = after[...]
    between = scale * entry + base
    keep[...] = jnp.where(odd_core, entry, between).astype(BF)
    give[...] = jnp.where(odd_core, between, entry).astype(BF)


def small(clock, kernel, outs, args, scratch):
    return clock.run(
        kernel,
        tuple(shape(dims, BF) for dims in outs),
        args,
        (1,),
        [whole(a.shape) for a in args],
        tuple(whole(dims) for dims in outs),
        [pltpu.VMEM(dims, F32) for dims in scratch],
        limit=10,
    )


def to_chips(values):
    return (values[0],) + tuple(
        swapped(value, "seq", 2 * far) for far, value in zip((1, 2, 3), values[1:])
    )


PAIR_WORK = [(4, 2, QUARTER, D), (4, QUARTER, D)]


def compose(clock, own, recv):
    return to_chips(small(clock, compose_kernel, [(2, QUARTER, D)] * 4, (own, recv), [(2, HALF, D)]))


def prefix(clock, got):
    return to_chips(small(clock, prefix_kernel, [(QUARTER, D)] * 4, got, PAIR_WORK))


def previous(clock, back, own, recv):
    mine, other = small(
        clock, previous_kernel, [(HALF, D)] * 2, back + (own, recv), [(HALF, D)]
    )
    return mine, swapped(other, "seq", 1)


def compose_back(clock, *args):
    return to_chips(small(clock, compose_back_kernel, [(QUARTER, D)] * 4, args, [(HALF, D)]))


def suffix(clock, got, kept):
    return to_chips(small(clock, suffix_kernel, [(QUARTER, D)] * 4, got + kept, PAIR_WORK))


def following(clock, back, *args):
    mine, other = small(clock, following_kernel, [(HALF, D)] * 2, back + args, [(HALF, D)])
    return mine, swapped(other, "seq", 1)


def state_kernel(
    flags, mine, other, initial, forget, update, wk, wv, state_in, state_low, state_out, pair
):
    @pl.when(pl.program_id(0) == 0)
    def _():
        start = flags[START].astype(F32)
        for core, came in ((flags[CORE], mine), (1 - flags[CORE], other)):
            rows = pl.ds(pl.multiple_of(core * HALF, HALF), HALF)
            entry = (1.0 - start) * came[...].astype(F32) + start * initial[rows, :]
            gate = forget[rows, :]
            state_in[rows, :] = entry
            state_low[rows, :] = entry.astype(BF)
            state_out[rows, :] = gate * entry + (1.0 - gate) * update[rows, :]

    rows = state_low[...]
    pair[0] = product(rows, wk[...]).astype(BF)
    pair[1] = product(rows, wv[...]).astype(BF)


def state_pair(clock, mine, other, initial, forget, update, wk, wv):
    step = 256
    column = pl.BlockSpec((D, step), lambda j, *_: (0, j))
    return clock.run(
        state_kernel,
        (shape((NS, D), F32), shape((NS, D), BF), shape((NS, D), F32), shape((2, NS, D), BF)),
        (mine, other, initial, forget, update, wk, wv),
        (D // step,),
        [whole((HALF, D))] * 2 + [whole((NS, D))] * 3 + [column, column],
        (
            whole((NS, D)),
            whole((NS, D)),
            whole((NS, D)),
            pl.BlockSpec((2, NS, step), lambda j, *_: (0, 0, j)),
        ),
        flops=4 * NS * D * D,
    )


def masked_scores(flags, queries, left, own, state):
    seen = []
    left_bias = jnp.where(flags[START] == 0, 0.0, NEGATIVE).astype(F32)
    seen.append(product_nt(left[0], queries) * SCALE_LOG2 + left_bias)
    rows = lax.broadcasted_iota(jnp.int32, (W, W), 0)
    cols = lax.broadcasted_iota(jnp.int32, (W, W), 1)
    seen.append(jnp.where(rows <= cols, product_nt(own[0], queries) * SCALE_LOG2, NEGATIVE))
    seen.append(product_nt(state[0], queries) * SCALE_LOG2)
    return seen


PER_STEP = 2


def each_head(*refs):
    for head in range(PER_STEP):
        at = pl.ds(head * HEAD_DIM, HEAD_DIM)
        yield head, [ref.at[..., at] for ref in refs]


def attend_kernel(flags, *refs):
    lse = refs[-1]
    for head, (queries, left, own, state, attended) in each_head(*refs[:-1]):
        seen = masked_scores(flags, queries[...], left, own, state)
        peak = functools.reduce(
            jnp.maximum, [jnp.max(part, axis=0, keepdims=True) for part in seen]
        )
        held = 0.0
        total = 0.0
        for part, pair in zip(seen, (left, own, state)):
            expos = jnp.exp2(part - peak)
            total = total + jnp.sum(expos, axis=0, keepdims=True)
            held = held + product_tn(pair[1], expos.astype(BF))
        attended[...] = (held / total).T.astype(BF)
        lse[head] = peak + jnp.log2(total)


HEADS_WIDE = PER_STEP * HEAD_DIM


def attend(clock, queries, left, own, state):
    head = pl.BlockSpec((W, HEADS_WIDE), lambda h, *_: (0, h))
    pair = pl.BlockSpec((2, W, HEADS_WIDE), lambda h, *_: (0, 0, h))
    return clock.run(
        attend_kernel,
        (shape((W, D), BF), shape((HEADS, 1, W), F32)),
        (queries, left, own, state),
        (HEADS // PER_STEP,),
        [head, pair, pair, pair],
        (head, pl.BlockSpec((PER_STEP, 1, W), lambda h, *_: (h, 0, 0))),
        flops=4 * W * (2 * W + NS) * D,
        stream=True,
        limit=26,
    )


def attend_back_kernel(flags, queries, left, own, state, grad, lse, *outs):
    for head, (asks, left_h, own_h, state_h, grad_h, queries_grad, *grads) in each_head(
        queries, left, own, state, grad, *outs
    ):
        asks, out_grad = asks[...], grad_h[...]
        pairs = (left_h, own_h, state_h)
        seen = masked_scores(flags, asks, *pairs)
        probs = [jnp.exp2(part - lse[head]) for part in seen]
        prob_grads = [product_nt(pair[1], out_grad) for pair in pairs]
        rowdot = sum(
            jnp.sum(prob * prob_grad, axis=0, keepdims=True)
            for prob, prob_grad in zip(probs, prob_grads)
        )
        total = 0.0
        for prob, prob_grad, pair, out in zip(probs, prob_grads, pairs, grads):
            score_grad = (prob * (prob_grad - rowdot)).astype(BF)
            out[0] = (product(score_grad, asks) * SCALE).astype(out.dtype)
            out[1] = product(prob.astype(BF), out_grad).astype(out.dtype)
            total = total + product_tn(pair[0], score_grad)
        queries_grad[...] = (total * SCALE).T.astype(BF)


def attend_back(clock, queries, left, own, state, grad, lse):
    head = pl.BlockSpec((W, HEADS_WIDE), lambda h, *_: (0, h))
    pair = pl.BlockSpec((2, W, HEADS_WIDE), lambda h, *_: (0, 0, h))
    return clock.run(
        attend_back_kernel,
        (shape((W, D), BF), shape((2, W, D), BF), shape((2, W, D), F32), shape((2, NS, D), BF)),
        (queries, left, own, state, grad, lse),
        (HEADS // PER_STEP,),
        [head, pair, pair, pair, head, pl.BlockSpec((PER_STEP, 1, W), lambda h, *_: (h, 0, 0))],
        (head, pair, pair, pair),
        flops=10 * W * (2 * W + NS) * D,
        stream=True,
        limit=36,
    )


def gelu_parts(upper):
    square = upper * upper
    inner = GELU_SCALE * (upper + GELU_CUBIC * square * upper)
    bent = jnp.tanh(inner)
    value = 0.5 * upper * (1.0 + bent)
    slope = 0.5 * (1.0 + bent) + 0.5 * upper * (1.0 - bent * bent) * GELU_SCALE * (
        1.0 + 3.0 * GELU_CUBIC * square
    )
    return value, slope


def mlp_step(normed_mlp, come, up1, up2, down, up, activated, upper_grad, total, grad):
    half = up1.shape[1]
    up[:, :half] = up1[...]
    up[:, half:] = up2[...]
    rows = down[...].reshape(2 * half, D)
    value, slope = gelu_parts(product(normed_mlp[...], up[...]))
    value = value.astype(BF)
    activated[...] = value
    total[...] += product(value, rows)
    back = (come[...].astype(F32) * slope).astype(BF)
    upper_grad[...] = back
    grad[...] += product_nt(back, up[...])


def come_kernel(flags, cotangent, down1, down2, come1, come2):
    for down, come in ((down1, come1), (down2, come2)):
        rows = down[...].reshape(come.shape[1], D)
        come[...] = product_nt(cotangent[...], rows).astype(BF)


def come_back(clock, cotangent, down):
    return clock.run(
        come_kernel,
        (shape((W, FF // 2), BF),) * 2,
        (cotangent, down, down),
        (PAIRS,),
        [fixed((W, D)), mlp_specs(0)[2], mlp_specs(1)[2]],
        (mlp_halves(),) * 2,
        flops=2 * W * D * FF,
    )


def mlp_first_kernel(
    flags,
    attended,
    tokens,
    out_weight,
    gain,
    come,
    up1,
    up2,
    down,
    activated,
    upper_grad,
    normed_mlp,
    hidden,
    total,
    grad,
    up,
):
    @pl.when(pl.program_id(0) == 0)
    def _():
        field = tokens[...].astype(F32) + product(attended[...], out_weight[...])
        hidden[...] = field
        normed_mlp[...] = (field * rms_scale(field) * gain[...]).astype(BF)
        total[...] = field
        grad[...] = jnp.zeros_like(field)

    mlp_step(normed_mlp, come, up1, up2, down, up, activated, upper_grad, total, grad)


def mlp_second_kernel(
    flags,
    normed_mlp,
    hidden,
    total_in,
    grad_in,
    out_weight,
    gain,
    cotangent,
    come,
    up1,
    up2,
    down,
    activated,
    upper_grad,
    mixed,
    hidden_grad,
    attended_grad,
    heads_grad,
    gain_grad,
    total,
    grad,
    up,
):
    step = pl.program_id(0)

    @pl.when(step == 0)
    def _():
        total[...] = total_in[...]
        grad[...] = grad_in[...]

    mlp_step(normed_mlp, come, up1, up2, down, up, activated, upper_grad, total, grad)

    @pl.when(step == pl.num_programs(0) - 1)
    def _():
        mixed[...] = total[...].astype(BF)
        field = hidden[...]
        scaled = rms_scale(field)
        gain_grad[...] = jnp.sum(grad[...] * field * scaled, axis=0, keepdims=True)
        weighted = grad[...] * gain[...]
        field_grad = (
            cotangent[...].astype(F32)
            + scaled * weighted
            - field
            * (scaled * scaled * scaled * jnp.mean(weighted * field, axis=-1, keepdims=True))
        )
        hidden_grad[...] = field_grad
        low = field_grad.astype(BF)
        attended_grad[...] = low
        heads_grad[...] = product_nt(low, out_weight[...]).astype(BF)


PIECE = 256
PAIRS = FF // (4 * PIECE)


def mlp_specs(part):
    return [
        pl.BlockSpec((D, PIECE), lambda j, *_: (0, 4 * j + part)),
        pl.BlockSpec((D, PIECE), lambda j, *_: (0, 4 * j + 2 + part)),
        pl.BlockSpec((2, PIECE, D), lambda j, *_: (j, part, 0)),
    ]


def mlp_halves():
    return pl.BlockSpec((W, 2 * PIECE), lambda j, *_: (0, j))


def mlp_first(clock, attended, tokens, out_weight, gain, come, up, down):
    rows = whole((W, D))
    return clock.run(
        mlp_first_kernel,
        (
            shape((W, FF // 2), BF),
            shape((W, FF // 2), BF),
            shape((W, D), BF),
            shape((W, D), F32),
            shape((W, D), F32),
            shape((W, D), F32),
        ),
        (attended, tokens, out_weight, gain, come, up, up, down),
        (PAIRS,),
        [fixed((W, D)), fixed((W, D)), fixed((D, D)), fixed((1, D)), mlp_halves()] + mlp_specs(0),
        (mlp_halves(), mlp_halves(), rows, rows, rows, rows),
        [pltpu.VMEM((D, 2 * PIECE), BF)],
        flops=3 * W * D * FF + 2 * W * D * D,
        limit=36,
    )


def mlp_second(
    clock, normed_mlp, hidden, total, grad, out_weight, gain, cotangent, come, up, down
):
    rows = whole((W, D))
    return clock.run(
        mlp_second_kernel,
        (
            shape((W, FF // 2), BF),
            shape((W, FF // 2), BF),
            shape((W, D), BF),
            shape((W, D), F32),
            shape((W, D), BF),
            shape((W, D), BF),
            shape((1, D), F32),
        ),
        (normed_mlp, hidden, total, grad, out_weight, gain, cotangent, come, up, up, down),
        (PAIRS,),
        [fixed((W, D))] * 4
        + [fixed((D, D)), fixed((1, D)), fixed((W, D)), mlp_halves()]
        + mlp_specs(1),
        (mlp_halves(), mlp_halves(), rows, rows, rows, rows, whole((1, D))),
        [pltpu.VMEM((W, D), F32), pltpu.VMEM((W, D), F32), pltpu.VMEM((D, 2 * PIECE), BF)],
        flops=3 * W * D * FF + 2 * W * D * D,
        limit=36,
    )


def direct_kernel(flags, state_grad, wk, wv, forget, cotangent, direct, own, give, work):
    grad = product_nt(state_grad[0], wk[...]) + product_nt(state_grad[1], wv[...])
    direct[...] = grad
    keep = 1.0 - flags[START].astype(F32)
    work[...] = keep * (forget[...] * cotangent[...] + grad)
    own[...] = work[pl.ds(pl.multiple_of(flags[CORE] * HALF, HALF), HALF)].astype(BF)
    give[...] = work[pl.ds(pl.multiple_of((1 - flags[CORE]) * HALF, HALF), HALF)].astype(BF)


def direct_grad(clock, state_grad, wk, wv, forget, cotangent):
    step = 256
    row = pl.BlockSpec((step, D), lambda j, *_: (j, 0))
    column = pl.BlockSpec((NS, step), lambda j, *_: (0, j))
    half = pl.BlockSpec((HALF, step), lambda j, *_: (0, j))
    return clock.run(
        direct_kernel,
        (shape((NS, D), F32), shape((HALF, D), BF), shape((HALF, D), BF)),
        (state_grad, wk, wv, forget, cotangent),
        (D // step,),
        [whole((2, NS, D)), row, row, column, column],
        (column, half, half),
        [pltpu.VMEM((NS, step), F32)],
        flops=4 * NS * D * D,
    )


def state_back_kernel(
    flags,
    mine,
    other,
    cotangent,
    forget,
    update,
    state_in,
    direct,
    wu,
    wg,
    initial_grad,
    projected_grad,
    bias_grad,
    summary_grad,
    work,
    total,
):
    step = pl.program_id(0)
    for core, came in ((flags[CORE], mine), (1 - flags[CORE], other)):
        work[pl.ds(pl.multiple_of(core * HALF, HALF), HALF)] = came[...].astype(F32)
    out_grad = cotangent[...] + work[...]
    gate = forget[...]
    start = flags[START].astype(F32)
    initial_grad[...] = (start * (gate * out_grad + direct[...])).astype(BF)
    rest = 1.0 - gate
    gate_grad = out_grad * (state_in[...] - update[...]) * gate * rest
    bias_grad[...] = jnp.sum(gate_grad, axis=0, keepdims=True)
    fresh_grad = (out_grad * rest).astype(BF)
    gate_low = gate_grad.astype(BF)
    projected_grad[0] = fresh_grad
    projected_grad[1] = gate_low
    part = product_nt(fresh_grad, wu[...]) + product_nt(gate_low, wg[...])

    @pl.when(step == 0)
    def _():
        total[...] = part

    @pl.when(step > 0)
    def _():
        total[...] += part

    @pl.when(step == pl.num_programs(0) - 1)
    def _():
        summary_grad[...] = total[...].astype(BF)


def state_back(clock, mine, other, cotangent, forget, update, state_in, direct, state_weight):
    step = 256
    column = pl.BlockSpec((NS, step), lambda j, *_: (0, j))
    half = pl.BlockSpec((HALF, step), lambda j, *_: (0, j))
    return clock.run(
        state_back_kernel,
        (
            shape((NS, D), BF),
            shape((2, NS, D), BF),
            shape((1, D), F32),
            shape((NS, D), BF),
        ),
        (mine, other, cotangent, forget, update, state_in, direct, state_weight, state_weight),
        (D // step,),
        [half, half, column, column, column, column, column]
        + [
            pl.BlockSpec((D, step), lambda j, *_: (0, j)),
            pl.BlockSpec((D, step), lambda j, *_: (0, j + D // step)),
        ],
        (
            column,
            pl.BlockSpec((2, NS, step), lambda j, *_: (0, 0, j)),
            pl.BlockSpec((1, step), lambda j, *_: (0, j)),
            whole((NS, D)),
        ),
        [pltpu.VMEM((NS, step), F32), pltpu.VMEM((NS, D), F32)],
        flops=4 * NS * D * D,
    )


def summary_back_kernel(flags, *refs):
    for _, (asks, pair, grad, own_grad, asks_grad, pair_total) in each_head(*refs):
        queries, out_grad = asks[...], grad[...]
        expos, total = summary_probs_of(pair[0], queries)
        probs = expos * (1.0 / total)
        prob_grad = product_nt(pair[1], out_grad)
        rowdot = jnp.sum(probs * prob_grad, axis=0, keepdims=True)
        score_grad = (probs * (prob_grad - rowdot)).astype(BF)
        asks_grad[...] = (product_tn(pair[0], score_grad) * SCALE).T.astype(BF)
        pair_total[0] = (own_grad[0] + product(score_grad, queries) * SCALE).astype(BF)
        pair_total[1] = (own_grad[1] + product(probs.astype(BF), out_grad)).astype(BF)


def summary_back(clock, asks, pair, grad, own_grad):
    head = pl.BlockSpec((W, HEADS_WIDE), lambda h, *_: (0, h))
    both = pl.BlockSpec((2, W, HEADS_WIDE), lambda h, *_: (0, 0, h))
    return clock.run(
        summary_back_kernel,
        (shape((NS, D), BF), shape((2, W, D), BF)),
        (asks, pair, grad, own_grad),
        (HEADS // PER_STEP,),
        [head, both, head, both],
        (head, both),
        flops=10 * NS * W * D,
        stream=True,
    )


def tokens_back_kernel(
    flags,
    queries_grad,
    pair_total,
    returned,
    wq,
    wk,
    wv,
    tokens,
    gain,
    hidden_grad,
    tokens_grad,
    gain_grad,
    total,
):
    step = pl.program_id(0)

    @pl.when(step < 2)
    def _():
        part = product_nt(queries_grad[...], wq[...])
        total[...] = jnp.where(step == 0, part, total[...] + part)

    @pl.when((step >= 2) & (step < 4))
    def _():
        total[...] += product_nt(add_low(pair_total[0], returned[0]), wk[...])

    @pl.when(step >= 4)
    def _():
        total[...] += product_nt(add_low(pair_total[0], returned[0]), wv[...])

    @pl.when(step == 5)
    def _():
        inputs = tokens[...].astype(F32)
        scaled = rms_scale(inputs)
        grad = total[...]
        gain_grad[...] = jnp.sum(grad * inputs * scaled, axis=0, keepdims=True)
        weighted = grad * gain[...]
        tokens_grad[...] = (
            hidden_grad[...]
            + scaled * weighted
            - inputs
            * (scaled * scaled * scaled * jnp.mean(weighted * inputs, axis=-1, keepdims=True))
        )


def tokens_back(clock, queries_grad, pair_total, returned, wq, wk, wv, tokens, gain, hidden_grad):
    step = D // 2
    clamp = lambda i, low: jnp.clip(i - low, 0, 1)
    weight = lambda low: pl.BlockSpec((D, step), lambda i, *_: (0, clamp(i, low)))
    later = lambda i: jnp.maximum(i - 2, 0)
    pair = pl.BlockSpec((1, W, step), lambda i, *_: (later(i) // 2, 0, later(i) % 2))
    return clock.run(
        tokens_back_kernel,
        (shape((W, D), F32), shape((1, D), F32)),
        (queries_grad, pair_total, returned, wq, wk, wv, tokens, gain, hidden_grad),
        (6,),
        [
            pl.BlockSpec((W, step), lambda i, *_: (0, clamp(i, 0))),
            pair,
            pair,
            weight(0),
            weight(2),
            weight(4),
            fixed((W, D)),
            fixed((1, D)),
            fixed((W, D)),
        ],
        (whole((W, D)), whole((1, D))),
        [pltpu.VMEM((W, D), F32)],
        flops=6 * W * D * D,
    )


def chunk_natural(flags, place):
    return place


def chunk_along_x(flags, place):
    x = flags[CHIP] & 1
    return 2 * (place % 2) + (1 - x if place < 2 else x)


def chunk_along_y(flags, place):
    y = flags[CHIP] >> 1
    return 2 * (1 - y if place < 2 else y) + place % 2


def column_blocks(terms):
    return terms[0][1][0][0].shape[2] // D


def weight_kernel(plan, merge, flags, *refs):
    refs = list(refs)
    lefts = [refs.pop(0) for _ in range(plan["lefts"])]
    rights = [[refs.pop(0) for _ in adds] for adds in plan["rights"]]
    extras = [refs.pop(0) for _ in range(plan["extras"])]
    recv = refs.pop(0) if merge else None
    work = refs.pop()
    core = flags[CORE] if merge else 1 - flags[CORE]
    step, base, start = pl.program_id(0), 0, 0

    def write(along, place, at, here, part):
        rows = part.shape[0]
        if merge:
            chunk = (chunk_along_x, chunk_along_y)[along](flags, place)
            part = part.astype(F32) + recv[chunk, at : at + rows].astype(F32)
            refs[2 * along + place // 2][place % 2, here : here + rows] = part.astype(BF)
        else:
            refs[0][place, at : at + rows] = part.astype(BF)

    def source(along, place):
        chunk_of = (chunk_along_x, chunk_along_y)[along] if merge else chunk_natural
        return 2 * chunk_of(flags, place) + core

    for along, group in enumerate(plan["grads"]):
        here = 0
        for rows, blocks, terms in group:

            @pl.when(step == base)
            def _():
                for term, (left, _) in enumerate(terms):
                    for place in range(4):
                        first = pl.multiple_of(source(along, place) * rows, rows)
                        block = lefts[left][:, pl.ds(first, rows)]
                        work[term, place * rows : (place + 1) * rows] = block.T

            for block in range(blocks):

                @pl.when(step == base + block)
                def _():
                    total = 0.0
                    for term, (_, right) in enumerate(terms):
                        parts = [part[0] for part in rights[right]]
                        value = parts[0] if len(parts) == 1 else add_low(*parts)
                        total = total + product(work[term, : 4 * rows], value)
                    at = block * rows
                    for place in range(4):
                        part = total[place * rows : (place + 1) * rows]
                        write(along, place, start + at, here + at, part)

            base += blocks
            start += blocks * rows
            here += blocks * rows
        if extras:
            rows = extras[along].shape[0] // 8

            @pl.when(step == 0)
            def _():
                for place in range(4):
                    first = pl.multiple_of(source(along, place) * rows, rows)
                    write(along, place, start, here, extras[along][pl.ds(first, rows)])

            start += rows


def weight_pair(clock, grads, extras, recv):
    lefts, left_ids, rights, args, specs, plans = [], {}, [], [], [], []
    base, start, tokens, most = 0, 0, grads[0][0][0][0].shape[0], 0
    sizes = []
    for along, group in enumerate(grads):
        total, plan = 0, []
        for terms in group:
            rows, blocks = terms[0][0].shape[1] // 8, column_blocks(terms)
            most = max(most, rows)
            steps = []
            for left, adds in terms:
                if id(left) not in left_ids:
                    left_ids[id(left)] = len(lefts)
                    lefts.append(left)
                steps.append((left_ids[id(left)], len(rights)))
                rights.append(tuple(index for _, index in adds))
                for right, index in adds:
                    args.append(right)
                    specs.append(
                        pl.BlockSpec(
                            (1, tokens, D),
                            lambda j, *_, index=index, base=base, blocks=blocks: (
                                index,
                                0,
                                jnp.clip(j - base, 0, blocks - 1),
                            ),
                        )
                    )
            plan.append((rows, blocks, steps))
            base += blocks
            total += blocks * rows
        if extras:
            total += extras[along].shape[0] // 8
        plans.append(plan)
        sizes.append(total)
        start += total
    args = lefts + args + list(extras)
    specs = [fixed(left.shape) for left in lefts] + specs + [fixed(e.shape) for e in extras]
    merge = recv is not None
    if merge:
        args.append(recv)
        specs.append(fixed(recv.shape))
        dims = [(2, total, D) for total in sizes for _ in range(2)]
    else:
        dims = [(4, start, D)]
    plan = {"lefts": len(lefts), "rights": rights, "extras": len(extras), "grads": plans}
    return clock.run(
        functools.partial(weight_kernel, plan, merge),
        tuple(shape(d, BF) for d in dims),
        tuple(args),
        (base,),
        specs,
        tuple(whole(d) for d in dims),
        [pltpu.VMEM((len(grads[0][0]), 4 * most, tokens), BF)],
        flops=2 * tokens * 4 * start * D * len(grads[0][0]),
        limit=24,
    )


def scatter_bits(value, bits, names):
    place = lax.axis_index("seq")
    names = list(names)
    for bit in bits:
        at = names.index(bit)
        mine = (place >> bit) & 1
        recv = swapped(pick(value, 1 - mine, at), "seq", 1 << bit)
        value = add_low(pick(value, mine, at), recv)
        names.pop(at)
    return value


def whole_scatter(value, along_x):
    count = lax.axis_size("seq")
    levels = count.bit_length() - 1
    names = list(range(levels - 1, -1, -1))
    value = value.reshape((2,) * levels + (value.shape[0] // count,) + value.shape[1:])
    bits = [0] + (names[-2::-1] if along_x else names[:-1])
    return scatter_bits(value, bits, names)


def in_rows(value):
    return jnp.concatenate([value[:, at : at + D] for at in range(0, value.shape[1], D)], axis=0)


def turn_kernel(flags, kept1, recv1, kept2, recv2, send1, send2):
    send1[...] = add_low(kept1[0], recv1[0])
    send2[...] = add_low(kept2[0], recv2[0])


def pack_kernel(flags, *refs):
    out, start = refs[-1], 0
    for at in range(0, len(refs) - 1, 3):
        kept, recv, last = refs[at : at + 3]
        rows = last.shape[0]
        out[start : start + rows] = add_low(kept[0], recv[0], last[...])
        start += rows


class Scatter:
    def __init__(self, clock, firsts, seconds, extras=()):
        self.grads, self.extras, self.plain = (firsts, seconds), extras, None
        if lax.axis_size("seq") != 8:
            sums = []
            for number, group in enumerate(self.grads):
                for terms in group:
                    total = 0.0
                    for left, adds in terms:
                        parts = [right[index] for right, index in adds]
                        right = add_low(*parts) if len(parts) > 1 else parts[0]
                        total = total + product_tn(left, right)
                    sums.append(in_rows(whole_scatter(total.astype(BF), number == 0)))
                if extras:
                    sums.append(whole_scatter(extras[number], number == 0))
            self.plain = jnp.concatenate(sums, axis=0)
            return
        (self.give,) = weight_pair(clock, self.grads, self.extras, None)

    def core(self, clock):
        if self.plain is None:
            self.recv = swapped(clock.at(self.give), "seq", 1)

    def keep(self, clock):
        if self.plain is None:
            send1, kept1, send2, kept2 = weight_pair(clock, self.grads, self.extras, self.recv)
            self.kept, self.send = (kept1, kept2), (send1, send2)

    def near(self, clock):
        if self.plain is None:
            self.recv = tuple(
                swapped(clock.at(send), "seq", far) for send, far in zip(self.send, (2, 4))
            )

    def held(self, other):
        args, specs = [], []
        for number, (kept, recv) in enumerate(zip(self.kept, self.recv)):
            bit = 1 - number
            mine = lambda i, flags, bit=bit: (((flags[CHIP] >> bit) & 1) ^ other, 0, 0)
            args.append([kept, recv])
            specs.append([pl.BlockSpec((1,) + kept.shape[1:], mine)] * 2)
        return args, specs

    def turn(self, clock, flops=0):
        if self.plain is None:
            args, specs = self.held(1)
            dims = [kept.shape[1:] for kept in self.kept]
            self.send = clock.run(
                turn_kernel,
                tuple(shape(d, BF) for d in dims),
                tuple(args[0] + args[1]),
                (1,),
                specs[0] + specs[1],
                tuple(whole(d) for d in dims),
                flops=flops,
                limit=10,
            )

    def far(self, clock):
        if self.plain is None:
            self.last = tuple(
                swapped(clock.at(send), "seq", far) for send, far in zip(self.send, (4, 2))
            )

    def parts(self):
        args, specs = self.held(0)
        for number, last in enumerate(self.last):
            args[number].append(last)
            specs[number].append(whole(last.shape))
        return args[0] + args[1], specs[0] + specs[1]


def pack(clock, *scatters):
    if scatters[0].plain is not None:
        return jnp.concatenate([scatter.plain for scatter in scatters], axis=0)
    args, specs = [], []
    for scatter in scatters:
        more = scatter.parts()
        args += more[0]
        specs += more[1]
    total = sum(arg.shape[0] for arg in args[2::3])
    return clock.run(
        pack_kernel,
        (shape((total, D), BF),),
        tuple(args),
        (1,),
        specs,
        (whole((total, D)),),
        limit=16,
    )[0]


class Line:
    def __init__(self, clock, value):
        count = lax.axis_size("dp")
        half = count // 2
        self.value = value
        self.rounds = (
            [([(s, s + 1), (count - 1 - s, count - 2 - s)], None) for s in range(half - 1)]
            + [([(half - 1, half), (half, half - 1)], None)]
            + [
                ([(s + 1, s), (count - 2 - s, count - 1 - s)], (s, count - 1 - s))
                for s in range(half - 2, -1, -1)
            ]
        )
        self.send(clock)

    def send(self, clock):
        self.recv = lax.ppermute(clock.at(self.value), "dp", self.rounds[0][0])

    def take(self, clock):
        place = lax.axis_index("dp")
        takers = self.rounds.pop(0)[1]
        value = clock.at(self.value)
        if takers is None:
            self.value = add_low(value, self.recv)
        else:
            outer = (place == takers[0]) | (place == takers[1])
            self.value = jnp.where(outer, self.recv, value)
        if self.rounds:
            clock.after(self.value)

    def step(self, clock):
        self.take(clock)
        if self.rounds:
            self.send(clock)

    def finish(self, clock):
        while self.rounds:
            self.step(clock)
        return self.value.astype(F32)


def interleaved(first, second):
    blocks = []
    for at in range(0, first.shape[1], PIECE):
        blocks += [first[:, at : at + PIECE], second[:, at : at + PIECE]]
    return jnp.concatenate(blocks, axis=1)


def body(
    tokens,
    item_starts,
    attn_gain,
    query_weight,
    key_weight,
    value_weight,
    output_weight,
    state_queries,
    state_weight,
    gate_bias,
    initial_state,
    mlp_gain,
    up_weight,
    down_weight,
    out_cotangent,
    state_cotangent,
):
    count = lax.axis_size("seq")
    place = lax.axis_index("seq")
    clock = Clock(
        jnp.stack([item_starts[0, 0], place & 1, (place >> 1) & 3]).astype(jnp.int32)
    )
    tokens, cotangent, state_cot = tokens[0], out_cotangent[0], state_cotangent[0, 0]
    attn_gain, gate_bias, mlp_gain = attn_gain[None], gate_bias[None], mlp_gain[None]
    down_weight = down_weight.reshape(FF // (2 * PIECE), 2 * PIECE, D)

    tokens_left = shifted(tokens, "seq", 1)
    normed, queries, own = front(clock, tokens, attn_gain, query_weight, key_weight, value_weight)
    summary, forget, update, give_pair, own_pair = gates(
        clock, state_queries, own, state_weight, gate_bias, initial_state
    )
    recv_pair = swapped(give_pair, "seq", 1)
    left = left_pair(clock, tokens_left, attn_gain, key_weight, value_weight)
    kept_chips = compose(clock, own_pair, recv_pair)
    come1, come2 = come_back(clock, cotangent, down_weight)
    back = prefix(clock, kept_chips)
    mine, other = previous(clock, back, own_pair, recv_pair)
    state_in, state_low, state_out, state = state_pair(
        clock, mine, other, initial_state, forget, update, key_weight, value_weight
    )
    attended, lse = attend(clock, queries, left, own, state)
    split = count == 8
    activated1, upper_grad1, normed_mlp, hidden, total, grad = mlp_first(
        clock, attended, tokens, output_weight, mlp_gain, come1, up_weight, down_weight
    )
    out_grads = (cotangent[None], 0)
    if split:
        feed1 = Scatter(
            clock,
            [[(activated1, [out_grads])]],
            [[(normed_mlp, [(upper_grad1[None], 0)])]],
        )
        feed1.core(clock)
        feed1.keep(clock)
        feed1.near(clock)
    activated2, upper_grad2, mixed, hidden_grad, attended_grad, heads_grad, mlp_gain_grad = (
        mlp_second(
            clock,
            normed_mlp,
            hidden,
            total,
            grad,
            output_weight,
            mlp_gain,
            cotangent,
            come2,
            up_weight,
            down_weight,
        )
    )
    if split:
        feed2 = Scatter(
            clock,
            [[(activated2, [out_grads])]],
            [[(normed_mlp, [(upper_grad2[None], 0)])]],
        )
        feed2.core(clock)
        feed1.turn(clock, LONG)
        feed1.far(clock)
        feed2.keep(clock)
        feed2.near(clock)
    else:
        feed1 = Scatter(
            clock,
            [[(interleaved(activated1, activated2), [out_grads])]],
            [[(normed_mlp, [(interleaved(upper_grad1, upper_grad2)[None], 0)])]],
        )
    queries_grad, left_grad, own_grad, state_grad = attend_back(
        clock, queries, left, own, state, heads_grad, lse
    )
    direct, own_base, give_base = direct_grad(
        clock, state_grad, key_weight, value_weight, forget, state_cot
    )
    recv_base = swapped(give_base, "seq", 1)
    line1 = Line(clock, pack(clock, feed1))
    got = compose_back(clock, own_base, recv_base, own_pair, recv_pair)
    if split:
        feed2.turn(clock)
    back = suffix(clock, got, kept_chips)
    mine, other = following(clock, back, own_base, recv_base, own_pair, recv_pair)
    if split:
        feed2.far(clock)
    returned = shifted(clock.at(left_grad), "seq", -1)
    line1.step(clock)
    initial_grad, projected_grad, gate_bias_grad, summary_grad = state_back(
        clock, mine, other, state_cot, forget, update, state_in, direct, state_weight
    )
    others = Scatter(
        clock,
        [[(attended, [(attended_grad[None], 0)])], [(summary, [(projected_grad, 0)])]],
        [[(normed, [(queries_grad[None], 0)])], [(summary, [(projected_grad, 1)])]],
    )
    line2 = Line(clock, pack(clock, feed2)) if split else None
    others.core(clock)
    state_queries_grad, pair_total = summary_back(
        clock, state_queries, own, summary_grad, own_grad
    )
    others.keep(clock)
    if split:
        line2.step(clock)
    others.near(clock)
    line1.take(clock)
    keys_values = Scatter(
        clock,
        [[(normed, [(pair_total, 0), (returned, 0)]), (state_low, [(state_grad, 0)])]],
        [[(normed, [(pair_total, 1), (returned, 1)]), (state_low, [(state_grad, 1)])]],
        (state_queries_grad, initial_grad),
    )
    keys_values.core(clock)
    if line1.rounds:
        line1.send(clock)
    keys_values.keep(clock)
    if split:
        line2.take(clock)
    keys_values.near(clock)
    tokens_grad, attn_gain_grad = tokens_back(
        clock,
        queries_grad,
        pair_total,
        returned,
        query_weight,
        key_weight,
        value_weight,
        tokens,
        attn_gain,
        hidden_grad,
    )
    others.turn(clock)
    others.far(clock)
    line1 = line1.finish(clock)
    clock.after(line1)
    lanes, rows = D // count, NS // count
    vectors = jnp.concatenate([attn_gain_grad, gate_bias_grad, mlp_gain_grad])
    vectors = vectors.reshape(3, count, lanes).transpose(1, 0, 2).reshape(count, 1, 3 * lanes)
    vectors = jnp.pad(vectors, ((0, 0), (0, 7), (0, D - 3 * lanes))).astype(BF)
    keys_values.turn(clock)
    keys_values.far(clock)
    vectors = whole_scatter(clock.at(vectors.reshape(-1, D)), True)
    line3 = [Line(clock, half) for half in jnp.split(pack(clock, others), 2)]
    if split:
        line2.send(clock)
    line4 = Line(clock, jnp.concatenate([pack(clock, keys_values), vectors], axis=0))
    for line in line3 + [line4] + line3 + [line4]:
        line.step(clock)
    line3 = [line.finish(clock) for line in line3]
    line4 = line4.finish(clock)
    clock.after(line3, line4)
    line2 = line2.finish(clock) if split else None

    def unpack(packed, *dims):
        pieces, start = [], 0
        for high, wide in dims:
            parts = [
                packed[start + high * part : start + high * (part + 1)] for part in range(wide // D)
            ]
            start += high * (wide // D)
            pieces.append(parts[0] if len(parts) == 1 else jnp.concatenate(parts, axis=1))
        return pieces

    high, deep = D // count, FF // count
    if split:
        down1, up1 = unpack(line1, (deep // 2, D), (high, FF // 2))
        down2, up2 = unpack(line2, (deep // 2, D), (high, FF // 2))
        down_grad = jnp.concatenate([down1, down2], axis=0)
        up_grad = interleaved(up1, up2)
    else:
        down_grad, up_grad = unpack(line1, (deep, D), (high, FF))
    output_grad, first_grad, query_grad, second_grad = unpack(
        jnp.concatenate(line3),
        (high, D),
        (high, D),
        (high, D),
        (high, D),
    )
    state_weight_grad = jnp.concatenate([first_grad, second_grad], axis=1)
    key_grad, state_queries_grad, value_grad, initial_grad, vectors = unpack(
        line4, (high, D), (rows, D), (high, D), (rows, D), (8, D)
    )
    vectors = vectors[0, : 3 * lanes]
    return (
        mixed[None],
        state_out[None, None],
        tokens_grad[None],
        vectors[:lanes],
        query_grad,
        key_grad,
        value_grad,
        output_grad,
        state_queries_grad,
        state_weight_grad,
        vectors[lanes : 2 * lanes],
        initial_grad,
        vectors[2 * lanes :],
        up_grad,
        down_grad,
    )


def solution(mesh):
    in_specs = (
        P("dp", "seq", None),
        P("dp", "seq"),
        P(),
        P(),
        P(),
        P(),
        P(),
        P(),
        P(),
        P(),
        P(),
        P(),
        P(),
        P(),
        P("dp", "seq", None),
        P("dp", "seq", None, None),
    )
    out_specs = (
        P("dp", "seq", None),
        P("dp", "seq", None, None),
        P("dp", "seq", None),
        P("seq"),
        P("seq", None),
        P("seq", None),
        P("seq", None),
        P("seq", None),
        P("seq", None),
        P("seq", None),
        P("seq"),
        P("seq", None),
        P("seq"),
        P("seq", None),
        P("seq", None),
    )
    return jax.shard_map(body, mesh=mesh, in_specs=in_specs, out_specs=out_specs, check_vma=False)
```

```python
import functools
import math

import jax
import jax.numpy as jnp
from jax import lax
from jax.experimental import pallas as pl
from jax.experimental.pallas import tpu as pltpu
from jax.sharding import PartitionSpec as P

D = 1024
HEADS = 8
HEAD_DIM = 128
FF = 4096
W = 512
NS = 512
HALF = NS // 2
QUARTER = NS // 8

EPSILON = 1e-06
NEGATIVE = -1e30
GELU_SCALE = 0.7978845608028654
GELU_CUBIC = 0.044715
SCALE = 1.0 / math.sqrt(HEAD_DIM)
SCALE_LOG2 = SCALE * math.log2(math.e)

BF = jnp.bfloat16
F32 = jnp.float32
MIB = 1 << 20
LONG = 1e11


def swapped(value, axis, distance):
    count = lax.axis_size(axis)
    return lax.ppermute(value, axis, [(place, place ^ distance) for place in range(count)])


def shifted(value, axis, steps):
    count = lax.axis_size(axis)
    first, last = (max(0, -steps), min(count, count - steps))
    return lax.ppermute(value, axis, [(source, source + steps) for source in range(first, last)])


def add_low(*terms):
    total = terms[0].astype(F32)
    for term in terms[1:]:
        total = total + term.astype(F32)
    return total.astype(BF)


def pick(value, index, axis):
    return lax.dynamic_index_in_dim(value, index, axis, False)


def product(left, right):
    return jnp.dot(left, right, preferred_element_type=F32)


def product_tn(left, right):
    return lax.dot_general(left, right, (((0,), (0,)), ((), ())), preferred_element_type=F32)


def product_nt(left, right):
    return lax.dot_general(left, right, (((1,), (1,)), ((), ())), preferred_element_type=F32)


def rms_scale(field):
    return lax.rsqrt(jnp.mean(field * field, axis=-1, keepdims=True) + EPSILON)


def shape(dims, dtype):
    return jax.ShapeDtypeStruct(dims, dtype)


def whole(dims):
    return pl.BlockSpec(dims, lambda *_: (0,) * len(dims))


def fixed(dims):
    return pl.BlockSpec(dims, lambda *_: (0,) * len(dims), pipeline_mode=pl.Buffered(1))


class Clock:
    def __init__(self, flags):
        self.flags = flags

    def after(self, *values):
        self.flags = lax.optimization_barrier((self.flags, values))[0]

    def at(self, value):
        return lax.optimization_barrier((value, self.flags))[0]

    def run(self, kernel, outs, args, grid, in_specs, out_specs, scratch=(), flops=0, limit=20, stream=False):
        nbytes = sum(math.prod(a.shape) * a.dtype.itemsize for a in args) + sum(
            math.prod(o.shape) * o.dtype.itemsize for o in outs
        )
        args = [
            pltpu.with_memory_space_constraint(arg, pltpu.HBM)
            if stream and spec.block_shape != arg.shape
            else arg
            for arg, spec in zip(args, in_specs)
        ]
        results = pl.pallas_call(
            kernel,
            out_shape=outs,
            grid_spec=pltpu.PrefetchScalarGridSpec(
                num_scalar_prefetch=1,
                grid=grid,
                in_specs=in_specs,
                out_specs=out_specs,
                scratch_shapes=list(scratch),
            ),
            compiler_params=pltpu.CompilerParams(
                dimension_semantics=("arbitrary",) * len(grid), vmem_limit_bytes=limit * MIB
            ),
            cost_estimate=pl.CostEstimate(
                flops=int(flops), bytes_accessed=int(nbytes), transcendentals=0
            ),
        )(self.flags, *args)
        self.after(results[0])
        return results


START, CORE, CHIP = 0, 1, 2


def front_kernel(flags, tokens, gain, wq, wk, wv, normed, queries, pair):
    @pl.when(pl.program_id(0) == 0)
    def _():
        inputs = tokens[...].astype(F32)
        normed[...] = (inputs * rms_scale(inputs) * gain[...]).astype(BF)

    rows = normed[...]
    queries[...] = product(rows, wq[...]).astype(BF)
    pair[0] = product(rows, wk[...]).astype(BF)
    pair[1] = product(rows, wv[...]).astype(BF)


def front(clock, tokens, gain, wq, wk, wv):
    step = 256
    column = pl.BlockSpec((D, step), lambda j, *_: (0, j))
    return clock.run(
        front_kernel,
        (shape((W, D), BF), shape((W, D), BF), shape((2, W, D), BF)),
        (tokens, gain, wq, wk, wv),
        (D // step,),
        [whole((W, D)), whole((1, D)), column, column, column],
        (
            whole((W, D)),
            pl.BlockSpec((W, step), lambda j, *_: (0, j)),
            pl.BlockSpec((2, W, step), lambda j, *_: (0, 0, j)),
        ),
        flops=6 * W * D * D,
        stream=True,
    )


def left_kernel(flags, tokens, gain, wk, wv, pair, normed):
    @pl.when(pl.program_id(0) == 0)
    def _():
        inputs = tokens[...].astype(F32)
        normed[...] = (inputs * rms_scale(inputs) * gain[...]).astype(BF)

    rows = normed[...]
    pair[0] = product(rows, wk[...]).astype(BF)
    pair[1] = product(rows, wv[...]).astype(BF)


def left_pair(clock, tokens, gain, wk, wv):
    step = 256
    column = pl.BlockSpec((D, step), lambda j, *_: (0, j))
    return clock.run(
        left_kernel,
        (shape((2, W, D), BF),),
        (tokens, gain, wk, wv),
        (D // step,),
        [whole((W, D)), whole((1, D)), column, column],
        (pl.BlockSpec((2, W, step), lambda j, *_: (0, 0, j)),),
        [pltpu.VMEM((W, D), BF)],
        flops=LONG,
    )[0]


def summary_probs_of(keys, asks):
    raw = product_nt(keys, asks) * SCALE_LOG2
    expos = jnp.exp2(raw - jnp.max(raw, axis=0, keepdims=True))
    return expos, jnp.sum(expos, axis=0, keepdims=True)


def gates_kernel(
    flags, asks, pair, wu, wg, bias, initial, summary, forget, update, give, own, work
):
    step = pl.program_id(0)

    @pl.when(step < 4)
    def _():
        for head in range(2):
            at = slice(head * HEAD_DIM, (head + 1) * HEAD_DIM)
            expos, total = summary_probs_of(pair[0, :, at], asks[:, at])
            held = product_tn(pair[1, :, at], expos.astype(BF)) / total
            place = pl.multiple_of(step * 256 + head * HEAD_DIM, HEAD_DIM)
            summary[:, pl.ds(place, HEAD_DIM)] = held.T.astype(BF)

    @pl.when(step >= 4)
    def _():
        start = flags[START].astype(F32)
        rows = summary[...]
        fresh = product(rows, wu[...])
        gate = jax.nn.sigmoid(product(rows, wg[...]) + bias[...])
        update[...] = fresh
        forget[...] = gate
        work[0] = (1.0 - start) * gate
        work[1] = start * gate * initial[...] + (1.0 - gate) * fresh
        mine = pl.multiple_of(flags[CORE] * HALF, HALF)
        others = pl.multiple_of((1 - flags[CORE]) * HALF, HALF)
        for part in range(2):
            own[part] = work[part, pl.ds(mine, HALF)].astype(BF)
            give[part] = work[part, pl.ds(others, HALF)].astype(BF)


def gates(clock, asks, pair, state_weight, bias, initial):
    step = 256
    early = lambda i, *_: (0, jnp.minimum(i, 3))
    late = lambda i, *_: (0, jnp.maximum(i - 4, 0))
    late3 = lambda i, *_: (0, 0, jnp.maximum(i - 4, 0))
    return clock.run(
        gates_kernel,
        (
            shape((NS, D), BF),
            shape((NS, D), F32),
            shape((NS, D), F32),
            shape((2, HALF, D), BF),
            shape((2, HALF, D), BF),
        ),
        (asks, pair, state_weight, state_weight, bias, initial),
        (8,),
        [
            pl.BlockSpec((NS, step), early),
            pl.BlockSpec((2, W, step), lambda i, *_: (0, 0, jnp.minimum(i, 3))),
            pl.BlockSpec((D, step), late),
            pl.BlockSpec((D, step), lambda i, *_: (0, jnp.maximum(i - 4, 0) + D // step)),
            pl.BlockSpec((1, step), late),
            pl.BlockSpec((NS, step), late),
        ],
        (
            whole((NS, D)),
            pl.BlockSpec((NS, step), late),
            pl.BlockSpec((NS, step), late),
            pl.BlockSpec((2, HALF, step), late3),
            pl.BlockSpec((2, HALF, step), late3),
        ),
        [pltpu.VMEM((2, NS, step), F32)],
        flops=4 * NS * W * D + 4 * NS * D * D,
    )


def rows_of(chip):
    return pl.ds(pl.multiple_of(chip * QUARTER, QUARTER), QUARTER)


def compose_kernel(flags, own, recv, keep, to1, to2, to3, work):
    odd_core = flags[CORE] == 1
    pick2 = lambda part: (own[part].astype(F32), recv[part].astype(F32))
    (own_scale, recv_scale), (own_base, recv_base) = pick2(0), pick2(1)
    later_scale = jnp.where(odd_core, own_scale, recv_scale)
    earlier_base = jnp.where(odd_core, recv_base, own_base)
    later_base = jnp.where(odd_core, own_base, recv_base)
    work[0] = own_scale * recv_scale
    work[1] = later_scale * earlier_base + later_base
    for far, out in enumerate((keep, to1, to2, to3)):
        out[...] = work[:, rows_of(flags[CHIP] ^ far)].astype(BF)


def prefix_kernel(flags, keep, from1, from2, from3, mine, to1, to2, to3, got, enter):
    for far, came in enumerate((keep, from1, from2, from3)):
        got[flags[CHIP] ^ far] = came[...].astype(F32)
    state = got[0, 1]
    enter[0] = jnp.zeros_like(state)
    enter[1] = state
    for chip in (1, 2):
        state = got[chip, 0] * state + got[chip, 1]
        enter[chip + 1] = state
    for far, out in enumerate((mine, to1, to2, to3)):
        out[...] = enter[flags[CHIP] ^ far].astype(BF)


def previous_kernel(flags, mine, from1, from2, from3, own, recv, keep, give, before):
    for far, came in enumerate((mine, from1, from2, from3)):
        before[rows_of(flags[CHIP] ^ far)] = came[...].astype(F32)
    odd_core = flags[CORE] == 1
    scale = jnp.where(odd_core, recv[0].astype(F32), own[0].astype(F32))
    base = jnp.where(odd_core, recv[1].astype(F32), own[1].astype(F32))
    entry = before[...]
    between = scale * entry + base
    keep[...] = jnp.where(odd_core, between, entry).astype(BF)
    give[...] = jnp.where(odd_core, entry, between).astype(BF)


def compose_back_kernel(flags, own, recv, own_pair, recv_pair, keep, to1, to2, to3, work):
    odd_core = flags[CORE] == 1
    scale = jnp.where(odd_core, recv_pair[0].astype(F32), own_pair[0].astype(F32))
    mine, other = own[...].astype(F32), recv[...].astype(F32)
    work[...] = scale * jnp.where(odd_core, mine, other) + jnp.where(odd_core, other, mine)
    for far, out in enumerate((keep, to1, to2, to3)):
        out[...] = work[rows_of(flags[CHIP] ^ far)].astype(BF)


def suffix_kernel(
    flags, keep, from1, from2, from3, kept0, kept1, kept2, kept3, mine, to1, to2, to3, got, enter
):
    pairs = ((keep, kept0), (from1, kept1), (from2, kept2), (from3, kept3))
    for far, (came, kept) in enumerate(pairs):
        got[flags[CHIP] ^ far, 0] = kept[0].astype(F32)
        got[flags[CHIP] ^ far, 1] = came[...].astype(F32)
    state = got[3, 1]
    enter[3] = jnp.zeros_like(state)
    enter[2] = state
    for chip in (2, 1):
        state = got[chip, 0] * state + got[chip, 1]
        enter[chip - 1] = state
    for far, out in enumerate((mine, to1, to2, to3)):
        out[...] = enter[flags[CHIP] ^ far].astype(BF)


def following_kernel(
    flags, mine, from1, from2, from3, own, recv, own_pair, recv_pair, keep, give, after
):
    for far, came in enumerate((mine, from1, from2, from3)):
        after[rows_of(flags[CHIP] ^ far)] = came[...].astype(F32)
    odd_core = flags[CORE] == 1
    scale = jnp.where(odd_core, own_pair[0].astype(F32), recv_pair[0].astype(F32))
    base = jnp.where(odd_core, own[...].astype(F32), recv[...].astype(F32))
    entry = after[...]
    between = scale * entry + base
    keep[...] = jnp.where(odd_core, entry, between).astype(BF)
    give[...] = jnp.where(odd_core, between, entry).astype(BF)


def small(clock, kernel, outs, args, scratch):
    return clock.run(
        kernel,
        tuple(shape(dims, BF) for dims in outs),
        args,
        (1,),
        [whole(a.shape) for a in args],
        tuple(whole(dims) for dims in outs),
        [pltpu.VMEM(dims, F32) for dims in scratch],
        limit=10,
    )


def to_chips(values):
    return (values[0],) + tuple(
        swapped(value, "seq", 2 * far) for far, value in zip((1, 2, 3), values[1:])
    )


PAIR_WORK = [(4, 2, QUARTER, D), (4, QUARTER, D)]


def compose(clock, own, recv):
    return to_chips(small(clock, compose_kernel, [(2, QUARTER, D)] * 4, (own, recv), [(2, HALF, D)]))


def prefix(clock, got):
    return to_chips(small(clock, prefix_kernel, [(QUARTER, D)] * 4, got, PAIR_WORK))


def previous(clock, back, own, recv):
    mine, other = small(
        clock, previous_kernel, [(HALF, D)] * 2, back + (own, recv), [(HALF, D)]
    )
    return mine, swapped(other, "seq", 1)


def compose_back(clock, *args):
    return to_chips(small(clock, compose_back_kernel, [(QUARTER, D)] * 4, args, [(HALF, D)]))


def suffix(clock, got, kept):
    return to_chips(small(clock, suffix_kernel, [(QUARTER, D)] * 4, got + kept, PAIR_WORK))


def following(clock, back, *args):
    mine, other = small(clock, following_kernel, [(HALF, D)] * 2, back + args, [(HALF, D)])
    return mine, swapped(other, "seq", 1)


def state_kernel(
    flags, mine, other, initial, forget, update, wk, wv, state_in, state_low, state_out, pair
):
    @pl.when(pl.program_id(0) == 0)
    def _():
        start = flags[START].astype(F32)
        for core, came in ((flags[CORE], mine), (1 - flags[CORE], other)):
            rows = pl.ds(pl.multiple_of(core * HALF, HALF), HALF)
            entry = (1.0 - start) * came[...].astype(F32) + start * initial[rows, :]
            gate = forget[rows, :]
            state_in[rows, :] = entry
            state_low[rows, :] = entry.astype(BF)
            state_out[rows, :] = gate * entry + (1.0 - gate) * update[rows, :]

    rows = state_low[...]
    pair[0] = product(rows, wk[...]).astype(BF)
    pair[1] = product(rows, wv[...]).astype(BF)


def state_pair(clock, mine, other, initial, forget, update, wk, wv):
    step = 256
    column = pl.BlockSpec((D, step), lambda j, *_: (0, j))
    return clock.run(
        state_kernel,
        (shape((NS, D), F32), shape((NS, D), BF), shape((NS, D), F32), shape((2, NS, D), BF)),
        (mine, other, initial, forget, update, wk, wv),
        (D // step,),
        [whole((HALF, D))] * 2 + [whole((NS, D))] * 3 + [column, column],
        (
            whole((NS, D)),
            whole((NS, D)),
            whole((NS, D)),
            pl.BlockSpec((2, NS, step), lambda j, *_: (0, 0, j)),
        ),
        flops=4 * NS * D * D,
    )


def masked_scores(flags, queries, left, own, state):
    seen = []
    left_bias = jnp.where(flags[START] == 0, 0.0, NEGATIVE).astype(F32)
    seen.append(product_nt(left[0], queries) * SCALE_LOG2 + left_bias)
    rows = lax.broadcasted_iota(jnp.int32, (W, W), 0)
    cols = lax.broadcasted_iota(jnp.int32, (W, W), 1)
    seen.append(jnp.where(rows <= cols, product_nt(own[0], queries) * SCALE_LOG2, NEGATIVE))
    seen.append(product_nt(state[0], queries) * SCALE_LOG2)
    return seen


PER_STEP = 2


def each_head(*refs):
    for head in range(PER_STEP):
        at = pl.ds(head * HEAD_DIM, HEAD_DIM)
        yield head, [ref.at[..., at] for ref in refs]


def attend_kernel(flags, *refs):
    lse = refs[-1]
    for head, (queries, left, own, state, attended) in each_head(*refs[:-1]):
        seen = masked_scores(flags, queries[...], left, own, state)
        peak = functools.reduce(
            jnp.maximum, [jnp.max(part, axis=0, keepdims=True) for part in seen]
        )
        held = 0.0
        total = 0.0
        for part, pair in zip(seen, (left, own, state)):
            expos = jnp.exp2(part - peak)
            total = total + jnp.sum(expos, axis=0, keepdims=True)
            held = held + product_tn(pair[1], expos.astype(BF))
        attended[...] = (held / total).T.astype(BF)
        lse[head] = peak + jnp.log2(total)


HEADS_WIDE = PER_STEP * HEAD_DIM


def attend(clock, queries, left, own, state):
    head = pl.BlockSpec((W, HEADS_WIDE), lambda h, *_: (0, h))
    pair = pl.BlockSpec((2, W, HEADS_WIDE), lambda h, *_: (0, 0, h))
    return clock.run(
        attend_kernel,
        (shape((W, D), BF), shape((HEADS, 1, W), F32)),
        (queries, left, own, state),
        (HEADS // PER_STEP,),
        [head, pair, pair, pair],
        (head, pl.BlockSpec((PER_STEP, 1, W), lambda h, *_: (h, 0, 0))),
        flops=4 * W * (2 * W + NS) * D,
        stream=True,
        limit=26,
    )


def attend_back_kernel(flags, queries, left, own, state, grad, lse, *outs):
    for head, (asks, left_h, own_h, state_h, grad_h, queries_grad, *grads) in each_head(
        queries, left, own, state, grad, *outs
    ):
        asks, out_grad = asks[...], grad_h[...]
        pairs = (left_h, own_h, state_h)
        seen = masked_scores(flags, asks, *pairs)
        probs = [jnp.exp2(part - lse[head]) for part in seen]
        prob_grads = [product_nt(pair[1], out_grad) for pair in pairs]
        rowdot = sum(
            jnp.sum(prob * prob_grad, axis=0, keepdims=True)
            for prob, prob_grad in zip(probs, prob_grads)
        )
        total = 0.0
        for prob, prob_grad, pair, out in zip(probs, prob_grads, pairs, grads):
            score_grad = (prob * (prob_grad - rowdot)).astype(BF)
            out[0] = (product(score_grad, asks) * SCALE).astype(out.dtype)
            out[1] = product(prob.astype(BF), out_grad).astype(out.dtype)
            total = total + product_tn(pair[0], score_grad)
        queries_grad[...] = (total * SCALE).T.astype(BF)


def attend_back(clock, queries, left, own, state, grad, lse):
    head = pl.BlockSpec((W, HEADS_WIDE), lambda h, *_: (0, h))
    pair = pl.BlockSpec((2, W, HEADS_WIDE), lambda h, *_: (0, 0, h))
    return clock.run(
        attend_back_kernel,
        (shape((W, D), BF), shape((2, W, D), BF), shape((2, W, D), F32), shape((2, NS, D), BF)),
        (queries, left, own, state, grad, lse),
        (HEADS // PER_STEP,),
        [head, pair, pair, pair, head, pl.BlockSpec((PER_STEP, 1, W), lambda h, *_: (h, 0, 0))],
        (head, pair, pair, pair),
        flops=10 * W * (2 * W + NS) * D,
        stream=True,
        limit=36,
    )


def gelu_parts(upper):
    square = upper * upper
    inner = GELU_SCALE * (upper + GELU_CUBIC * square * upper)
    bent = jnp.tanh(inner)
    value = 0.5 * upper * (1.0 + bent)
    slope = 0.5 * (1.0 + bent) + 0.5 * upper * (1.0 - bent * bent) * GELU_SCALE * (
        1.0 + 3.0 * GELU_CUBIC * square
    )
    return value, slope


def mlp_step(normed_mlp, come, up1, up2, down, up, activated, upper_grad, total, grad):
    half = up1.shape[1]
    up[:, :half] = up1[...]
    up[:, half:] = up2[...]
    rows = down[...].reshape(2 * half, D)
    value, slope = gelu_parts(product(normed_mlp[...], up[...]))
    value = value.astype(BF)
    activated[...] = value
    total[...] += product(value, rows)
    back = (come[...].astype(F32) * slope).astype(BF)
    upper_grad[...] = back
    grad[...] += product_nt(back, up[...])


def come_kernel(flags, cotangent, down1, down2, come1, come2):
    for down, come in ((down1, come1), (down2, come2)):
        rows = down[...].reshape(come.shape[1], D)
        come[...] = product_nt(cotangent[...], rows).astype(BF)


def come_back(clock, cotangent, down):
    return clock.run(
        come_kernel,
        (shape((W, FF // 2), BF),) * 2,
        (cotangent, down, down),
        (PAIRS,),
        [fixed((W, D)), mlp_specs(0)[2], mlp_specs(1)[2]],
        (mlp_halves(),) * 2,
        flops=2 * W * D * FF,
    )


def mlp_first_kernel(
    flags,
    attended,
    tokens,
    out_weight,
    gain,
    come,
    up1,
    up2,
    down,
    activated,
    upper_grad,
    normed_mlp,
    hidden,
    total,
    grad,
    up,
):
    @pl.when(pl.program_id(0) == 0)
    def _():
        field = tokens[...].astype(F32) + product(attended[...], out_weight[...])
        hidden[...] = field
        normed_mlp[...] = (field * rms_scale(field) * gain[...]).astype(BF)
        total[...] = field
        grad[...] = jnp.zeros_like(field)

    mlp_step(normed_mlp, come, up1, up2, down, up, activated, upper_grad, total, grad)


def mlp_second_kernel(
    flags,
    normed_mlp,
    hidden,
    total_in,
    grad_in,
    out_weight,
    gain,
    cotangent,
    come,
    up1,
    up2,
    down,
    activated,
    upper_grad,
    mixed,
    hidden_grad,
    attended_grad,
    heads_grad,
    gain_grad,
    total,
    grad,
    up,
):
    step = pl.program_id(0)

    @pl.when(step == 0)
    def _():
        total[...] = total_in[...]
        grad[...] = grad_in[...]

    mlp_step(normed_mlp, come, up1, up2, down, up, activated, upper_grad, total, grad)

    @pl.when(step == pl.num_programs(0) - 1)
    def _():
        mixed[...] = total[...].astype(BF)
        field = hidden[...]
        scaled = rms_scale(field)
        gain_grad[...] = jnp.sum(grad[...] * field * scaled, axis=0, keepdims=True)
        weighted = grad[...] * gain[...]
        field_grad = (
            cotangent[...].astype(F32)
            + scaled * weighted
            - field
            * (scaled * scaled * scaled * jnp.mean(weighted * field, axis=-1, keepdims=True))
        )
        hidden_grad[...] = field_grad
        low = field_grad.astype(BF)
        attended_grad[...] = low
        heads_grad[...] = product_nt(low, out_weight[...]).astype(BF)


PIECE = 256
PAIRS = FF // (4 * PIECE)


def mlp_specs(part):
    return [
        pl.BlockSpec((D, PIECE), lambda j, *_: (0, 4 * j + part)),
        pl.BlockSpec((D, PIECE), lambda j, *_: (0, 4 * j + 2 + part)),
        pl.BlockSpec((2, PIECE, D), lambda j, *_: (j, part, 0)),
    ]


def mlp_halves():
    return pl.BlockSpec((W, 2 * PIECE), lambda j, *_: (0, j))


def mlp_first(clock, attended, tokens, out_weight, gain, come, up, down):
    rows = whole((W, D))
    return clock.run(
        mlp_first_kernel,
        (
            shape((W, FF // 2), BF),
            shape((W, FF // 2), BF),
            shape((W, D), BF),
            shape((W, D), F32),
            shape((W, D), F32),
            shape((W, D), F32),
        ),
        (attended, tokens, out_weight, gain, come, up, up, down),
        (PAIRS,),
        [fixed((W, D)), fixed((W, D)), fixed((D, D)), fixed((1, D)), mlp_halves()] + mlp_specs(0),
        (mlp_halves(), mlp_halves(), rows, rows, rows, rows),
        [pltpu.VMEM((D, 2 * PIECE), BF)],
        flops=3 * W * D * FF + 2 * W * D * D,
        limit=36,
    )


def mlp_second(
    clock, normed_mlp, hidden, total, grad, out_weight, gain, cotangent, come, up, down
):
    rows = whole((W, D))
    return clock.run(
        mlp_second_kernel,
        (
            shape((W, FF // 2), BF),
            shape((W, FF // 2), BF),
            shape((W, D), BF),
            shape((W, D), F32),
            shape((W, D), BF),
            shape((W, D), BF),
            shape((1, D), F32),
        ),
        (normed_mlp, hidden, total, grad, out_weight, gain, cotangent, come, up, up, down),
        (PAIRS,),
        [fixed((W, D))] * 4
        + [fixed((D, D)), fixed((1, D)), fixed((W, D)), mlp_halves()]
        + mlp_specs(1),
        (mlp_halves(), mlp_halves(), rows, rows, rows, rows, whole((1, D))),
        [pltpu.VMEM((W, D), F32), pltpu.VMEM((W, D), F32), pltpu.VMEM((D, 2 * PIECE), BF)],
        flops=3 * W * D * FF + 2 * W * D * D,
        limit=36,
    )


def direct_kernel(flags, state_grad, wk, wv, forget, cotangent, direct, own, give, work):
    grad = product_nt(state_grad[0], wk[...]) + product_nt(state_grad[1], wv[...])
    direct[...] = grad
    keep = 1.0 - flags[START].astype(F32)
    work[...] = keep * (forget[...] * cotangent[...] + grad)
    own[...] = work[pl.ds(pl.multiple_of(flags[CORE] * HALF, HALF), HALF)].astype(BF)
    give[...] = work[pl.ds(pl.multiple_of((1 - flags[CORE]) * HALF, HALF), HALF)].astype(BF)


def direct_grad(clock, state_grad, wk, wv, forget, cotangent):
    step = 256
    row = pl.BlockSpec((step, D), lambda j, *_: (j, 0))
    column = pl.BlockSpec((NS, step), lambda j, *_: (0, j))
    half = pl.BlockSpec((HALF, step), lambda j, *_: (0, j))
    return clock.run(
        direct_kernel,
        (shape((NS, D), F32), shape((HALF, D), BF), shape((HALF, D), BF)),
        (state_grad, wk, wv, forget, cotangent),
        (D // step,),
        [whole((2, NS, D)), row, row, column, column],
        (column, half, half),
        [pltpu.VMEM((NS, step), F32)],
        flops=4 * NS * D * D,
    )


def state_back_kernel(
    flags,
    mine,
    other,
    cotangent,
    forget,
    update,
    state_in,
    direct,
    wu,
    wg,
    initial_grad,
    projected_grad,
    bias_grad,
    summary_grad,
    work,
    total,
):
    step = pl.program_id(0)
    for core, came in ((flags[CORE], mine), (1 - flags[CORE], other)):
        work[pl.ds(pl.multiple_of(core * HALF, HALF), HALF)] = came[...].astype(F32)
    out_grad = cotangent[...] + work[...]
    gate = forget[...]
    start = flags[START].astype(F32)
    initial_grad[...] = (start * (gate * out_grad + direct[...])).astype(BF)
    rest = 1.0 - gate
    gate_grad = out_grad * (state_in[...] - update[...]) * gate * rest
    bias_grad[...] = jnp.sum(gate_grad, axis=0, keepdims=True)
    fresh_grad = (out_grad * rest).astype(BF)
    gate_low = gate_grad.astype(BF)
    projected_grad[0] = fresh_grad
    projected_grad[1] = gate_low
    part = product_nt(fresh_grad, wu[...]) + product_nt(gate_low, wg[...])

    @pl.when(step == 0)
    def _():
        total[...] = part

    @pl.when(step > 0)
    def _():
        total[...] += part

    @pl.when(step == pl.num_programs(0) - 1)
    def _():
        summary_grad[...] = total[...].astype(BF)


def state_back(clock, mine, other, cotangent, forget, update, state_in, direct, state_weight):
    step = 256
    column = pl.BlockSpec((NS, step), lambda j, *_: (0, j))
    half = pl.BlockSpec((HALF, step), lambda j, *_: (0, j))
    return clock.run(
        state_back_kernel,
        (
            shape((NS, D), BF),
            shape((2, NS, D), BF),
            shape((1, D), F32),
            shape((NS, D), BF),
        ),
        (mine, other, cotangent, forget, update, state_in, direct, state_weight, state_weight),
        (D // step,),
        [half, half, column, column, column, column, column]
        + [
            pl.BlockSpec((D, step), lambda j, *_: (0, j)),
            pl.BlockSpec((D, step), lambda j, *_: (0, j + D // step)),
        ],
        (
            column,
            pl.BlockSpec((2, NS, step), lambda j, *_: (0, 0, j)),
            pl.BlockSpec((1, step), lambda j, *_: (0, j)),
            whole((NS, D)),
        ),
        [pltpu.VMEM((NS, step), F32), pltpu.VMEM((NS, D), F32)],
        flops=4 * NS * D * D,
    )


def summary_back_kernel(flags, *refs):
    for _, (asks, pair, grad, own_grad, asks_grad, pair_total) in each_head(*refs):
        queries, out_grad = asks[...], grad[...]
        expos, total = summary_probs_of(pair[0], queries)
        probs = expos * (1.0 / total)
        prob_grad = product_nt(pair[1], out_grad)
        rowdot = jnp.sum(probs * prob_grad, axis=0, keepdims=True)
        score_grad = (probs * (prob_grad - rowdot)).astype(BF)
        asks_grad[...] = (product_tn(pair[0], score_grad) * SCALE).T.astype(BF)
        pair_total[0] = (own_grad[0] + product(score_grad, queries) * SCALE).astype(BF)
        pair_total[1] = (own_grad[1] + product(probs.astype(BF), out_grad)).astype(BF)


def summary_back(clock, asks, pair, grad, own_grad):
    head = pl.BlockSpec((W, HEADS_WIDE), lambda h, *_: (0, h))
    both = pl.BlockSpec((2, W, HEADS_WIDE), lambda h, *_: (0, 0, h))
    return clock.run(
        summary_back_kernel,
        (shape((NS, D), BF), shape((2, W, D), BF)),
        (asks, pair, grad, own_grad),
        (HEADS // PER_STEP,),
        [head, both, head, both],
        (head, both),
        flops=10 * NS * W * D,
        stream=True,
    )


def tokens_back_kernel(
    flags,
    queries_grad,
    pair_total,
    returned,
    wq,
    wk,
    wv,
    tokens,
    gain,
    hidden_grad,
    tokens_grad,
    gain_grad,
    total,
):
    step = pl.program_id(0)

    @pl.when(step < 2)
    def _():
        part = product_nt(queries_grad[...], wq[...])
        total[...] = jnp.where(step == 0, part, total[...] + part)

    @pl.when((step >= 2) & (step < 4))
    def _():
        total[...] += product_nt(add_low(pair_total[0], returned[0]), wk[...])

    @pl.when(step >= 4)
    def _():
        total[...] += product_nt(add_low(pair_total[0], returned[0]), wv[...])

    @pl.when(step == 5)
    def _():
        inputs = tokens[...].astype(F32)
        scaled = rms_scale(inputs)
        grad = total[...]
        gain_grad[...] = jnp.sum(grad * inputs * scaled, axis=0, keepdims=True)
        weighted = grad * gain[...]
        tokens_grad[...] = (
            hidden_grad[...]
            + scaled * weighted
            - inputs
            * (scaled * scaled * scaled * jnp.mean(weighted * inputs, axis=-1, keepdims=True))
        )


def tokens_back(clock, queries_grad, pair_total, returned, wq, wk, wv, tokens, gain, hidden_grad):
    step = D // 2
    clamp = lambda i, low: jnp.clip(i - low, 0, 1)
    weight = lambda low: pl.BlockSpec((D, step), lambda i, *_: (0, clamp(i, low)))
    later = lambda i: jnp.maximum(i - 2, 0)
    pair = pl.BlockSpec((1, W, step), lambda i, *_: (later(i) // 2, 0, later(i) % 2))
    return clock.run(
        tokens_back_kernel,
        (shape((W, D), F32), shape((1, D), F32)),
        (queries_grad, pair_total, returned, wq, wk, wv, tokens, gain, hidden_grad),
        (6,),
        [
            pl.BlockSpec((W, step), lambda i, *_: (0, clamp(i, 0))),
            pair,
            pair,
            weight(0),
            weight(2),
            weight(4),
            fixed((W, D)),
            fixed((1, D)),
            fixed((W, D)),
        ],
        (whole((W, D)), whole((1, D))),
        [pltpu.VMEM((W, D), F32)],
        flops=6 * W * D * D,
    )


def chunk_natural(flags, place):
    return place


def chunk_along_x(flags, place):
    x = flags[CHIP] & 1
    return 2 * (place % 2) + (1 - x if place < 2 else x)


def chunk_along_y(flags, place):
    y = flags[CHIP] >> 1
    return 2 * (1 - y if place < 2 else y) + place % 2


def column_blocks(terms):
    return terms[0][1][0][0].shape[2] // D


def weight_kernel(plan, merge, flags, *refs):
    refs = list(refs)
    lefts = [refs.pop(0) for _ in range(plan["lefts"])]
    rights = [[refs.pop(0) for _ in adds] for adds in plan["rights"]]
    extras = [refs.pop(0) for _ in range(plan["extras"])]
    recv = refs.pop(0) if merge else None
    work = refs.pop()
    core = flags[CORE] if merge else 1 - flags[CORE]
    step, base, start = pl.program_id(0), 0, 0

    def write(along, place, at, here, part):
        rows = part.shape[0]
        if merge:
            chunk = (chunk_along_x, chunk_along_y)[along](flags, place)
            part = part.astype(F32) + recv[chunk, at : at + rows].astype(F32)
            refs[2 * along + place // 2][place % 2, here : here + rows] = part.astype(BF)
        else:
            refs[0][place, at : at + rows] = part.astype(BF)

    def source(along, place):
        chunk_of = (chunk_along_x, chunk_along_y)[along] if merge else chunk_natural
        return 2 * chunk_of(flags, place) + core

    for along, group in enumerate(plan["grads"]):
        here = 0
        for rows, blocks, terms in group:

            @pl.when(step == base)
            def _():
                for term, (left, _) in enumerate(terms):
                    for place in range(4):
                        first = pl.multiple_of(source(along, place) * rows, rows)
                        block = lefts[left][:, pl.ds(first, rows)]
                        work[term, place * rows : (place + 1) * rows] = block.T

            for block in range(blocks):

                @pl.when(step == base + block)
                def _():
                    total = 0.0
                    for term, (_, right) in enumerate(terms):
                        parts = [part[0] for part in rights[right]]
                        value = parts[0] if len(parts) == 1 else add_low(*parts)
                        total = total + product(work[term, : 4 * rows], value)
                    at = block * rows
                    for place in range(4):
                        part = total[place * rows : (place + 1) * rows]
                        write(along, place, start + at, here + at, part)

            base += blocks
            start += blocks * rows
            here += blocks * rows
        if extras:
            rows = extras[along].shape[0] // 8

            @pl.when(step == 0)
            def _():
                for place in range(4):
                    first = pl.multiple_of(source(along, place) * rows, rows)
                    write(along, place, start, here, extras[along][pl.ds(first, rows)])

            start += rows


def weight_pair(clock, grads, extras, recv):
    lefts, left_ids, rights, args, specs, plans = [], {}, [], [], [], []
    base, start, tokens, most = 0, 0, grads[0][0][0][0].shape[0], 0
    sizes = []
    for along, group in enumerate(grads):
        total, plan = 0, []
        for terms in group:
            rows, blocks = terms[0][0].shape[1] // 8, column_blocks(terms)
            most = max(most, rows)
            steps = []
            for left, adds in terms:
                if id(left) not in left_ids:
                    left_ids[id(left)] = len(lefts)
                    lefts.append(left)
                steps.append((left_ids[id(left)], len(rights)))
                rights.append(tuple(index for _, index in adds))
                for right, index in adds:
                    args.append(right)
                    specs.append(
                        pl.BlockSpec(
                            (1, tokens, D),
                            lambda j, *_, index=index, base=base, blocks=blocks: (
                                index,
                                0,
                                jnp.clip(j - base, 0, blocks - 1),
                            ),
                        )
                    )
            plan.append((rows, blocks, steps))
            base += blocks
            total += blocks * rows
        if extras:
            total += extras[along].shape[0] // 8
        plans.append(plan)
        sizes.append(total)
        start += total
    args = lefts + args + list(extras)
    specs = [fixed(left.shape) for left in lefts] + specs + [fixed(e.shape) for e in extras]
    merge = recv is not None
    if merge:
        args.append(recv)
        specs.append(fixed(recv.shape))
        dims = [(2, total, D) for total in sizes for _ in range(2)]
    else:
        dims = [(4, start, D)]
    plan = {"lefts": len(lefts), "rights": rights, "extras": len(extras), "grads": plans}
    return clock.run(
        functools.partial(weight_kernel, plan, merge),
        tuple(shape(d, BF) for d in dims),
        tuple(args),
        (base,),
        specs,
        tuple(whole(d) for d in dims),
        [pltpu.VMEM((len(grads[0][0]), 4 * most, tokens), BF)],
        flops=2 * tokens * 4 * start * D * len(grads[0][0]),
        limit=24,
    )


def scatter_bits(value, bits, names):
    place = lax.axis_index("seq")
    names = list(names)
    for bit in bits:
        at = names.index(bit)
        mine = (place >> bit) & 1
        recv = swapped(pick(value, 1 - mine, at), "seq", 1 << bit)
        value = add_low(pick(value, mine, at), recv)
        names.pop(at)
    return value


def whole_scatter(value, along_x):
    count = lax.axis_size("seq")
    levels = count.bit_length() - 1
    names = list(range(levels - 1, -1, -1))
    value = value.reshape((2,) * levels + (value.shape[0] // count,) + value.shape[1:])
    bits = [0] + (names[-2::-1] if along_x else names[:-1])
    return scatter_bits(value, bits, names)


def in_rows(value):
    return jnp.concatenate([value[:, at : at + D] for at in range(0, value.shape[1], D)], axis=0)


def turn_kernel(flags, kept1, recv1, kept2, recv2, send1, send2):
    send1[...] = add_low(kept1[0], recv1[0])
    send2[...] = add_low(kept2[0], recv2[0])


def pack_kernel(flags, *refs):
    out, start = refs[-1], 0
    for at in range(0, len(refs) - 1, 3):
        kept, recv, last = refs[at : at + 3]
        rows = last.shape[0]
        out[start : start + rows] = add_low(kept[0], recv[0], last[...])
        start += rows


class Scatter:
    def __init__(self, clock, firsts, seconds, extras=()):
        self.grads, self.extras, self.plain = (firsts, seconds), extras, None
        if lax.axis_size("seq") != 8:
            sums = []
            for number, group in enumerate(self.grads):
                for terms in group:
                    total = 0.0
                    for left, adds in terms:
                        parts = [right[index] for right, index in adds]
                        right = add_low(*parts) if len(parts) > 1 else parts[0]
                        total = total + product_tn(left, right)
                    sums.append(in_rows(whole_scatter(total.astype(BF), number == 0)))
                if extras:
                    sums.append(whole_scatter(extras[number], number == 0))
            self.plain = jnp.concatenate(sums, axis=0)
            return
        (self.give,) = weight_pair(clock, self.grads, self.extras, None)

    def core(self, clock):
        if self.plain is None:
            self.recv = swapped(clock.at(self.give), "seq", 1)

    def keep(self, clock):
        if self.plain is None:
            send1, kept1, send2, kept2 = weight_pair(clock, self.grads, self.extras, self.recv)
            self.kept, self.send = (kept1, kept2), (send1, send2)

    def near(self, clock):
        if self.plain is None:
            self.recv = tuple(
                swapped(clock.at(send), "seq", far) for send, far in zip(self.send, (2, 4))
            )

    def held(self, other):
        args, specs = [], []
        for number, (kept, recv) in enumerate(zip(self.kept, self.recv)):
            bit = 1 - number
            mine = lambda i, flags, bit=bit: (((flags[CHIP] >> bit) & 1) ^ other, 0, 0)
            args.append([kept, recv])
            specs.append([pl.BlockSpec((1,) + kept.shape[1:], mine)] * 2)
        return args, specs

    def turn(self, clock, flops=0):
        if self.plain is None:
            args, specs = self.held(1)
            dims = [kept.shape[1:] for kept in self.kept]
            self.send = clock.run(
                turn_kernel,
                tuple(shape(d, BF) for d in dims),
                tuple(args[0] + args[1]),
                (1,),
                specs[0] + specs[1],
                tuple(whole(d) for d in dims),
                flops=flops,
                limit=10,
            )

    def far(self, clock):
        if self.plain is None:
            self.last = tuple(
                swapped(clock.at(send), "seq", far) for send, far in zip(self.send, (4, 2))
            )

    def parts(self):
        args, specs = self.held(0)
        for number, last in enumerate(self.last):
            args[number].append(last)
            specs[number].append(whole(last.shape))
        return args[0] + args[1], specs[0] + specs[1]


def pack(clock, *scatters):
    if scatters[0].plain is not None:
        return jnp.concatenate([scatter.plain for scatter in scatters], axis=0)
    args, specs = [], []
    for scatter in scatters:
        more = scatter.parts()
        args += more[0]
        specs += more[1]
    total = sum(arg.shape[0] for arg in args[2::3])
    args = [pltpu.with_memory_space_constraint(arg, pltpu.HBM) for arg in args]
    return clock.run(
        pack_kernel,
        (shape((total, D), BF),),
        tuple(args),
        (1,),
        specs,
        (whole((total, D)),),
        limit=16,
    )[0]


class Line:
    def __init__(self, clock, value):
        count = lax.axis_size("dp")
        half = count // 2
        self.value = value
        self.rounds = (
            [([(s, s + 1), (count - 1 - s, count - 2 - s)], None) for s in range(half - 1)]
            + [([(half - 1, half), (half, half - 1)], None)]
            + [
                ([(s + 1, s), (count - 2 - s, count - 1 - s)], (s, count - 1 - s))
                for s in range(half - 2, -1, -1)
            ]
        )
        self.send(clock)

    def send(self, clock):
        self.recv = lax.ppermute(clock.at(self.value), "dp", self.rounds[0][0])

    def take(self, clock):
        place = lax.axis_index("dp")
        takers = self.rounds.pop(0)[1]
        value = clock.at(self.value)
        if takers is None:
            self.value = add_low(value, self.recv)
        else:
            outer = (place == takers[0]) | (place == takers[1])
            self.value = jnp.where(outer, self.recv, value)
        if self.rounds:
            clock.after(self.value)

    def step(self, clock):
        self.take(clock)
        if self.rounds:
            self.send(clock)

    def finish(self, clock):
        while self.rounds:
            self.step(clock)
        return self.value.astype(F32)


def interleaved(first, second):
    blocks = []
    for at in range(0, first.shape[1], PIECE):
        blocks += [first[:, at : at + PIECE], second[:, at : at + PIECE]]
    return jnp.concatenate(blocks, axis=1)


def body(
    tokens,
    item_starts,
    attn_gain,
    query_weight,
    key_weight,
    value_weight,
    output_weight,
    state_queries,
    state_weight,
    gate_bias,
    initial_state,
    mlp_gain,
    up_weight,
    down_weight,
    out_cotangent,
    state_cotangent,
):
    count = lax.axis_size("seq")
    place = lax.axis_index("seq")
    clock = Clock(
        jnp.stack([item_starts[0, 0], place & 1, (place >> 1) & 3]).astype(jnp.int32)
    )
    tokens, cotangent, state_cot = tokens[0], out_cotangent[0], state_cotangent[0, 0]
    attn_gain, gate_bias, mlp_gain = attn_gain[None], gate_bias[None], mlp_gain[None]
    down_weight = down_weight.reshape(FF // (2 * PIECE), 2 * PIECE, D)

    tokens_left = shifted(tokens, "seq", 1)
    normed, queries, own = front(clock, tokens, attn_gain, query_weight, key_weight, value_weight)
    summary, forget, update, give_pair, own_pair = gates(
        clock, state_queries, own, state_weight, gate_bias, initial_state
    )
    recv_pair = swapped(give_pair, "seq", 1)
    left = left_pair(clock, tokens_left, attn_gain, key_weight, value_weight)
    kept_chips = compose(clock, own_pair, recv_pair)
    come1, come2 = come_back(clock, cotangent, down_weight)
    back = prefix(clock, kept_chips)
    mine, other = previous(clock, back, own_pair, recv_pair)
    state_in, state_low, state_out, state = state_pair(
        clock, mine, other, initial_state, forget, update, key_weight, value_weight
    )
    attended, lse = attend(clock, queries, left, own, state)
    split = count == 8
    activated1, upper_grad1, normed_mlp, hidden, total, grad = mlp_first(
        clock, attended, tokens, output_weight, mlp_gain, come1, up_weight, down_weight
    )
    out_grads = (cotangent[None], 0)
    if split:
        feed1 = Scatter(
            clock,
            [[(activated1, [out_grads])]],
            [[(normed_mlp, [(upper_grad1[None], 0)])]],
        )
        feed1.core(clock)
        feed1.keep(clock)
        feed1.near(clock)
    activated2, upper_grad2, mixed, hidden_grad, attended_grad, heads_grad, mlp_gain_grad = (
        mlp_second(
            clock,
            normed_mlp,
            hidden,
            total,
            grad,
            output_weight,
            mlp_gain,
            cotangent,
            come2,
            up_weight,
            down_weight,
        )
    )
    if split:
        feed2 = Scatter(
            clock,
            [[(activated2, [out_grads])]],
            [[(normed_mlp, [(upper_grad2[None], 0)])]],
        )
        feed2.core(clock)
        feed1.turn(clock, LONG)
        feed1.far(clock)
        feed2.keep(clock)
        feed2.near(clock)
    else:
        feed1 = Scatter(
            clock,
            [[(interleaved(activated1, activated2), [out_grads])]],
            [[(normed_mlp, [(interleaved(upper_grad1, upper_grad2)[None], 0)])]],
        )
    queries_grad, left_grad, own_grad, state_grad = attend_back(
        clock, queries, left, own, state, heads_grad, lse
    )
    direct, own_base, give_base = direct_grad(
        clock, state_grad, key_weight, value_weight, forget, state_cot
    )
    recv_base = swapped(give_base, "seq", 1)
    line1 = Line(clock, pack(clock, feed1))
    got = compose_back(clock, own_base, recv_base, own_pair, recv_pair)
    if split:
        feed2.turn(clock)
    back = suffix(clock, got, kept_chips)
    mine, other = following(clock, back, own_base, recv_base, own_pair, recv_pair)
    if split:
        feed2.far(clock)
    returned = shifted(clock.at(left_grad), "seq", -1)
    line1.step(clock)
    initial_grad, projected_grad, gate_bias_grad, summary_grad = state_back(
        clock, mine, other, state_cot, forget, update, state_in, direct, state_weight
    )
    others = Scatter(
        clock,
        [[(attended, [(attended_grad[None], 0)])], [(summary, [(projected_grad, 0)])]],
        [[(normed, [(queries_grad[None], 0)])], [(summary, [(projected_grad, 1)])]],
    )
    line2 = Line(clock, pack(clock, feed2)) if split else None
    others.core(clock)
    state_queries_grad, pair_total = summary_back(
        clock, state_queries, own, summary_grad, own_grad
    )
    others.keep(clock)
    if split:
        line2.step(clock)
    others.near(clock)
    line1.take(clock)
    keys_values = Scatter(
        clock,
        [[(normed, [(pair_total, 0), (returned, 0)]), (state_low, [(state_grad, 0)])]],
        [[(normed, [(pair_total, 1), (returned, 1)]), (state_low, [(state_grad, 1)])]],
        (state_queries_grad, initial_grad),
    )
    keys_values.core(clock)
    if line1.rounds:
        line1.send(clock)
    keys_values.keep(clock)
    if split:
        line2.take(clock)
    keys_values.near(clock)
    tokens_grad, attn_gain_grad = tokens_back(
        clock,
        queries_grad,
        pair_total,
        returned,
        query_weight,
        key_weight,
        value_weight,
        tokens,
        attn_gain,
        hidden_grad,
    )
    others.turn(clock)
    others.far(clock)
    line1 = line1.finish(clock)
    clock.after(line1)
    lanes, rows = D // count, NS // count
    vectors = jnp.concatenate([attn_gain_grad, gate_bias_grad, mlp_gain_grad])
    vectors = vectors.reshape(3, count, lanes).transpose(1, 0, 2).reshape(count, 1, 3 * lanes)
    vectors = jnp.pad(vectors, ((0, 0), (0, 7), (0, D - 3 * lanes))).astype(BF)
    keys_values.turn(clock)
    keys_values.far(clock)
    vectors = whole_scatter(clock.at(vectors.reshape(-1, D)), True)
    line3 = [Line(clock, half) for half in jnp.split(pack(clock, others), 2)]
    if split:
        line2.send(clock)
    line4 = Line(clock, jnp.concatenate([pack(clock, keys_values), vectors], axis=0))
    for line in line3 + [line4] + line3 + [line4]:
        line.step(clock)
    line3 = [line.finish(clock) for line in line3]
    line4 = line4.finish(clock)
    clock.after(line3, line4)
    line2 = line2.finish(clock) if split else None

    def unpack(packed, *dims):
        pieces, start = [], 0
        for high, wide in dims:
            parts = [
                packed[start + high * part : start + high * (part + 1)] for part in range(wide // D)
            ]
            start += high * (wide // D)
            pieces.append(parts[0] if len(parts) == 1 else jnp.concatenate(parts, axis=1))
        return pieces

    high, deep = D // count, FF // count
    if split:
        down1, up1 = unpack(line1, (deep // 2, D), (high, FF // 2))
        down2, up2 = unpack(line2, (deep // 2, D), (high, FF // 2))
        down_grad = jnp.concatenate([down1, down2], axis=0)
        up_grad = interleaved(up1, up2)
    else:
        down_grad, up_grad = unpack(line1, (deep, D), (high, FF))
    output_grad, first_grad, query_grad, second_grad = unpack(
        jnp.concatenate(line3),
        (high, D),
        (high, D),
        (high, D),
        (high, D),
    )
    state_weight_grad = jnp.concatenate([first_grad, second_grad], axis=1)
    key_grad, state_queries_grad, value_grad, initial_grad, vectors = unpack(
        line4, (high, D), (rows, D), (high, D), (rows, D), (8, D)
    )
    vectors = vectors[0, : 3 * lanes]
    return (
        mixed[None],
        state_out[None, None],
        tokens_grad[None],
        vectors[:lanes],
        query_grad,
        key_grad,
        value_grad,
        output_grad,
        state_queries_grad,
        state_weight_grad,
        vectors[lanes : 2 * lanes],
        initial_grad,
        vectors[2 * lanes :],
        up_grad,
        down_grad,
    )


def solution(mesh):
    in_specs = (
        P("dp", "seq", None),
        P("dp", "seq"),
        P(),
        P(),
        P(),
        P(),
        P(),
        P(),
        P(),
        P(),
        P(),
        P(),
        P(),
        P(),
        P("dp", "seq", None),
        P("dp", "seq", None, None),
    )
    out_specs = (
        P("dp", "seq", None),
        P("dp", "seq", None, None),
        P("dp", "seq", None),
        P("seq"),
        P("seq", None),
        P("seq", None),
        P("seq", None),
        P("seq", None),
        P("seq", None),
        P("seq", None),
        P("seq"),
        P("seq", None),
        P("seq"),
        P("seq", None),
        P("seq", None),
    )
    return jax.shard_map(body, mesh=mesh, in_specs=in_specs, out_specs=out_specs, check_vma=False)
```

```python
import functools
import math

import jax
import jax.numpy as jnp
from jax import lax
from jax.experimental import pallas as pl
from jax.experimental.pallas import tpu as pltpu
from jax.sharding import PartitionSpec as P

D = 1024
HEADS = 8
HEAD_DIM = 128
FF = 4096
W = 512
NS = 512
HALF = NS // 2
QUARTER = NS // 8

EPSILON = 1e-06
NEGATIVE = -1e30
GELU_SCALE = 0.7978845608028654
GELU_CUBIC = 0.044715
SCALE = 1.0 / math.sqrt(HEAD_DIM)
SCALE_LOG2 = SCALE * math.log2(math.e)

BF = jnp.bfloat16
F32 = jnp.float32
MIB = 1 << 20
LONG = 1e11


def swapped(value, axis, distance):
    count = lax.axis_size(axis)
    return lax.ppermute(value, axis, [(place, place ^ distance) for place in range(count)])


def shifted(value, axis, steps):
    count = lax.axis_size(axis)
    first, last = (max(0, -steps), min(count, count - steps))
    return lax.ppermute(value, axis, [(source, source + steps) for source in range(first, last)])


def add_low(*terms):
    total = terms[0].astype(F32)
    for term in terms[1:]:
        total = total + term.astype(F32)
    return total.astype(BF)


def pick(value, index, axis):
    return lax.dynamic_index_in_dim(value, index, axis, False)


def product(left, right):
    return jnp.dot(left, right, preferred_element_type=F32)


def product_tn(left, right):
    return lax.dot_general(left, right, (((0,), (0,)), ((), ())), preferred_element_type=F32)


def product_nt(left, right):
    return lax.dot_general(left, right, (((1,), (1,)), ((), ())), preferred_element_type=F32)


def rms_scale(field):
    return lax.rsqrt(jnp.mean(field * field, axis=-1, keepdims=True) + EPSILON)


def shape(dims, dtype):
    return jax.ShapeDtypeStruct(dims, dtype)


def whole(dims):
    return pl.BlockSpec(dims, lambda *_: (0,) * len(dims))


def fixed(dims):
    return pl.BlockSpec(dims, lambda *_: (0,) * len(dims), pipeline_mode=pl.Buffered(1))


class Clock:
    def __init__(self, flags):
        self.flags = flags

    def after(self, *values):
        self.flags = lax.optimization_barrier((self.flags, values))[0]

    def at(self, value):
        return lax.optimization_barrier((value, self.flags))[0]

    def run(self, kernel, outs, args, grid, in_specs, out_specs, scratch=(), flops=0, limit=20, stream=False):
        nbytes = sum(math.prod(a.shape) * a.dtype.itemsize for a in args) + sum(
            math.prod(o.shape) * o.dtype.itemsize for o in outs
        )
        args = [
            pltpu.with_memory_space_constraint(arg, pltpu.HBM)
            if stream and spec.block_shape != arg.shape
            else arg
            for arg, spec in zip(args, in_specs)
        ]
        results = pl.pallas_call(
            kernel,
            out_shape=outs,
            grid_spec=pltpu.PrefetchScalarGridSpec(
                num_scalar_prefetch=1,
                grid=grid,
                in_specs=in_specs,
                out_specs=out_specs,
                scratch_shapes=list(scratch),
            ),
            compiler_params=pltpu.CompilerParams(
                dimension_semantics=("arbitrary",) * len(grid), vmem_limit_bytes=limit * MIB
            ),
            cost_estimate=pl.CostEstimate(
                flops=int(flops), bytes_accessed=int(nbytes), transcendentals=0
            ),
        )(self.flags, *args)
        self.after(results[0])
        return results


START, CORE, CHIP = 0, 1, 2


def front_kernel(flags, tokens, gain, wq, wk, wv, normed, queries, pair):
    @pl.when(pl.program_id(0) == 0)
    def _():
        inputs = tokens[...].astype(F32)
        normed[...] = (inputs * rms_scale(inputs) * gain[...]).astype(BF)

    rows = normed[...]
    queries[...] = product(rows, wq[...]).astype(BF)
    pair[0] = product(rows, wk[...]).astype(BF)
    pair[1] = product(rows, wv[...]).astype(BF)


def front(clock, tokens, gain, wq, wk, wv):
    step = 256
    column = pl.BlockSpec((D, step), lambda j, *_: (0, j))
    return clock.run(
        front_kernel,
        (shape((W, D), BF), shape((W, D), BF), shape((2, W, D), BF)),
        (tokens, gain, wq, wk, wv),
        (D // step,),
        [whole((W, D)), whole((1, D)), column, column, column],
        (
            whole((W, D)),
            pl.BlockSpec((W, step), lambda j, *_: (0, j)),
            pl.BlockSpec((2, W, step), lambda j, *_: (0, 0, j)),
        ),
        flops=6 * W * D * D,
        stream=True,
    )


def left_kernel(flags, tokens, gain, wk, wv, pair, normed):
    @pl.when(pl.program_id(0) == 0)
    def _():
        inputs = tokens[...].astype(F32)
        normed[...] = (inputs * rms_scale(inputs) * gain[...]).astype(BF)

    rows = normed[...]
    pair[0] = product(rows, wk[...]).astype(BF)
    pair[1] = product(rows, wv[...]).astype(BF)


def left_pair(clock, tokens, gain, wk, wv):
    step = 256
    column = pl.BlockSpec((D, step), lambda j, *_: (0, j))
    return clock.run(
        left_kernel,
        (shape((2, W, D), BF),),
        (tokens, gain, wk, wv),
        (D // step,),
        [whole((W, D)), whole((1, D)), column, column],
        (pl.BlockSpec((2, W, step), lambda j, *_: (0, 0, j)),),
        [pltpu.VMEM((W, D), BF)],
        flops=LONG,
    )[0]


def summary_probs_of(keys, asks):
    raw = product_nt(keys, asks) * SCALE_LOG2
    expos = jnp.exp2(raw - jnp.max(raw, axis=0, keepdims=True))
    return expos, jnp.sum(expos, axis=0, keepdims=True)


def gates_kernel(
    flags, asks, pair, wu, wg, bias, initial, summary, forget, update, give, own, work
):
    step = pl.program_id(0)

    @pl.when(step < 4)
    def _():
        for head in range(2):
            at = slice(head * HEAD_DIM, (head + 1) * HEAD_DIM)
            expos, total = summary_probs_of(pair[0, :, at], asks[:, at])
            held = product_tn(pair[1, :, at], expos.astype(BF)) / total
            place = pl.multiple_of(step * 256 + head * HEAD_DIM, HEAD_DIM)
            summary[:, pl.ds(place, HEAD_DIM)] = held.T.astype(BF)

    @pl.when(step >= 4)
    def _():
        start = flags[START].astype(F32)
        rows = summary[...]
        fresh = product(rows, wu[...])
        gate = jax.nn.sigmoid(product(rows, wg[...]) + bias[...])
        update[...] = fresh
        forget[...] = gate
        work[0] = (1.0 - start) * gate
        work[1] = start * gate * initial[...] + (1.0 - gate) * fresh
        mine = pl.multiple_of(flags[CORE] * HALF, HALF)
        others = pl.multiple_of((1 - flags[CORE]) * HALF, HALF)
        for part in range(2):
            own[part] = work[part, pl.ds(mine, HALF)].astype(BF)
            give[part] = work[part, pl.ds(others, HALF)].astype(BF)


def gates(clock, asks, pair, state_weight, bias, initial):
    step = 256
    early = lambda i, *_: (0, jnp.minimum(i, 3))
    late = lambda i, *_: (0, jnp.maximum(i - 4, 0))
    late3 = lambda i, *_: (0, 0, jnp.maximum(i - 4, 0))
    return clock.run(
        gates_kernel,
        (
            shape((NS, D), BF),
            shape((NS, D), F32),
            shape((NS, D), F32),
            shape((2, HALF, D), BF),
            shape((2, HALF, D), BF),
        ),
        (asks, pair, state_weight, state_weight, bias, initial),
        (8,),
        [
            pl.BlockSpec((NS, step), early),
            pl.BlockSpec((2, W, step), lambda i, *_: (0, 0, jnp.minimum(i, 3))),
            pl.BlockSpec((D, step), late),
            pl.BlockSpec((D, step), lambda i, *_: (0, jnp.maximum(i - 4, 0) + D // step)),
            pl.BlockSpec((1, step), late),
            pl.BlockSpec((NS, step), late),
        ],
        (
            whole((NS, D)),
            pl.BlockSpec((NS, step), late),
            pl.BlockSpec((NS, step), late),
            pl.BlockSpec((2, HALF, step), late3),
            pl.BlockSpec((2, HALF, step), late3),
        ),
        [pltpu.VMEM((2, NS, step), F32)],
        flops=4 * NS * W * D + 4 * NS * D * D,
    )


def rows_of(chip):
    return pl.ds(pl.multiple_of(chip * QUARTER, QUARTER), QUARTER)


def compose_kernel(flags, own, recv, keep, to1, to2, to3, work):
    odd_core = flags[CORE] == 1
    pick2 = lambda part: (own[part].astype(F32), recv[part].astype(F32))
    (own_scale, recv_scale), (own_base, recv_base) = pick2(0), pick2(1)
    later_scale = jnp.where(odd_core, own_scale, recv_scale)
    earlier_base = jnp.where(odd_core, recv_base, own_base)
    later_base = jnp.where(odd_core, own_base, recv_base)
    work[0] = own_scale * recv_scale
    work[1] = later_scale * earlier_base + later_base
    for far, out in enumerate((keep, to1, to2, to3)):
        out[...] = work[:, rows_of(flags[CHIP] ^ far)].astype(BF)


def prefix_kernel(flags, keep, from1, from2, from3, mine, to1, to2, to3, got, enter):
    for far, came in enumerate((keep, from1, from2, from3)):
        got[flags[CHIP] ^ far] = came[...].astype(F32)
    state = got[0, 1]
    enter[0] = jnp.zeros_like(state)
    enter[1] = state
    for chip in (1, 2):
        state = got[chip, 0] * state + got[chip, 1]
        enter[chip + 1] = state
    for far, out in enumerate((mine, to1, to2, to3)):
        out[...] = enter[flags[CHIP] ^ far].astype(BF)


def previous_kernel(flags, mine, from1, from2, from3, own, recv, keep, give, before):
    for far, came in enumerate((mine, from1, from2, from3)):
        before[rows_of(flags[CHIP] ^ far)] = came[...].astype(F32)
    odd_core = flags[CORE] == 1
    scale = jnp.where(odd_core, recv[0].astype(F32), own[0].astype(F32))
    base = jnp.where(odd_core, recv[1].astype(F32), own[1].astype(F32))
    entry = before[...]
    between = scale * entry + base
    keep[...] = jnp.where(odd_core, between, entry).astype(BF)
    give[...] = jnp.where(odd_core, entry, between).astype(BF)


def compose_back_kernel(flags, own, recv, own_pair, recv_pair, keep, to1, to2, to3, work):
    odd_core = flags[CORE] == 1
    scale = jnp.where(odd_core, recv_pair[0].astype(F32), own_pair[0].astype(F32))
    mine, other = own[...].astype(F32), recv[...].astype(F32)
    work[...] = scale * jnp.where(odd_core, mine, other) + jnp.where(odd_core, other, mine)
    for far, out in enumerate((keep, to1, to2, to3)):
        out[...] = work[rows_of(flags[CHIP] ^ far)].astype(BF)


def suffix_kernel(
    flags, keep, from1, from2, from3, kept0, kept1, kept2, kept3, mine, to1, to2, to3, got, enter
):
    pairs = ((keep, kept0), (from1, kept1), (from2, kept2), (from3, kept3))
    for far, (came, kept) in enumerate(pairs):
        got[flags[CHIP] ^ far, 0] = kept[0].astype(F32)
        got[flags[CHIP] ^ far, 1] = came[...].astype(F32)
    state = got[3, 1]
    enter[3] = jnp.zeros_like(state)
    enter[2] = state
    for chip in (2, 1):
        state = got[chip, 0] * state + got[chip, 1]
        enter[chip - 1] = state
    for far, out in enumerate((mine, to1, to2, to3)):
        out[...] = enter[flags[CHIP] ^ far].astype(BF)


def following_kernel(
    flags, mine, from1, from2, from3, own, recv, own_pair, recv_pair, keep, give, after
):
    for far, came in enumerate((mine, from1, from2, from3)):
        after[rows_of(flags[CHIP] ^ far)] = came[...].astype(F32)
    odd_core = flags[CORE] == 1
    scale = jnp.where(odd_core, own_pair[0].astype(F32), recv_pair[0].astype(F32))
    base = jnp.where(odd_core, own[...].astype(F32), recv[...].astype(F32))
    entry = after[...]
    between = scale * entry + base
    keep[...] = jnp.where(odd_core, entry, between).astype(BF)
    give[...] = jnp.where(odd_core, between, entry).astype(BF)


def small(clock, kernel, outs, args, scratch):
    return clock.run(
        kernel,
        tuple(shape(dims, BF) for dims in outs),
        args,
        (1,),
        [whole(a.shape) for a in args],
        tuple(whole(dims) for dims in outs),
        [pltpu.VMEM(dims, F32) for dims in scratch],
        limit=10,
    )


def to_chips(values):
    return (values[0],) + tuple(
        swapped(value, "seq", 2 * far) for far, value in zip((1, 2, 3), values[1:])
    )


PAIR_WORK = [(4, 2, QUARTER, D), (4, QUARTER, D)]


def compose(clock, own, recv):
    return to_chips(small(clock, compose_kernel, [(2, QUARTER, D)] * 4, (own, recv), [(2, HALF, D)]))


def prefix(clock, got):
    return to_chips(small(clock, prefix_kernel, [(QUARTER, D)] * 4, got, PAIR_WORK))


def previous(clock, back, own, recv):
    mine, other = small(
        clock, previous_kernel, [(HALF, D)] * 2, back + (own, recv), [(HALF, D)]
    )
    return mine, swapped(other, "seq", 1)


def compose_back(clock, *args):
    return to_chips(small(clock, compose_back_kernel, [(QUARTER, D)] * 4, args, [(HALF, D)]))


def suffix(clock, got, kept):
    return to_chips(small(clock, suffix_kernel, [(QUARTER, D)] * 4, got + kept, PAIR_WORK))


def following(clock, back, *args):
    mine, other = small(clock, following_kernel, [(HALF, D)] * 2, back + args, [(HALF, D)])
    return mine, swapped(other, "seq", 1)


def state_kernel(
    flags, mine, other, initial, forget, update, wk, wv, state_in, state_low, state_out, pair
):
    @pl.when(pl.program_id(0) == 0)
    def _():
        start = flags[START].astype(F32)
        for core, came in ((flags[CORE], mine), (1 - flags[CORE], other)):
            rows = pl.ds(pl.multiple_of(core * HALF, HALF), HALF)
            entry = (1.0 - start) * came[...].astype(F32) + start * initial[rows, :]
            gate = forget[rows, :]
            state_in[rows, :] = entry
            state_low[rows, :] = entry.astype(BF)
            state_out[rows, :] = gate * entry + (1.0 - gate) * update[rows, :]

    rows = state_low[...]
    pair[0] = product(rows, wk[...]).astype(BF)
    pair[1] = product(rows, wv[...]).astype(BF)


def state_pair(clock, mine, other, initial, forget, update, wk, wv):
    step = 256
    column = pl.BlockSpec((D, step), lambda j, *_: (0, j))
    return clock.run(
        state_kernel,
        (shape((NS, D), F32), shape((NS, D), BF), shape((NS, D), F32), shape((2, NS, D), BF)),
        (mine, other, initial, forget, update, wk, wv),
        (D // step,),
        [whole((HALF, D))] * 2 + [whole((NS, D))] * 3 + [column, column],
        (
            whole((NS, D)),
            whole((NS, D)),
            whole((NS, D)),
            pl.BlockSpec((2, NS, step), lambda j, *_: (0, 0, j)),
        ),
        flops=4 * NS * D * D,
    )


def masked_scores(flags, queries, left, own, state):
    seen = []
    left_bias = jnp.where(flags[START] == 0, 0.0, NEGATIVE).astype(F32)
    seen.append(product_nt(left[0], queries) * SCALE_LOG2 + left_bias)
    rows = lax.broadcasted_iota(jnp.int32, (W, W), 0)
    cols = lax.broadcasted_iota(jnp.int32, (W, W), 1)
    seen.append(jnp.where(rows <= cols, product_nt(own[0], queries) * SCALE_LOG2, NEGATIVE))
    seen.append(product_nt(state[0], queries) * SCALE_LOG2)
    return seen


PER_STEP = 2


def each_head(*refs):
    for head in range(PER_STEP):
        at = pl.ds(head * HEAD_DIM, HEAD_DIM)
        yield head, [ref.at[..., at] for ref in refs]


def attend_kernel(flags, *refs):
    lse = refs[-1]
    for head, (queries, left, own, state, attended) in each_head(*refs[:-1]):
        seen = masked_scores(flags, queries[...], left, own, state)
        peak = functools.reduce(
            jnp.maximum, [jnp.max(part, axis=0, keepdims=True) for part in seen]
        )
        held = 0.0
        total = 0.0
        for part, pair in zip(seen, (left, own, state)):
            expos = jnp.exp2(part - peak)
            total = total + jnp.sum(expos, axis=0, keepdims=True)
            held = held + product_tn(pair[1], expos.astype(BF))
        attended[...] = (held / total).T.astype(BF)
        lse[head] = peak + jnp.log2(total)


HEADS_WIDE = PER_STEP * HEAD_DIM


def attend(clock, queries, left, own, state):
    head = pl.BlockSpec((W, HEADS_WIDE), lambda h, *_: (0, h))
    pair = pl.BlockSpec((2, W, HEADS_WIDE), lambda h, *_: (0, 0, h))
    return clock.run(
        attend_kernel,
        (shape((W, D), BF), shape((HEADS, 1, W), F32)),
        (queries, left, own, state),
        (HEADS // PER_STEP,),
        [head, pair, pair, pair],
        (head, pl.BlockSpec((PER_STEP, 1, W), lambda h, *_: (h, 0, 0))),
        flops=4 * W * (2 * W + NS) * D,
        stream=True,
        limit=26,
    )


def attend_back_kernel(flags, queries, left, own, state, grad, lse, *outs):
    for head, (asks, left_h, own_h, state_h, grad_h, queries_grad, *grads) in each_head(
        queries, left, own, state, grad, *outs
    ):
        asks, out_grad = asks[...], grad_h[...]
        pairs = (left_h, own_h, state_h)
        seen = masked_scores(flags, asks, *pairs)
        probs = [jnp.exp2(part - lse[head]) for part in seen]
        prob_grads = [product_nt(pair[1], out_grad) for pair in pairs]
        rowdot = sum(
            jnp.sum(prob * prob_grad, axis=0, keepdims=True)
            for prob, prob_grad in zip(probs, prob_grads)
        )
        total = 0.0
        for prob, prob_grad, pair, out in zip(probs, prob_grads, pairs, grads):
            score_grad = (prob * (prob_grad - rowdot)).astype(BF)
            out[0] = (product(score_grad, asks) * SCALE).astype(out.dtype)
            out[1] = product(prob.astype(BF), out_grad).astype(out.dtype)
            total = total + product_tn(pair[0], score_grad)
        queries_grad[...] = (total * SCALE).T.astype(BF)


def attend_back(clock, queries, left, own, state, grad, lse):
    head = pl.BlockSpec((W, HEADS_WIDE), lambda h, *_: (0, h))
    pair = pl.BlockSpec((2, W, HEADS_WIDE), lambda h, *_: (0, 0, h))
    return clock.run(
        attend_back_kernel,
        (shape((W, D), BF), shape((2, W, D), BF), shape((2, W, D), F32), shape((2, NS, D), BF)),
        (queries, left, own, state, grad, lse),
        (HEADS // PER_STEP,),
        [head, pair, pair, pair, head, pl.BlockSpec((PER_STEP, 1, W), lambda h, *_: (h, 0, 0))],
        (head, pair, pair, pair),
        flops=10 * W * (2 * W + NS) * D,
        stream=True,
        limit=36,
    )


def gelu_parts(upper):
    square = upper * upper
    inner = GELU_SCALE * (upper + GELU_CUBIC * square * upper)
    bent = jnp.tanh(inner)
    value = 0.5 * upper * (1.0 + bent)
    slope = 0.5 * (1.0 + bent) + 0.5 * upper * (1.0 - bent * bent) * GELU_SCALE * (
        1.0 + 3.0 * GELU_CUBIC * square
    )
    return value, slope


def mlp_step(normed_mlp, come, up1, up2, down, up, activated, upper_grad, total, grad):
    half = up1.shape[1]
    up[:, :half] = up1[...]
    up[:, half:] = up2[...]
    rows = down[...].reshape(2 * half, D)
    value, slope = gelu_parts(product(normed_mlp[...], up[...]))
    value = value.astype(BF)
    activated[...] = value
    total[...] += product(value, rows)
    back = (come[...].astype(F32) * slope).astype(BF)
    upper_grad[...] = back
    grad[...] += product_nt(back, up[...])


def come_kernel(flags, cotangent, down1, down2, come1, come2):
    for down, come in ((down1, come1), (down2, come2)):
        rows = down[...].reshape(come.shape[1], D)
        come[...] = product_nt(cotangent[...], rows).astype(BF)


def come_back(clock, cotangent, down):
    return clock.run(
        come_kernel,
        (shape((W, FF // 2), BF),) * 2,
        (cotangent, down, down),
        (PAIRS,),
        [fixed((W, D)), mlp_specs(0)[2], mlp_specs(1)[2]],
        (mlp_halves(),) * 2,
        flops=2 * W * D * FF,
    )


def mlp_first_kernel(
    flags,
    attended,
    tokens,
    out_weight,
    gain,
    come,
    up1,
    up2,
    down,
    activated,
    upper_grad,
    normed_mlp,
    hidden,
    total,
    grad,
    up,
):
    @pl.when(pl.program_id(0) == 0)
    def _():
        field = tokens[...].astype(F32) + product(attended[...], out_weight[...])
        hidden[...] = field
        normed_mlp[...] = (field * rms_scale(field) * gain[...]).astype(BF)
        total[...] = field
        grad[...] = jnp.zeros_like(field)

    mlp_step(normed_mlp, come, up1, up2, down, up, activated, upper_grad, total, grad)


def mlp_second_kernel(
    flags,
    normed_mlp,
    hidden,
    total_in,
    grad_in,
    out_weight,
    gain,
    cotangent,
    come,
    up1,
    up2,
    down,
    activated,
    upper_grad,
    mixed,
    hidden_grad,
    attended_grad,
    heads_grad,
    gain_grad,
    total,
    grad,
    up,
):
    step = pl.program_id(0)

    @pl.when(step == 0)
    def _():
        total[...] = total_in[...]
        grad[...] = grad_in[...]

    mlp_step(normed_mlp, come, up1, up2, down, up, activated, upper_grad, total, grad)

    @pl.when(step == pl.num_programs(0) - 1)
    def _():
        mixed[...] = total[...].astype(BF)
        field = hidden[...]
        scaled = rms_scale(field)
        gain_grad[...] = jnp.sum(grad[...] * field * scaled, axis=0, keepdims=True)
        weighted = grad[...] * gain[...]
        field_grad = (
            cotangent[...].astype(F32)
            + scaled * weighted
            - field
            * (scaled * scaled * scaled * jnp.mean(weighted * field, axis=-1, keepdims=True))
        )
        hidden_grad[...] = field_grad
        low = field_grad.astype(BF)
        attended_grad[...] = low
        heads_grad[...] = product_nt(low, out_weight[...]).astype(BF)


PIECE = 256
PAIRS = FF // (4 * PIECE)


def mlp_specs(part):
    return [
        pl.BlockSpec((D, PIECE), lambda j, *_: (0, 4 * j + part)),
        pl.BlockSpec((D, PIECE), lambda j, *_: (0, 4 * j + 2 + part)),
        pl.BlockSpec((2, PIECE, D), lambda j, *_: (j, part, 0)),
    ]


def mlp_halves():
    return pl.BlockSpec((W, 2 * PIECE), lambda j, *_: (0, j))


def mlp_first(clock, attended, tokens, out_weight, gain, come, up, down):
    rows = whole((W, D))
    return clock.run(
        mlp_first_kernel,
        (
            shape((W, FF // 2), BF),
            shape((W, FF // 2), BF),
            shape((W, D), BF),
            shape((W, D), F32),
            shape((W, D), F32),
            shape((W, D), F32),
        ),
        (attended, tokens, out_weight, gain, come, up, up, down),
        (PAIRS,),
        [fixed((W, D)), fixed((W, D)), fixed((D, D)), fixed((1, D)), mlp_halves()] + mlp_specs(0),
        (mlp_halves(), mlp_halves(), rows, rows, rows, rows),
        [pltpu.VMEM((D, 2 * PIECE), BF)],
        flops=3 * W * D * FF + 2 * W * D * D,
        limit=36,
    )


def mlp_second(
    clock, normed_mlp, hidden, total, grad, out_weight, gain, cotangent, come, up, down
):
    rows = whole((W, D))
    return clock.run(
        mlp_second_kernel,
        (
            shape((W, FF // 2), BF),
            shape((W, FF // 2), BF),
            shape((W, D), BF),
            shape((W, D), F32),
            shape((W, D), BF),
            shape((W, D), BF),
            shape((1, D), F32),
        ),
        (normed_mlp, hidden, total, grad, out_weight, gain, cotangent, come, up, up, down),
        (PAIRS,),
        [fixed((W, D))] * 4
        + [fixed((D, D)), fixed((1, D)), fixed((W, D)), mlp_halves()]
        + mlp_specs(1),
        (mlp_halves(), mlp_halves(), rows, rows, rows, rows, whole((1, D))),
        [pltpu.VMEM((W, D), F32), pltpu.VMEM((W, D), F32), pltpu.VMEM((D, 2 * PIECE), BF)],
        flops=3 * W * D * FF + 2 * W * D * D,
        limit=36,
    )


def direct_kernel(flags, state_grad, wk, wv, forget, cotangent, direct, own, give, work):
    grad = product_nt(state_grad[0], wk[...]) + product_nt(state_grad[1], wv[...])
    direct[...] = grad
    keep = 1.0 - flags[START].astype(F32)
    work[...] = keep * (forget[...] * cotangent[...] + grad)
    own[...] = work[pl.ds(pl.multiple_of(flags[CORE] * HALF, HALF), HALF)].astype(BF)
    give[...] = work[pl.ds(pl.multiple_of((1 - flags[CORE]) * HALF, HALF), HALF)].astype(BF)


def direct_grad(clock, state_grad, wk, wv, forget, cotangent):
    step = 256
    row = pl.BlockSpec((step, D), lambda j, *_: (j, 0))
    column = pl.BlockSpec((NS, step), lambda j, *_: (0, j))
    half = pl.BlockSpec((HALF, step), lambda j, *_: (0, j))
    return clock.run(
        direct_kernel,
        (shape((NS, D), F32), shape((HALF, D), BF), shape((HALF, D), BF)),
        (state_grad, wk, wv, forget, cotangent),
        (D // step,),
        [whole((2, NS, D)), row, row, column, column],
        (column, half, half),
        [pltpu.VMEM((NS, step), F32)],
        flops=4 * NS * D * D,
    )


def state_back_kernel(
    flags,
    mine,
    other,
    cotangent,
    forget,
    update,
    state_in,
    direct,
    wu,
    wg,
    initial_grad,
    projected_grad,
    bias_grad,
    summary_grad,
    work,
    total,
):
    step = pl.program_id(0)
    for core, came in ((flags[CORE], mine), (1 - flags[CORE], other)):
        work[pl.ds(pl.multiple_of(core * HALF, HALF), HALF)] = came[...].astype(F32)
    out_grad = cotangent[...] + work[...]
    gate = forget[...]
    start = flags[START].astype(F32)
    initial_grad[...] = (start * (gate * out_grad + direct[...])).astype(BF)
    rest = 1.0 - gate
    gate_grad = out_grad * (state_in[...] - update[...]) * gate * rest
    bias_grad[...] = jnp.sum(gate_grad, axis=0, keepdims=True)
    fresh_grad = (out_grad * rest).astype(BF)
    gate_low = gate_grad.astype(BF)
    projected_grad[0] = fresh_grad
    projected_grad[1] = gate_low
    part = product_nt(fresh_grad, wu[...]) + product_nt(gate_low, wg[...])

    @pl.when(step == 0)
    def _():
        total[...] = part

    @pl.when(step > 0)
    def _():
        total[...] += part

    @pl.when(step == pl.num_programs(0) - 1)
    def _():
        summary_grad[...] = total[...].astype(BF)


def state_back(clock, mine, other, cotangent, forget, update, state_in, direct, state_weight):
    step = 256
    column = pl.BlockSpec((NS, step), lambda j, *_: (0, j))
    half = pl.BlockSpec((HALF, step), lambda j, *_: (0, j))
    return clock.run(
        state_back_kernel,
        (
            shape((NS, D), BF),
            shape((2, NS, D), BF),
            shape((1, D), F32),
            shape((NS, D), BF),
        ),
        (mine, other, cotangent, forget, update, state_in, direct, state_weight, state_weight),
        (D // step,),
        [half, half, column, column, column, column, column]
        + [
            pl.BlockSpec((D, step), lambda j, *_: (0, j)),
            pl.BlockSpec((D, step), lambda j, *_: (0, j + D // step)),
        ],
        (
            column,
            pl.BlockSpec((2, NS, step), lambda j, *_: (0, 0, j)),
            pl.BlockSpec((1, step), lambda j, *_: (0, j)),
            whole((NS, D)),
        ),
        [pltpu.VMEM((NS, step), F32), pltpu.VMEM((NS, D), F32)],
        flops=4 * NS * D * D,
    )


def summary_back_kernel(flags, *refs):
    for _, (asks, pair, grad, own_grad, asks_grad, pair_total) in each_head(*refs):
        queries, out_grad = asks[...], grad[...]
        expos, total = summary_probs_of(pair[0], queries)
        probs = expos * (1.0 / total)
        prob_grad = product_nt(pair[1], out_grad)
        rowdot = jnp.sum(probs * prob_grad, axis=0, keepdims=True)
        score_grad = (probs * (prob_grad - rowdot)).astype(BF)
        asks_grad[...] = (product_tn(pair[0], score_grad) * SCALE).T.astype(BF)
        pair_total[0] = (own_grad[0] + product(score_grad, queries) * SCALE).astype(BF)
        pair_total[1] = (own_grad[1] + product(probs.astype(BF), out_grad)).astype(BF)


def summary_back(clock, asks, pair, grad, own_grad):
    head = pl.BlockSpec((W, HEADS_WIDE), lambda h, *_: (0, h))
    both = pl.BlockSpec((2, W, HEADS_WIDE), lambda h, *_: (0, 0, h))
    return clock.run(
        summary_back_kernel,
        (shape((NS, D), BF), shape((2, W, D), BF)),
        (asks, pair, grad, own_grad),
        (HEADS // PER_STEP,),
        [head, both, head, both],
        (head, both),
        flops=10 * NS * W * D,
        stream=True,
    )


def tokens_back_kernel(
    flags,
    queries_grad,
    pair_total,
    returned,
    wq,
    wk,
    wv,
    tokens,
    gain,
    hidden_grad,
    tokens_grad,
    gain_grad,
    total,
):
    step = pl.program_id(0)

    @pl.when(step < 2)
    def _():
        part = product_nt(queries_grad[...], wq[...])
        total[...] = jnp.where(step == 0, part, total[...] + part)

    @pl.when((step >= 2) & (step < 4))
    def _():
        total[...] += product_nt(add_low(pair_total[0], returned[0]), wk[...])

    @pl.when(step >= 4)
    def _():
        total[...] += product_nt(add_low(pair_total[0], returned[0]), wv[...])

    @pl.when(step == 5)
    def _():
        inputs = tokens[...].astype(F32)
        scaled = rms_scale(inputs)
        grad = total[...]
        gain_grad[...] = jnp.sum(grad * inputs * scaled, axis=0, keepdims=True)
        weighted = grad * gain[...]
        tokens_grad[...] = (
            hidden_grad[...]
            + scaled * weighted
            - inputs
            * (scaled * scaled * scaled * jnp.mean(weighted * inputs, axis=-1, keepdims=True))
        )


def tokens_back(clock, queries_grad, pair_total, returned, wq, wk, wv, tokens, gain, hidden_grad):
    step = D // 2
    clamp = lambda i, low: jnp.clip(i - low, 0, 1)
    weight = lambda low: pl.BlockSpec((D, step), lambda i, *_: (0, clamp(i, low)))
    later = lambda i: jnp.maximum(i - 2, 0)
    pair = pl.BlockSpec((1, W, step), lambda i, *_: (later(i) // 2, 0, later(i) % 2))
    return clock.run(
        tokens_back_kernel,
        (shape((W, D), F32), shape((1, D), F32)),
        (queries_grad, pair_total, returned, wq, wk, wv, tokens, gain, hidden_grad),
        (6,),
        [
            pl.BlockSpec((W, step), lambda i, *_: (0, clamp(i, 0))),
            pair,
            pair,
            weight(0),
            weight(2),
            weight(4),
            fixed((W, D)),
            fixed((1, D)),
            fixed((W, D)),
        ],
        (whole((W, D)), whole((1, D))),
        [pltpu.VMEM((W, D), F32)],
        flops=6 * W * D * D,
    )


def chunk_natural(flags, place):
    return place


def chunk_along_x(flags, place):
    x = flags[CHIP] & 1
    return 2 * (place % 2) + (1 - x if place < 2 else x)


def chunk_along_y(flags, place):
    y = flags[CHIP] >> 1
    return 2 * (1 - y if place < 2 else y) + place % 2


def column_blocks(terms):
    return terms[0][1][0][0].shape[2] // D


def weight_kernel(plan, merge, flags, *refs):
    refs = list(refs)
    lefts = [refs.pop(0) for _ in range(plan["lefts"])]
    rights = [[refs.pop(0) for _ in adds] for adds in plan["rights"]]
    extras = [refs.pop(0) for _ in range(plan["extras"])]
    recv = refs.pop(0) if merge else None
    work = refs.pop()
    core = flags[CORE] if merge else 1 - flags[CORE]
    step, base, start = pl.program_id(0), 0, 0

    def write(along, place, at, here, part):
        rows = part.shape[0]
        if merge:
            chunk = (chunk_along_x, chunk_along_y)[along](flags, place)
            part = part.astype(F32) + recv[chunk, at : at + rows].astype(F32)
            refs[2 * along + place // 2][place % 2, here : here + rows] = part.astype(BF)
        else:
            refs[0][place, at : at + rows] = part.astype(BF)

    def source(along, place):
        chunk_of = (chunk_along_x, chunk_along_y)[along] if merge else chunk_natural
        return 2 * chunk_of(flags, place) + core

    for along, group in enumerate(plan["grads"]):
        here = 0
        for rows, blocks, terms in group:

            @pl.when(step == base)
            def _():
                for term, (left, _) in enumerate(terms):
                    for place in range(4):
                        first = pl.multiple_of(source(along, place) * rows, rows)
                        block = lefts[left][:, pl.ds(first, rows)]
                        work[term, place * rows : (place + 1) * rows] = block.T

            for block in range(blocks):

                @pl.when(step == base + block)
                def _():
                    total = 0.0
                    for term, (_, right) in enumerate(terms):
                        parts = [part[0] for part in rights[right]]
                        value = parts[0] if len(parts) == 1 else add_low(*parts)
                        total = total + product(work[term, : 4 * rows], value)
                    at = block * rows
                    for place in range(4):
                        part = total[place * rows : (place + 1) * rows]
                        write(along, place, start + at, here + at, part)

            base += blocks
            start += blocks * rows
            here += blocks * rows
        if extras:
            rows = extras[along].shape[0] // 8

            @pl.when(step == 0)
            def _():
                for place in range(4):
                    first = pl.multiple_of(source(along, place) * rows, rows)
                    write(along, place, start, here, extras[along][pl.ds(first, rows)])

            start += rows


def weight_pair(clock, grads, extras, recv):
    lefts, left_ids, rights, args, specs, plans = [], {}, [], [], [], []
    base, start, tokens, most = 0, 0, grads[0][0][0][0].shape[0], 0
    sizes = []
    for along, group in enumerate(grads):
        total, plan = 0, []
        for terms in group:
            rows, blocks = terms[0][0].shape[1] // 8, column_blocks(terms)
            most = max(most, rows)
            steps = []
            for left, adds in terms:
                if id(left) not in left_ids:
                    left_ids[id(left)] = len(lefts)
                    lefts.append(left)
                steps.append((left_ids[id(left)], len(rights)))
                rights.append(tuple(index for _, index in adds))
                for right, index in adds:
                    args.append(right)
                    specs.append(
                        pl.BlockSpec(
                            (1, tokens, D),
                            lambda j, *_, index=index, base=base, blocks=blocks: (
                                index,
                                0,
                                jnp.clip(j - base, 0, blocks - 1),
                            ),
                        )
                    )
            plan.append((rows, blocks, steps))
            base += blocks
            total += blocks * rows
        if extras:
            total += extras[along].shape[0] // 8
        plans.append(plan)
        sizes.append(total)
        start += total
    if extras and recv is not None:
        args = [pltpu.with_memory_space_constraint(arg, pltpu.HBM) for arg in args]
    args = lefts + args + list(extras)
    specs = [fixed(left.shape) for left in lefts] + specs + [fixed(e.shape) for e in extras]
    merge = recv is not None
    if merge:
        args.append(recv)
        specs.append(fixed(recv.shape))
        dims = [(2, total, D) for total in sizes for _ in range(2)]
    else:
        dims = [(4, start, D)]
    plan = {"lefts": len(lefts), "rights": rights, "extras": len(extras), "grads": plans}
    return clock.run(
        functools.partial(weight_kernel, plan, merge),
        tuple(shape(d, BF) for d in dims),
        tuple(args),
        (base,),
        specs,
        tuple(whole(d) for d in dims),
        [pltpu.VMEM((len(grads[0][0]), 4 * most, tokens), BF)],
        flops=2 * tokens * 4 * start * D * len(grads[0][0]),
        limit=24,
    )


def scatter_bits(value, bits, names):
    place = lax.axis_index("seq")
    names = list(names)
    for bit in bits:
        at = names.index(bit)
        mine = (place >> bit) & 1
        recv = swapped(pick(value, 1 - mine, at), "seq", 1 << bit)
        value = add_low(pick(value, mine, at), recv)
        names.pop(at)
    return value


def whole_scatter(value, along_x):
    count = lax.axis_size("seq")
    levels = count.bit_length() - 1
    names = list(range(levels - 1, -1, -1))
    value = value.reshape((2,) * levels + (value.shape[0] // count,) + value.shape[1:])
    bits = [0] + (names[-2::-1] if along_x else names[:-1])
    return scatter_bits(value, bits, names)


def in_rows(value):
    return jnp.concatenate([value[:, at : at + D] for at in range(0, value.shape[1], D)], axis=0)


def turn_kernel(flags, kept1, recv1, kept2, recv2, send1, send2):
    send1[...] = add_low(kept1[0], recv1[0])
    send2[...] = add_low(kept2[0], recv2[0])


def pack_kernel(flags, *refs):
    out, start = refs[-1], 0
    for at in range(0, len(refs) - 1, 3):
        kept, recv, last = refs[at : at + 3]
        rows = last.shape[0]
        out[start : start + rows] = add_low(kept[0], recv[0], last[...])
        start += rows


class Scatter:
    def __init__(self, clock, firsts, seconds, extras=()):
        self.grads, self.extras, self.plain = (firsts, seconds), extras, None
        if lax.axis_size("seq") != 8:
            sums = []
            for number, group in enumerate(self.grads):
                for terms in group:
                    total = 0.0
                    for left, adds in terms:
                        parts = [right[index] for right, index in adds]
                        right = add_low(*parts) if len(parts) > 1 else parts[0]
                        total = total + product_tn(left, right)
                    sums.append(in_rows(whole_scatter(total.astype(BF), number == 0)))
                if extras:
                    sums.append(whole_scatter(extras[number], number == 0))
            self.plain = jnp.concatenate(sums, axis=0)
            return
        (self.give,) = weight_pair(clock, self.grads, self.extras, None)

    def core(self, clock):
        if self.plain is None:
            self.recv = swapped(clock.at(self.give), "seq", 1)

    def keep(self, clock):
        if self.plain is None:
            send1, kept1, send2, kept2 = weight_pair(clock, self.grads, self.extras, self.recv)
            self.kept, self.send = (kept1, kept2), (send1, send2)

    def near(self, clock):
        if self.plain is None:
            self.recv = tuple(
                swapped(clock.at(send), "seq", far) for send, far in zip(self.send, (2, 4))
            )

    def held(self, other):
        args, specs = [], []
        for number, (kept, recv) in enumerate(zip(self.kept, self.recv)):
            bit = 1 - number
            mine = lambda i, flags, bit=bit: (((flags[CHIP] >> bit) & 1) ^ other, 0, 0)
            args.append([kept, recv])
            specs.append([pl.BlockSpec((1,) + kept.shape[1:], mine)] * 2)
        return args, specs

    def turn(self, clock, flops=0):
        if self.plain is None:
            args, specs = self.held(1)
            dims = [kept.shape[1:] for kept in self.kept]
            self.send = clock.run(
                turn_kernel,
                tuple(shape(d, BF) for d in dims),
                tuple(args[0] + args[1]),
                (1,),
                specs[0] + specs[1],
                tuple(whole(d) for d in dims),
                flops=flops,
                limit=10,
            )

    def far(self, clock):
        if self.plain is None:
            self.last = tuple(
                swapped(clock.at(send), "seq", far) for send, far in zip(self.send, (4, 2))
            )

    def parts(self):
        args, specs = self.held(0)
        for number, last in enumerate(self.last):
            args[number].append(last)
            specs[number].append(whole(last.shape))
        return args[0] + args[1], specs[0] + specs[1]


def pack(clock, *scatters):
    if scatters[0].plain is not None:
        return jnp.concatenate([scatter.plain for scatter in scatters], axis=0)
    args, specs = [], []
    for scatter in scatters:
        more = scatter.parts()
        args += more[0]
        specs += more[1]
    total = sum(arg.shape[0] for arg in args[2::3])
    args = [pltpu.with_memory_space_constraint(arg, pltpu.HBM) for arg in args]
    return clock.run(
        pack_kernel,
        (shape((total, D), BF),),
        tuple(args),
        (1,),
        specs,
        (whole((total, D)),),
        limit=16,
    )[0]


class Line:
    def __init__(self, clock, value):
        count = lax.axis_size("dp")
        half = count // 2
        self.value = value
        self.rounds = (
            [([(s, s + 1), (count - 1 - s, count - 2 - s)], None) for s in range(half - 1)]
            + [([(half - 1, half), (half, half - 1)], None)]
            + [
                ([(s + 1, s), (count - 2 - s, count - 1 - s)], (s, count - 1 - s))
                for s in range(half - 2, -1, -1)
            ]
        )
        self.send(clock)

    def send(self, clock):
        self.recv = lax.ppermute(clock.at(self.value), "dp", self.rounds[0][0])

    def take(self, clock):
        place = lax.axis_index("dp")
        takers = self.rounds.pop(0)[1]
        value = clock.at(self.value)
        if takers is None:
            self.value = add_low(value, self.recv)
        else:
            outer = (place == takers[0]) | (place == takers[1])
            self.value = jnp.where(outer, self.recv, value)
        if self.rounds:
            clock.after(self.value)

    def step(self, clock):
        self.take(clock)
        if self.rounds:
            self.send(clock)

    def finish(self, clock):
        while self.rounds:
            self.step(clock)
        return self.value.astype(F32)


def interleaved(first, second):
    blocks = []
    for at in range(0, first.shape[1], PIECE):
        blocks += [first[:, at : at + PIECE], second[:, at : at + PIECE]]
    return jnp.concatenate(blocks, axis=1)


def body(
    tokens,
    item_starts,
    attn_gain,
    query_weight,
    key_weight,
    value_weight,
    output_weight,
    state_queries,
    state_weight,
    gate_bias,
    initial_state,
    mlp_gain,
    up_weight,
    down_weight,
    out_cotangent,
    state_cotangent,
):
    count = lax.axis_size("seq")
    place = lax.axis_index("seq")
    clock = Clock(
        jnp.stack([item_starts[0, 0], place & 1, (place >> 1) & 3]).astype(jnp.int32)
    )
    tokens, cotangent, state_cot = tokens[0], out_cotangent[0], state_cotangent[0, 0]
    attn_gain, gate_bias, mlp_gain = attn_gain[None], gate_bias[None], mlp_gain[None]
    down_weight = down_weight.reshape(FF // (2 * PIECE), 2 * PIECE, D)

    tokens_left = shifted(tokens, "seq", 1)
    normed, queries, own = front(clock, tokens, attn_gain, query_weight, key_weight, value_weight)
    summary, forget, update, give_pair, own_pair = gates(
        clock, state_queries, own, state_weight, gate_bias, initial_state
    )
    recv_pair = swapped(give_pair, "seq", 1)
    left = left_pair(clock, tokens_left, attn_gain, key_weight, value_weight)
    kept_chips = compose(clock, own_pair, recv_pair)
    come1, come2 = come_back(clock, cotangent, down_weight)
    back = prefix(clock, kept_chips)
    mine, other = previous(clock, back, own_pair, recv_pair)
    state_in, state_low, state_out, state = state_pair(
        clock, mine, other, initial_state, forget, update, key_weight, value_weight
    )
    attended, lse = attend(clock, queries, left, own, state)
    split = count == 8
    activated1, upper_grad1, normed_mlp, hidden, total, grad = mlp_first(
        clock, attended, tokens, output_weight, mlp_gain, come1, up_weight, down_weight
    )
    out_grads = (cotangent[None], 0)
    if split:
        feed1 = Scatter(
            clock,
            [[(activated1, [out_grads])]],
            [[(normed_mlp, [(upper_grad1[None], 0)])]],
        )
        feed1.core(clock)
        feed1.keep(clock)
        feed1.near(clock)
    activated2, upper_grad2, mixed, hidden_grad, attended_grad, heads_grad, mlp_gain_grad = (
        mlp_second(
            clock,
            normed_mlp,
            hidden,
            total,
            grad,
            output_weight,
            mlp_gain,
            cotangent,
            come2,
            up_weight,
            down_weight,
        )
    )
    if split:
        feed2 = Scatter(
            clock,
            [[(activated2, [out_grads])]],
            [[(normed_mlp, [(upper_grad2[None], 0)])]],
        )
        feed2.core(clock)
        feed1.turn(clock, LONG)
        feed1.far(clock)
        feed2.keep(clock)
        feed2.near(clock)
    else:
        feed1 = Scatter(
            clock,
            [[(interleaved(activated1, activated2), [out_grads])]],
            [[(normed_mlp, [(interleaved(upper_grad1, upper_grad2)[None], 0)])]],
        )
    queries_grad, left_grad, own_grad, state_grad = attend_back(
        clock, queries, left, own, state, heads_grad, lse
    )
    direct, own_base, give_base = direct_grad(
        clock, state_grad, key_weight, value_weight, forget, state_cot
    )
    recv_base = swapped(give_base, "seq", 1)
    line1 = Line(clock, pack(clock, feed1))
    got = compose_back(clock, own_base, recv_base, own_pair, recv_pair)
    if split:
        feed2.turn(clock)
    back = suffix(clock, got, kept_chips)
    mine, other = following(clock, back, own_base, recv_base, own_pair, recv_pair)
    if split:
        feed2.far(clock)
    returned = shifted(clock.at(left_grad), "seq", -1)
    line1.step(clock)
    initial_grad, projected_grad, gate_bias_grad, summary_grad = state_back(
        clock, mine, other, state_cot, forget, update, state_in, direct, state_weight
    )
    others = Scatter(
        clock,
        [[(attended, [(attended_grad[None], 0)])], [(summary, [(projected_grad, 0)])]],
        [[(normed, [(queries_grad[None], 0)])], [(summary, [(projected_grad, 1)])]],
    )
    line2 = Line(clock, pack(clock, feed2)) if split else None
    others.core(clock)
    state_queries_grad, pair_total = summary_back(
        clock, state_queries, own, summary_grad, own_grad
    )
    others.keep(clock)
    if split:
        line2.step(clock)
    others.near(clock)
    line1.take(clock)
    keys_values = Scatter(
        clock,
        [[(normed, [(pair_total, 0), (returned, 0)]), (state_low, [(state_grad, 0)])]],
        [[(normed, [(pair_total, 1), (returned, 1)]), (state_low, [(state_grad, 1)])]],
        (state_queries_grad, initial_grad),
    )
    keys_values.core(clock)
    if line1.rounds:
        line1.send(clock)
    keys_values.keep(clock)
    if split:
        line2.take(clock)
    keys_values.near(clock)
    tokens_grad, attn_gain_grad = tokens_back(
        clock,
        queries_grad,
        pair_total,
        returned,
        query_weight,
        key_weight,
        value_weight,
        tokens,
        attn_gain,
        hidden_grad,
    )
    others.turn(clock)
    others.far(clock)
    line1 = line1.finish(clock)
    clock.after(line1)
    lanes, rows = D // count, NS // count
    vectors = jnp.concatenate([attn_gain_grad, gate_bias_grad, mlp_gain_grad])
    vectors = vectors.reshape(3, count, lanes).transpose(1, 0, 2).reshape(count, 1, 3 * lanes)
    vectors = jnp.pad(vectors, ((0, 0), (0, 7), (0, D - 3 * lanes))).astype(BF)
    keys_values.turn(clock)
    keys_values.far(clock)
    vectors = whole_scatter(clock.at(vectors.reshape(-1, D)), True)
    line3 = [Line(clock, half) for half in jnp.split(pack(clock, others), 2)]
    if split:
        line2.send(clock)
    line4 = Line(clock, jnp.concatenate([pack(clock, keys_values), vectors], axis=0))
    for line in line3 + [line4] + line3 + [line4]:
        line.step(clock)
    line3 = [line.finish(clock) for line in line3]
    line4 = line4.finish(clock)
    clock.after(line3, line4)
    line2 = line2.finish(clock) if split else None

    def unpack(packed, *dims):
        pieces, start = [], 0
        for high, wide in dims:
            parts = [
                packed[start + high * part : start + high * (part + 1)] for part in range(wide // D)
            ]
            start += high * (wide // D)
            pieces.append(parts[0] if len(parts) == 1 else jnp.concatenate(parts, axis=1))
        return pieces

    high, deep = D // count, FF // count
    if split:
        down1, up1 = unpack(line1, (deep // 2, D), (high, FF // 2))
        down2, up2 = unpack(line2, (deep // 2, D), (high, FF // 2))
        down_grad = jnp.concatenate([down1, down2], axis=0)
        up_grad = interleaved(up1, up2)
    else:
        down_grad, up_grad = unpack(line1, (deep, D), (high, FF))
    output_grad, first_grad, query_grad, second_grad = unpack(
        jnp.concatenate(line3),
        (high, D),
        (high, D),
        (high, D),
        (high, D),
    )
    state_weight_grad = jnp.concatenate([first_grad, second_grad], axis=1)
    key_grad, state_queries_grad, value_grad, initial_grad, vectors = unpack(
        line4, (high, D), (rows, D), (high, D), (rows, D), (8, D)
    )
    vectors = vectors[0, : 3 * lanes]
    return (
        mixed[None],
        state_out[None, None],
        tokens_grad[None],
        vectors[:lanes],
        query_grad,
        key_grad,
        value_grad,
        output_grad,
        state_queries_grad,
        state_weight_grad,
        vectors[lanes : 2 * lanes],
        initial_grad,
        vectors[2 * lanes :],
        up_grad,
        down_grad,
    )


def solution(mesh):
    in_specs = (
        P("dp", "seq", None),
        P("dp", "seq"),
        P(),
        P(),
        P(),
        P(),
        P(),
        P(),
        P(),
        P(),
        P(),
        P(),
        P(),
        P(),
        P("dp", "seq", None),
        P("dp", "seq", None, None),
    )
    out_specs = (
        P("dp", "seq", None),
        P("dp", "seq", None, None),
        P("dp", "seq", None),
        P("seq"),
        P("seq", None),
        P("seq", None),
        P("seq", None),
        P("seq", None),
        P("seq", None),
        P("seq", None),
        P("seq"),
        P("seq", None),
        P("seq"),
        P("seq", None),
        P("seq", None),
    )
    return jax.shard_map(body, mesh=mesh, in_specs=in_specs, out_specs=out_specs, check_vma=False)
```
